128 devices in a mesh: req: 8 (over z, core), unit: 16 (over x, y).
Axes of the slice: x: 4, y: 4, z: 4, core: 2. Of those that a mesh axis runs over, the one named last changes fastest.
Arguments:
- tokens: bfloat16 [128, 384, 1536], P('req'), may hold values from -6 to 6
- lengths: int32 [128], P('req'), may hold values from 1 to 384, 30720 in all
- gate_proj: float32 [1536, 3072], P(('req', 'unit')), may hold values from -0.15625 to 0.15625
- input_proj: float32 [1536, 3072], P(('req', 'unit')), may hold values from -0.15625 to 0.15625
- state_proj: float32 [1536, 256], P(('req', 'unit')), may hold values from -0.15625 to 0.15625
- step_proj: float32 [1536, 48], P(('req', 'unit')), may hold values from -0.15625 to 0.15625
- out_proj: float32 [1536, 3072], P(('req', 'unit')), may hold values from -0.109375 to 0.109375
- conv_weight: float32 [4, 3328], replicated, may hold values from -3 to 3
- step_bias: float32 [48], replicated, may hold values from -4 to -1
- log_rate: float32 [48], replicated, may hold values from -3.5 to 0
- skip_gain: float32 [48], replicated, may hold values from 0.5 to 3
- norm_gain: float32 [3072], replicated, may hold values from 0.1 to 1.9
Outputs:
- mixed: bfloat16 [128, 384, 1536], P(('req', 'unit'))
- final_state: float32 [128, 48, 64, 128], P(('req', 'unit'))
The draws below stay inside these ranges and needn't reach their ends.
All inputs are finite; a program needn't handle non-finite values. No bound on the sum of `lengths` on one device may be relied on, other than what follows from the above.
Results may differ from the reference program's by a relative error of at most 0.0084.
Values may be sent and summed in bfloat16 or wider, within the bound.
No kernel may reach another device: no remote copies, remote signals or barrier semaphores. Data moves between devices by JAX's collectives and lax.ppermute only.
A program may use at most 192 MiB of HBM per device.

```python
import math
import jax
import jax.numpy as jnp
import numpy as np
from jax import lax

D = 1536
H = 48
HEADDIM = 64
NSTATE = 128
KCONV = 4
SPAN = 128
SEQ = 384
E = 3072
REQS = 128


def block_scale(key, shape, shards, smallest, high):
    loudness, own = 1.0, jax.random.fold_in(key, 6)
    for axis_at, parts in shards:
        heights = jnp.exp(jax.random.uniform(jax.random.fold_in(own, axis_at), (parts,), jnp.float32, smallest / len(shards), high / len(shards)))
        loudness = loudness * jnp.repeat(heights, shape[axis_at] // parts).reshape([-1 if axis == axis_at else 1 for axis in range(len(shape))])
    return loudness


def profile(number_of, total, bound, lean):
    weights = [(1 << 20) // math.isqrt(grade ** lean) + 1 for grade in range(2, number_of + 1)]
    rest, counts = total - bound - (number_of - 1), [1] * (number_of - 1)
    while rest > 0:
        movable = [i for i in range(number_of - 1) if counts[i] < bound]
        mass, budget = sum([weights[i] for i in movable]), rest
        for i in movable:
            more = min(bound - counts[i], max(1, budget * weights[i] // mass), rest)
            counts[i] = counts[i] + more
            rest = rest - more
    return np.array([bound] + counts)


def uneven(stream_key, amount, total, bound, slope):
    if amount == 2:
        one = jax.random.randint(stream_key, (), max(1, total - bound), min(bound, total - 1) + 1)
        return jnp.stack([one, total - one])
    sizes = jnp.asarray(profile(amount, total, bound, slope), jnp.int32)
    twos = (amount - 1) // 2
    donor, receiver = sizes[1:1 + 2 * twos:2], sizes[2:2 + 2 * twos:2]
    room = jnp.minimum(donor - 1, bound - receiver)
    shifted = jax.random.randint(jax.random.fold_in(stream_key, 1), (twos,), 0, 1 << 20) % (room + 1)
    sizes = sizes.at[1:1 + 2 * twos:2].set(donor - shifted).at[2:2 + 2 * twos:2].set(receiver + shifted)
    return sizes[jax.random.permutation(jax.random.fold_in(stream_key, 2), amount)]


def normal_values(own_key, shape, deviation, bound, cuts=(), kind=jnp.bfloat16):
    array = jax.random.normal(own_key, shape, jnp.float32) * deviation
    if len(cuts) > 0:
        array = block_scale(own_key, shape, cuts, -0.22, 0.18) * array
    return jnp.clip(array, min=-bound, max=bound).astype(kind)


def setup_inputs(seed: int = 0) -> dict:
    arg_keys = jax.random.split(jax.random.key(seed), 13)
    tokens = normal_values(arg_keys[0], (REQS, SEQ, D), 1.0, 6.0, ((0, 8),))
    lengths = uneven(arg_keys[1], REQS, REQS * SEQ * 5 // 8, SEQ, 2).astype(jnp.int32)
    gate_proj = normal_values(arg_keys[2], (D, E), D ** -0.5, 0.15625, ((0, 128),), jnp.float32)
    input_proj = normal_values(arg_keys[3], (D, E), D ** -0.5, 0.15625, ((0, 128),), jnp.float32)
    state_proj = normal_values(arg_keys[4], (D, 2 * NSTATE), D ** -0.5, 0.15625, ((0, 128),), jnp.float32)
    step_proj = normal_values(arg_keys[5], (D, H), D ** -0.5, 0.15625, ((0, 128),), jnp.float32)
    out_proj = normal_values(arg_keys[6], (D, E), E ** -0.5, 0.109375, ((0, 128),), jnp.float32)
    conv_weight = normal_values(arg_keys[7], (KCONV, E + 2 * NSTATE), KCONV ** -0.5, 3.0, (), jnp.float32)
    step_bias = jnp.clip(jax.random.uniform(arg_keys[8], (H,), jnp.float32, -4.0, -1.0), -4.0, -1.0)
    log_rate = jnp.clip(jax.random.uniform(arg_keys[9], (H,), jnp.float32, -3.5, 0.0), -3.5, 0.0)
    skip_gain = jnp.clip(jax.random.uniform(arg_keys[10], (H,), jnp.float32, 0.5, 3.0), 0.5, 3.0)
    norm_gain = jnp.clip(1.0 + 0.18 * jax.random.normal(arg_keys[11], (E,), jnp.float32), 0.1, 1.9)
    return dict(tokens=tokens, lengths=lengths, gate_proj=gate_proj, input_proj=input_proj, state_proj=state_proj, step_proj=step_proj, out_proj=out_proj, conv_weight=conv_weight, step_bias=step_bias, log_rate=log_rate, skip_gain=skip_gain, norm_gain=norm_gain)


EPSILON = 1e-05
HIGHEST = lax.Precision.HIGHEST

def causal_conv(values, kernel):
    kernel_len = kernel.shape[0]
    seq_len = values.shape[-2]
    axis_time = values.ndim - 2
    padding = [(0, 0)] * axis_time + [(kernel_len - 1, 0), (0, 0)]
    padded = jnp.pad(values.astype(jnp.float32), padding)
    running = jnp.zeros(values.shape, jnp.float32)
    for offset in range(kernel_len):
        running = running + kernel[offset] * lax.slice_in_dim(padded, offset, offset + seq_len, axis=axis_time)
    return jax.nn.silu(running)

def ssd_scan(head_in, step_size, b_matrix, c_matrix, rate_per, skip_gain, block_len):
    req_count, seq_len, head_count, head_dim = head_in.shape
    state_dim = b_matrix.shape[-1]
    blocks = seq_len // block_len
    b_short = b_matrix.astype(jnp.bfloat16)
    c_short = c_matrix.astype(jnp.bfloat16)
    b_wide = lax.optimization_barrier(b_short).astype(jnp.float32)
    c_wide = lax.optimization_barrier(c_short).astype(jnp.float32)
    shaped_x = jnp.moveaxis(head_in.reshape(req_count, blocks, block_len, head_count, head_dim), 1, 0)
    shaped_dt = jnp.moveaxis(step_size.reshape(req_count, blocks, block_len, head_count), 1, 0)
    shaped_bs = jnp.moveaxis(b_short.reshape(req_count, blocks, block_len, state_dim), 1, 0)
    shaped_cs = jnp.moveaxis(c_short.reshape(req_count, blocks, block_len, state_dim), 1, 0)
    shaped_b = jnp.moveaxis(b_wide.reshape(req_count, blocks, block_len, state_dim), 1, 0)
    shaped_c = jnp.moveaxis(c_wide.reshape(req_count, blocks, block_len, state_dim), 1, 0)
    decays = jnp.cumsum(shaped_dt * rate_per, axis=2)
    where_lower = jnp.arange(block_len)[:, None] >= jnp.arange(block_len)[None, :]

    def advance(carried, pieces):
        piece_x, piece_dt, piece_bs, piece_cs, piece_b, piece_c, piece_log = pieces
        intersection = jnp.einsum('rtn,rsn->rts', piece_cs, piece_bs, preferred_element_type=jnp.float32)
        log_gaps = piece_log[:, :, None, :] - piece_log[:, None, :, :]
        factor = jnp.exp(jnp.where(where_lower[None, :, :, None], log_gaps, -jnp.inf))
        mixing = intersection[..., None] * factor * piece_dt[:, None, :, :]
        inside = jnp.einsum('rtsh,rshp->rthp', mixing, piece_x, precision=HIGHEST)
        earlier = jnp.einsum('rtn,rhpn->rthp', piece_c, carried, precision=HIGHEST) * jnp.exp(piece_log)[..., None]
        ending = piece_log[:, -1, :]
        weight_in = jnp.exp(ending[:, None, :] - piece_log) * piece_dt
        fresh_state = jnp.einsum('rsh,rshp,rsn->rhpn', weight_in, piece_x, piece_b, precision=HIGHEST)
        carried = jnp.exp(ending)[:, :, None, None] * carried + fresh_state
        return (carried, inside + earlier)
    start_state = jnp.zeros((req_count, head_count, head_dim, state_dim), jnp.float32)
    final_state, outputs = lax.scan(advance, start_state, (shaped_x, shaped_dt, shaped_bs, shaped_cs, shaped_b, shaped_c, decays))
    scanned = jnp.moveaxis(outputs, 0, 1).reshape(req_count, seq_len, head_count, head_dim)
    return (scanned + skip_gain[:, None] * head_in, final_state)

def reference(tokens, lengths, gate_proj, input_proj, state_proj, step_proj, out_proj, conv_weight, step_bias, log_rate, skip_gain, norm_gain):
    gate_w = gate_proj.astype(jnp.bfloat16)
    input_w = input_proj.astype(jnp.bfloat16)
    state_w = state_proj.astype(jnp.bfloat16)
    step_w = step_proj.astype(jnp.bfloat16)
    out_w = out_proj.astype(jnp.bfloat16)
    rate_per = -jnp.exp(log_rate)
    position = jnp.arange(SEQ).astype(jnp.int32)

    def per_request(inputs):
        tokens_one, length = inputs
        gate_cols = jnp.dot(tokens_one, gate_w, preferred_element_type=jnp.float32).astype(jnp.bfloat16)
        input_cols = jnp.dot(tokens_one, input_w, preferred_element_type=jnp.float32).astype(jnp.bfloat16)
        state_cols = jnp.dot(tokens_one, state_w, preferred_element_type=jnp.float32).astype(jnp.bfloat16)
        step_cols = jnp.dot(tokens_one, step_w, preferred_element_type=jnp.float32).astype(jnp.bfloat16)
        joined = jnp.concatenate([input_cols, state_cols], axis=-1)
        convolved = causal_conv(joined, conv_weight)
        live = (position < length.astype(jnp.int32)).astype(jnp.float32)
        step_size = jax.nn.softplus(step_cols.astype(jnp.float32) + step_bias) * live[:, None]
        head_in = convolved[:, :E].reshape(1, SEQ, H, HEADDIM)
        b_matrix = convolved[None, :, E:E + NSTATE]
        c_matrix = convolved[None, :, E + NSTATE:]
        scanned, final_state = ssd_scan(head_in, step_size[None], b_matrix, c_matrix, rate_per, skip_gain, SPAN)
        gated = scanned.reshape(SEQ, E) * jax.nn.silu(gate_cols.astype(jnp.float32))
        spread = lax.optimization_barrier(jnp.mean(gated * gated, axis=-1, keepdims=True))
        normed = (gated * lax.rsqrt(spread + EPSILON) * norm_gain).astype(jnp.bfloat16)
        mixed_one = jnp.dot(normed, out_w.T, preferred_element_type=jnp.float32) * live[:, None]
        return (mixed_one.astype(jnp.bfloat16), final_state[0])
    mixed, final_state = lax.map(per_request, (tokens, lengths))
    return (mixed, final_state)
```

```python
import jax
import jax.numpy as jnp
from jax import lax
from jax.experimental import pallas as pl
from jax.experimental.pallas import tpu as pltpu
from jax.sharding import PartitionSpec as P

SPAN = 128
LANES = 128
HEADS_STEP = 8
EPSILON = 1e-05
BF = jnp.bfloat16
F32 = jnp.float32


def silu(v):
    h = 0.5 * v
    return h + h * jnp.tanh(h)


def causal_conv(values, taps):
    rows = lax.broadcasted_iota(jnp.int32, values.shape, 0)
    count = taps.shape[0]
    total = values * taps[count - 1 : count]
    for back in range(1, count):
        moved = jnp.where(rows >= back, pltpu.roll(values, back, 0), 0.0)
        total = total + moved * taps[count - 1 - back : count - back]
    return silu(total)


def scan_kernel(
    len_ref,
    input_ref,
    gate_ref,
    side_ref,
    taps_ref,
    side_taps_ref,
    bias_ref,
    log_rate_ref,
    skip_ref,
    gain_ref,
    gated_ref,
    state_ref,
    scale_ref,
    decay_col,
    delta_col,
    decay_row,
    b_scr,
    c_scr,
    cb_scr,
    square_scr,
):
    step = pl.program_id(0)
    seq = input_ref.shape[0]
    state_dim = side_taps_ref.shape[1] // 2
    groups = decay_col.shape[0]
    blocks = seq // SPAN
    inner = groups * input_ref.shape[1]
    position = lax.broadcasted_iota(jnp.int32, (seq, LANES), 0)
    live = (position < len_ref[0]).astype(F32)

    @pl.when(step == 0)
    def _():
        side = side_ref[...].astype(F32)
        conv = causal_conv(side[:, : 2 * state_dim], side_taps_ref[...])
        b_short = conv[:, :state_dim].astype(BF)
        c_short = conv[:, state_dim:].astype(BF)
        b_scr[...] = b_short
        c_scr[...] = c_short
        for block in range(blocks):
            at = slice(block * SPAN, (block + 1) * SPAN)
            cb_scr[block] = lax.dot_general(
                c_short[at], b_short[at], (((1,), (1,)), ((), ())), preferred_element_type=F32
            )
        raw = side[:, 2 * state_dim :] + bias_ref[...]
        delta = (jnp.maximum(raw, 0.0) + jnp.log1p(jnp.exp(-jnp.abs(raw)))) * live
        total = delta * -jnp.exp(log_rate_ref[...])
        within = position % SPAN
        reach = 1
        while reach < SPAN:
            total = total + jnp.where(within >= reach, pltpu.roll(total, reach, 0), 0.0)
            reach *= 2
        turned = jnp.transpose(total)
        for group in range(groups):
            at = slice(group * HEADS_STEP, (group + 1) * HEADS_STEP)
            decay_col[group] = total[:, at]
            delta_col[group] = delta[:, at]
            decay_row[group] = turned[at]
        square_scr[...] = jnp.zeros_like(square_scr)

    decays = decay_col[step]
    deltas = delta_col[step]
    rows_of = decay_row[step]
    lower = lax.broadcasted_iota(jnp.int32, (SPAN, SPAN), 0) >= lax.broadcasted_iota(
        jnp.int32, (SPAN, SPAN), 1
    )
    left = lax.broadcasted_iota(jnp.int32, (SPAN, LANES), 1) < LANES // 2
    top = lax.broadcasted_iota(jnp.int32, (LANES, state_dim), 0) < LANES // 2
    for pair in range(HEADS_STEP // 2):
        cols = slice(pair * LANES, (pair + 1) * LANES)
        one, two = 2 * pair, 2 * pair + 1
        x_conv = causal_conv(input_ref[:, cols].astype(F32), taps_ref[:, cols])
        gate = silu(gate_ref[:, cols].astype(F32))
        skip = skip_ref[:, cols]
        gain = gain_ref[:, cols]
        state = jnp.zeros((LANES, state_dim), F32)
        for block in range(blocks):
            at = slice(block * SPAN, (block + 1) * SPAN)
            x_here = x_conv[at]
            cb = cb_scr[block]
            d_one, d_two = decays[at, one : one + 1], decays[at, two : two + 1]
            mix_one = cb * jnp.exp(
                jnp.where(lower, d_one - rows_of[one : one + 1, at], -jnp.inf)
            )
            mix_two = cb * jnp.exp(
                jnp.where(lower, d_two - rows_of[two : two + 1, at], -jnp.inf)
            )
            decay = jnp.where(left, d_one, d_two)
            x_step = x_here * jnp.where(
                left, deltas[at, one : one + 1], deltas[at, two : two + 1]
            )
            short = x_step.astype(BF)
            zero = jnp.zeros_like(short)
            mixing = jnp.concatenate([mix_one.astype(BF), mix_two.astype(BF)], axis=1)
            spread = jnp.concatenate(
                [jnp.where(left, short, zero), jnp.where(left, zero, short)], axis=0
            )
            out = jnp.dot(mixing, spread, preferred_element_type=F32)
            if block:
                out = out + jnp.exp(decay) * lax.dot_general(
                    c_scr[at],
                    state.astype(BF),
                    (((1,), (1,)), ((), ())),
                    preferred_element_type=F32,
                )
            ending = decay[SPAN - 1 : SPAN]
            weighted = (x_step * jnp.exp(ending - decay)).astype(BF)
            fresh = lax.dot_general(
                weighted, b_scr[at], (((0,), (0,)), ((), ())), preferred_element_type=F32
            )
            if block:
                fade = jnp.where(
                    top,
                    jnp.exp(d_one[SPAN - 1 : SPAN]),
                    jnp.exp(d_two[SPAN - 1 : SPAN]),
                )
                fresh = fade * state + fresh
            state = fresh
            gated = (out + skip * x_here) * gate[at]
            square_scr[at, :] += gated * gated
            gated_ref[at, cols] = (gated * gain).astype(BF)
        state_ref[cols, :] = state

    @pl.when(step == groups - 1)
    def _():
        mean = jnp.sum(square_scr[...], axis=1, keepdims=True) / inner
        scale_ref[...] = lax.rsqrt(mean + EPSILON) * live


def scan_gate(length, inputs, gate, side, taps, side_taps, bias, log_rate, skip, gain):
    seq, inner = inputs.shape
    width = side_taps.shape[1]
    state_dim = width // 2
    cols = HEADS_STEP * LANES // 2
    groups = inner // cols
    whole = lambda i: (0, 0)
    part = lambda i: (0, i)
    return pl.pallas_call(
        scan_kernel,
        grid=(groups,),
        in_specs=[
            pl.BlockSpec(memory_space=pltpu.SMEM),
            pl.BlockSpec((seq, cols), part),
            pl.BlockSpec((seq, cols), part),
            pl.BlockSpec((seq, width + LANES), whole),
            pl.BlockSpec((taps.shape[0], cols), part),
            pl.BlockSpec((taps.shape[0], width), whole),
            pl.BlockSpec((1, LANES), whole),
            pl.BlockSpec((1, LANES), whole),
            pl.BlockSpec((1, cols), part),
            pl.BlockSpec((1, cols), part),
        ],
        out_specs=[
            pl.BlockSpec((seq, cols), part),
            pl.BlockSpec((cols, state_dim), lambda i: (i, 0)),
            pl.BlockSpec((seq, LANES), whole),
        ],
        out_shape=[
            jax.ShapeDtypeStruct((seq, inner), BF),
            jax.ShapeDtypeStruct((inner, state_dim), F32),
            jax.ShapeDtypeStruct((seq, LANES), F32),
        ],
        scratch_shapes=[
            pltpu.VMEM((groups, seq, HEADS_STEP), F32),
            pltpu.VMEM((groups, seq, HEADS_STEP), F32),
            pltpu.VMEM((groups, HEADS_STEP, seq), F32),
            pltpu.VMEM((seq, state_dim), BF),
            pltpu.VMEM((seq, state_dim), BF),
            pltpu.VMEM((seq // SPAN, SPAN, SPAN), F32),
            pltpu.VMEM((seq, LANES), F32),
        ],
        compiler_params=pltpu.CompilerParams(
            dimension_semantics=("arbitrary",), vmem_limit_bytes=40 << 20
        ),
        cost_estimate=pl.CostEstimate(
            flops=2 * inner * seq * 640, transcendentals=inner * seq * 6, bytes_accessed=9 << 20
        ),
        name="scan_gate",
    )(length, inputs, gate, side, taps, side_taps, bias, log_rate, skip, gain)


def body(
    tokens,
    lengths,
    gate_proj,
    input_proj,
    state_proj,
    step_proj,
    out_proj,
    conv_weight,
    step_bias,
    log_rate,
    skip_gain,
    norm_gain,
):
    unit_id = lax.axis_index("unit")
    group_reqs, seq_len, model_dim = tokens.shape
    inner_dim = gate_proj.shape[1]
    head_count = log_rate.shape[0]
    head_dim = inner_dim // head_count
    state_dim = state_proj.shape[1] // 2
    everyone = ("req", "unit")

    side_proj = jnp.concatenate([state_proj, step_proj], axis=1)
    spare = LANES - head_count
    side_proj = jnp.pad(side_proj, ((0, 0), (0, spare)))
    first = jnp.concatenate([side_proj.astype(BF), input_proj.astype(BF)], axis=1)
    first = lax.all_gather(first, everyone, axis=0, tiled=True)
    second = lax.all_gather(gate_proj.astype(BF), everyone, axis=0, tiled=True)
    third = lax.all_gather(out_proj.astype(BF), everyone, axis=0, tiled=True)

    own = lax.dynamic_index_in_dim(tokens, unit_id, 0, keepdims=False)
    length = lax.dynamic_slice_in_dim(lengths, unit_id, 1, 0)
    width = side_proj.shape[1]
    projected = jnp.dot(own, first, preferred_element_type=F32).astype(BF)
    side, inputs = projected[:, :width], projected[:, width:]
    gate = jnp.dot(own, second, preferred_element_type=F32).astype(BF)
    gated, state, scale = scan_gate(
        length,
        inputs,
        gate,
        side,
        conv_weight[:, :inner_dim],
        conv_weight[:, inner_dim:],
        jnp.pad(step_bias, (0, spare))[None],
        jnp.pad(log_rate, (0, spare))[None],
        jnp.repeat(skip_gain, head_dim)[None],
        norm_gain[None],
    )
    mixed = lax.dot_general(gated, third, (((1,), (1,)), ((), ())), preferred_element_type=F32)
    mixed = (mixed * scale[:, :1]).astype(BF)
    return (mixed[None], state.reshape(1, head_count, head_dim, state_dim))


def solution(mesh):
    placed = (
        P("req", None, None),
        P("req"),
        P(("req", "unit"), None),
        P(("req", "unit"), None),
        P(("req", "unit"), None),
        P(("req", "unit"), None),
        P(("req", "unit"), None),
        P(),
        P(),
        P(),
        P(),
        P(),
    )
    return jax.shard_map(
        body,
        mesh=mesh,
        in_specs=placed,
        out_specs=(P(("req", "unit"), None, None), P(("req", "unit"), None, None, None)),
        check_vma=False,
    )
```

```python
import jax
import jax.numpy as jnp
from jax import lax
from jax.experimental import pallas as pl
from jax.experimental.pallas import tpu as pltpu
from jax.sharding import PartitionSpec as P

SPAN = 128
LANES = 128
HEADS_STEP = 8
EPSILON = 1e-05
BF = jnp.bfloat16
F32 = jnp.float32


def silu(v):
    h = 0.5 * v
    return h + h * jnp.tanh(h)


def causal_conv(values, taps):
    rows = lax.broadcasted_iota(jnp.int32, values.shape, 0)
    count = taps.shape[0]
    total = values * taps[count - 1 : count]
    for back in range(1, count):
        moved = jnp.where(rows >= back, pltpu.roll(values, back, 0), 0.0)
        total = total + moved * taps[count - 1 - back : count - back]
    return silu(total)


def scan_kernel(
    meta_ref,
    input_ref,
    gate_ref,
    side_ref,
    taps_ref,
    side_taps_ref,
    bias_ref,
    log_rate_ref,
    skip_ref,
    gain_ref,
    gated_ref,
    state_ref,
    square_ref,
    decay_col,
    delta_col,
    decay_row,
    b_scr,
    c_scr,
    cb_scr,
):
    which = pl.program_id(0)
    step = pl.program_id(1)
    seq = input_ref.shape[0]
    state_dim = side_taps_ref.shape[1] // 2
    groups = decay_col.shape[0]
    blocks = seq // SPAN
    position = lax.broadcasted_iota(jnp.int32, (seq, LANES), 0)
    group_here = meta_ref[0] * pl.num_programs(1) + step

    @pl.when(step == 0)
    def _():
        side = side_ref[...].astype(F32)
        conv = causal_conv(side[:, : 2 * state_dim], side_taps_ref[...])
        b_short = conv[:, :state_dim].astype(BF)
        c_short = conv[:, state_dim:].astype(BF)
        b_scr[...] = b_short
        c_scr[...] = c_short
        for block in range(blocks):
            at = slice(block * SPAN, (block + 1) * SPAN)
            cb_scr[block] = lax.dot_general(
                c_short[at], b_short[at], (((1,), (1,)), ((), ())), preferred_element_type=F32
            )
        raw = side[:, 2 * state_dim :] + bias_ref[...]
        live = (position < meta_ref[1 + which]).astype(F32)
        delta = (jnp.maximum(raw, 0.0) + jnp.log1p(jnp.exp(-jnp.abs(raw)))) * live
        total = delta * -jnp.exp(log_rate_ref[...])
        within = position % SPAN
        reach = 1
        while reach < SPAN:
            total = total + jnp.where(within >= reach, pltpu.roll(total, reach, 0), 0.0)
            reach *= 2
        turned = jnp.transpose(total)
        for group in range(groups):
            at = slice(group * HEADS_STEP, (group + 1) * HEADS_STEP)
            decay_col[group] = total[:, at]
            delta_col[group] = delta[:, at]
            decay_row[group] = turned[at]
        square_ref[...] = jnp.zeros_like(square_ref)

    decays = decay_col[group_here]
    deltas = delta_col[group_here]
    rows_of = decay_row[group_here]
    lower = lax.broadcasted_iota(jnp.int32, (SPAN, SPAN), 0) >= lax.broadcasted_iota(
        jnp.int32, (SPAN, SPAN), 1
    )
    left = lax.broadcasted_iota(jnp.int32, (SPAN, LANES), 1) < LANES // 2
    top = lax.broadcasted_iota(jnp.int32, (LANES, state_dim), 0) < LANES // 2
    for pair in range(HEADS_STEP // 2):
        cols = slice(pair * LANES, (pair + 1) * LANES)
        one, two = 2 * pair, 2 * pair + 1
        x_conv = causal_conv(input_ref[:, cols].astype(F32), taps_ref[:, cols])
        gate = silu(gate_ref[:, cols].astype(F32))
        skip = skip_ref[:, cols]
        gain = gain_ref[:, cols]
        state = jnp.zeros((LANES, state_dim), F32)
        for block in range(blocks):
            at = slice(block * SPAN, (block + 1) * SPAN)
            x_here = x_conv[at]
            cb = cb_scr[block]
            d_one, d_two = decays[at, one : one + 1], decays[at, two : two + 1]
            mix_one = cb * jnp.exp(
                jnp.where(lower, d_one - rows_of[one : one + 1, at], -jnp.inf)
            )
            mix_two = cb * jnp.exp(
                jnp.where(lower, d_two - rows_of[two : two + 1, at], -jnp.inf)
            )
            decay = jnp.where(left, d_one, d_two)
            x_step = x_here * jnp.where(
                left, deltas[at, one : one + 1], deltas[at, two : two + 1]
            )
            short = x_step.astype(BF)
            zero = jnp.zeros_like(short)
            mixing = jnp.concatenate([mix_one.astype(BF), mix_two.astype(BF)], axis=1)
            spread = jnp.concatenate(
                [jnp.where(left, short, zero), jnp.where(left, zero, short)], axis=0
            )
            out = jnp.dot(mixing, spread, preferred_element_type=F32)
            if block:
                out = out + jnp.exp(decay) * lax.dot_general(
                    c_scr[at],
                    state.astype(BF),
                    (((1,), (1,)), ((), ())),
                    preferred_element_type=F32,
                )
            ending = decay[SPAN - 1 : SPAN]
            weighted = (x_step * jnp.exp(ending - decay)).astype(BF)
            fresh = lax.dot_general(
                weighted, b_scr[at], (((0,), (0,)), ((), ())), preferred_element_type=F32
            )
            if block:
                fade = jnp.where(
                    top,
                    jnp.exp(d_one[SPAN - 1 : SPAN]),
                    jnp.exp(d_two[SPAN - 1 : SPAN]),
                )
                fresh = fade * state + fresh
            state = fresh
            gated = (out + skip * x_here) * gate[at]
            square_ref[at, :] += gated * gated
            gated_ref[at, cols] = (gated * gain).astype(BF)
        state_ref[cols, :] = state


def scan_gate(meta, projected, conv_weight, bias, log_rate, skip, gain, width):
    rows, total = projected.shape
    seq = rows // 2
    state_dim = width // 2
    half = (total - width - LANES) // 2
    inner = 2 * half
    cols = HEADS_STEP * LANES // 2
    groups = half // cols
    taps = conv_weight.shape[0]
    here = lambda r, g, m: (0, m[0] * groups + g)
    fixed = lambda r, g, m: (0, 0)
    grid_spec = pltpu.PrefetchScalarGridSpec(
        num_scalar_prefetch=1,
        grid=(2, groups),
        in_specs=[
            pl.BlockSpec((seq, cols), lambda r, g, m: (r, g)),
            pl.BlockSpec((seq, cols), lambda r, g, m: (r, groups + g)),
            pl.BlockSpec((seq, width + LANES), lambda r, g, m: (r, inner // (width + LANES))),
            pl.BlockSpec((taps, cols), here),
            pl.BlockSpec((taps, width), lambda r, g, m: (0, inner // width)),
            pl.BlockSpec((1, LANES), fixed),
            pl.BlockSpec((1, LANES), fixed),
            pl.BlockSpec((1, cols), here),
            pl.BlockSpec((1, cols), here),
        ],
        out_specs=[
            pl.BlockSpec((None, seq, cols), lambda r, g, m: (r, 0, g)),
            pl.BlockSpec((None, cols, state_dim), lambda r, g, m: (r, g, 0)),
            pl.BlockSpec((None, seq, LANES), lambda r, g, m: (r, 0, 0)),
        ],
        scratch_shapes=[
            pltpu.VMEM((2 * groups, seq, HEADS_STEP), F32),
            pltpu.VMEM((2 * groups, seq, HEADS_STEP), F32),
            pltpu.VMEM((2 * groups, HEADS_STEP, seq), F32),
            pltpu.VMEM((seq, state_dim), BF),
            pltpu.VMEM((seq, state_dim), BF),
            pltpu.VMEM((seq // SPAN, SPAN, SPAN), F32),
        ],
    )
    return pl.pallas_call(
        scan_kernel,
        grid_spec=grid_spec,
        out_shape=[
            jax.ShapeDtypeStruct((2, seq, half), BF),
            jax.ShapeDtypeStruct((2, half, state_dim), F32),
            jax.ShapeDtypeStruct((2, seq, LANES), F32),
        ],
        compiler_params=pltpu.CompilerParams(
            dimension_semantics=("arbitrary", "arbitrary"), vmem_limit_bytes=40 << 20
        ),
        cost_estimate=pl.CostEstimate(
            flops=2 * inner * seq * 640, transcendentals=inner * seq * 6, bytes_accessed=9 << 20
        ),
        name="scan_gate",
    )(meta, projected, projected, projected, conv_weight, conv_weight, bias, log_rate, skip, gain)


def project_kernel(tokens_ref, *refs):
    pieces, out_ref = refs[:-1], refs[-1]
    depth = pieces[0].shape[0]
    total = None
    for index, piece in enumerate(pieces):
        part = jnp.dot(
            tokens_ref[:, index * depth : (index + 1) * depth],
            piece[...],
            preferred_element_type=F32,
        )
        total = part if total is None else total + part
    out_ref[...] = total.astype(BF)


def project(tokens, pieces):
    rows, model = tokens.shape
    depth, total = pieces[0].shape
    tile = total // 3
    return pl.pallas_call(
        project_kernel,
        grid=(3,),
        in_specs=[pl.BlockSpec((rows, model), lambda n: (0, 0))]
        + [pl.BlockSpec((depth, tile), lambda n: (0, n)) for _ in pieces],
        out_specs=pl.BlockSpec((rows, tile), lambda n: (0, n)),
        out_shape=jax.ShapeDtypeStruct((rows, total), BF),
        compiler_params=pltpu.CompilerParams(
            dimension_semantics=("arbitrary",), vmem_limit_bytes=40 << 20
        ),
        cost_estimate=pl.CostEstimate(
            flops=2 * rows * model * total, transcendentals=0, bytes_accessed=20 << 20
        ),
        name="project",
    )(tokens, *pieces)


def mix_kernel(meta_ref, mine_ref, other_ref, w_mine_ref, w_other_ref, sq_mine, sq_other, out_ref):
    seq = mine_ref.shape[0]
    dims = (((1,), (1,)), ((), ()))
    inner = 2 * mine_ref.shape[1]
    wide = lax.dot_general(mine_ref[...], w_mine_ref[...], dims, preferred_element_type=F32)
    wide += lax.dot_general(other_ref[...], w_other_ref[...], dims, preferred_element_type=F32)
    mean = jnp.sum(sq_mine[...] + sq_other[...], axis=1, keepdims=True) / inner
    live = lax.broadcasted_iota(jnp.int32, (seq, 1), 0) < meta_ref[1]
    scale = jnp.where(live, lax.rsqrt(mean + EPSILON), 0.0)
    short = (wide * scale).astype(BF)
    padded, kept = wide.shape[1], out_ref.shape[1]
    row = lax.broadcasted_iota(jnp.int32, (padded, kept), 0)
    col = lax.broadcasted_iota(jnp.int32, (padded, kept), 1)
    part = row & (PADDED_ROWS - 1)
    place = (row >> PADDED_SHIFT) * SHARD_ROWS + part
    pick = jnp.where((place == col) & (part < SHARD_ROWS), 1.0, 0.0).astype(BF)
    out_ref[...] = jnp.dot(short, pick, preferred_element_type=F32).astype(BF)


def mix(meta, mine, other, weight, sq_mine, sq_other, model):
    seq, half = mine.shape
    padded = weight.shape[0]
    steps = 4
    fixed = lambda n, m: (0, 0)
    return pl.pallas_call(
        mix_kernel,
        grid_spec=pltpu.PrefetchScalarGridSpec(
            num_scalar_prefetch=1,
            grid=(steps,),
            in_specs=[
                pl.BlockSpec((seq, half), fixed),
                pl.BlockSpec((seq, half), fixed),
                pl.BlockSpec((padded // steps, half), lambda n, m: (n, m[0])),
                pl.BlockSpec((padded // steps, half), lambda n, m: (n, 1 - m[0])),
                pl.BlockSpec((seq, LANES), fixed),
                pl.BlockSpec((seq, LANES), fixed),
            ],
            out_specs=pl.BlockSpec((seq, model // steps), lambda n, m: (0, n)),
        ),
        out_shape=jax.ShapeDtypeStruct((seq, model), BF),
        compiler_params=pltpu.CompilerParams(
            dimension_semantics=("arbitrary",), vmem_limit_bytes=40 << 20
        ),
        cost_estimate=pl.CostEstimate(
            flops=6 * seq * half * padded, transcendentals=0, bytes_accessed=16 << 20
        ),
        name="mix",
    )(meta, mine, other, weight, weight, sq_mine, sq_other)


EVERYONE = ("req", "unit")
DEVICES = 128
CORE = 16
SHARD_ROWS = 12
PADDED_ROWS = 16
PADDED_SHIFT = 4
COLOURS = 3
LINKS = (1 << 2, 1, 1 << 5, 3 << 2, 3, 3 << 5)


def link_of(colour, core, step):
    return LINKS[(colour + 3 * core + step) % 6]


def hop(value, mask_of):
    return lax.ppermute(
        value, EVERYONE, [(d, d ^ mask_of((d // CORE) % 2)) for d in range(DEVICES)]
    )


def swap(value):
    return hop(value, lambda core: CORE)


def row_sources(me, core):
    sources = []
    block = jnp.arange(64, dtype=jnp.int32)
    row = jnp.arange(8, dtype=jnp.int32)
    for colour in range(COLOURS):
        masks = []
        for side in range(2):
            mask = jnp.zeros_like(block)
            for step in range(6):
                mask = mask ^ (((block >> step) & 1) * link_of(colour, side, step))
            masks.append(mask)
        chip = (me ^ jnp.where(core == 0, masks[0], masks[1])) & ~CORE
        local = colour * 8 + row
        upper = (local >= SHARD_ROWS).astype(jnp.int32)
        device = chip[:, None] + CORE * upper[None]
        sources.append((device * SHARD_ROWS + (local - SHARD_ROWS * upper)[None]).reshape(-1))
    return jnp.concatenate(sources)


def body(
    tokens,
    lengths,
    gate_proj,
    input_proj,
    state_proj,
    step_proj,
    out_proj,
    conv_weight,
    step_bias,
    log_rate,
    skip_gain,
    norm_gain,
):
    unit_id = lax.axis_index("unit")
    me = lax.axis_index(EVERYONE).astype(jnp.int32)
    core = (me // CORE) % 2
    first_core = core == 0
    seq_len, model_dim = tokens.shape[1:]
    inner_dim = gate_proj.shape[1]
    head_count = log_rate.shape[0]
    head_dim = inner_dim // head_count
    width = state_proj.shape[1]
    half = inner_dim // 2
    spare = LANES - head_count

    padded_out = jnp.pad(out_proj.astype(BF), ((0, PADDED_ROWS - SHARD_ROWS), (0, 0)))
    out_weight = lax.all_gather(padded_out, EVERYONE, axis=0, tiled=True)

    side = jnp.pad(jnp.concatenate([state_proj, step_proj], axis=1), ((0, 0), (0, spare)))
    low = jnp.concatenate([input_proj[:, :half], gate_proj[:, :half], side], axis=1).astype(BF)
    high = jnp.concatenate([input_proj[:, half:], gate_proj[:, half:], side], axis=1).astype(BF)
    received = swap(jnp.where(first_core, high, low))
    kept = jnp.where(first_core, low, high)
    pair = jnp.concatenate(
        [jnp.where(first_core, kept, received), jnp.where(first_core, received, kept)], axis=0
    )
    held = [pair[8 * c : 8 * c + 8] for c in range(COLOURS)]
    for step in range(5):
        moved = [
            hop(held[c], lambda core, c=c: link_of(c, core, step)) for c in range(COLOURS)
        ]
        held = [jnp.concatenate([h, m], axis=0) for h, m in zip(held, moved)]
    moved = [hop(held[c], lambda core, c=c: link_of(c, core, 5)) for c in range(COLOURS)]
    pieces = [piece for both in zip(held, moved) for piece in both]

    own = lax.dynamic_index_in_dim(tokens, unit_id, 0, keepdims=False)
    length = lax.dynamic_slice_in_dim(lengths, unit_id, 1, 0)
    coded = jnp.stack([length // 16, length % 16], axis=1).astype(BF)
    coded = jnp.pad(coded, ((0, 7), (0, model_dim - 2)))
    other = swap(jnp.concatenate([own, coded], axis=0))
    code = other[seq_len, :2].astype(jnp.int32)
    meta = jnp.stack([core, length[0], code[0] * 16 + code[1]])
    both = jnp.concatenate([own, other[:seq_len]], axis=0)
    pick = jnp.arange(model_dim, dtype=jnp.int32)[:, None] == row_sources(me, core)[None]
    both = jnp.dot(both, pick.astype(BF), preferred_element_type=F32).astype(BF)

    projected = project(both, pieces)
    gated, state, squares = scan_gate(
        meta,
        projected,
        conv_weight,
        jnp.pad(step_bias, (0, spare))[None],
        jnp.pad(log_rate, (0, spare))[None],
        jnp.repeat(skip_gain, head_dim)[None],
        norm_gain[None],
        width,
    )
    gated_other, squares_other, state_other = swap(gated[1]), swap(squares[1]), swap(state[1])
    mixed = mix(meta, gated[0], gated_other, out_weight, squares[0], squares_other, model_dim)
    state = jnp.concatenate(
        [jnp.where(first_core, state[0], state_other), jnp.where(first_core, state_other, state[0])]
    )
    return (mixed[None], state.reshape(1, head_count, head_dim, width // 2))


def solution(mesh):
    placed = (
        P("req", None, None),
        P("req"),
        P(("req", "unit"), None),
        P(("req", "unit"), None),
        P(("req", "unit"), None),
        P(("req", "unit"), None),
        P(("req", "unit"), None),
        P(),
        P(),
        P(),
        P(),
        P(),
    )
    return jax.shard_map(
        body,
        mesh=mesh,
        in_specs=placed,
        out_specs=(P(("req", "unit"), None, None), P(("req", "unit"), None, None, None)),
        check_vma=False,
    )
```

```python
import jax
import jax.numpy as jnp
from jax import lax
from jax.experimental import pallas as pl
from jax.experimental.pallas import tpu as pltpu
from jax.sharding import PartitionSpec as P

SPAN = 128
LANES = 128
HEADS_STEP = 8
EPSILON = 1e-05
BF = jnp.bfloat16
F32 = jnp.float32


def silu(v):
    h = 0.5 * v
    return h + h * jnp.tanh(h)


def causal_conv(values, taps):
    rows = lax.broadcasted_iota(jnp.int32, values.shape, 0)
    count = taps.shape[0]
    total = values * taps[count - 1 : count]
    for back in range(1, count):
        moved = jnp.where(rows >= back, pltpu.roll(values, back, 0), 0.0)
        total = total + moved * taps[count - 1 - back : count - back]
    return silu(total)


def scan_kernel(
    meta_ref,
    input_ref,
    side_ref,
    taps_ref,
    side_taps_ref,
    bias_ref,
    log_rate_ref,
    skip_ref,
    scanned_ref,
    state_ref,
    decay_col,
    delta_col,
    decay_row,
    b_scr,
    c_scr,
    cb_scr,
):
    which = pl.program_id(0)
    step = pl.program_id(1)
    seq = input_ref.shape[0]
    state_dim = side_taps_ref.shape[1] // 2
    groups = decay_col.shape[0]
    blocks = seq // SPAN
    position = lax.broadcasted_iota(jnp.int32, (seq, LANES), 0)
    group_here = meta_ref[0] * pl.num_programs(1) + step

    @pl.when(step == 0)
    def _():
        side = side_ref[...].astype(F32)
        conv = causal_conv(side[:, : 2 * state_dim], side_taps_ref[...])
        b_short = conv[:, :state_dim].astype(BF)
        c_short = conv[:, state_dim:].astype(BF)
        b_scr[...] = b_short
        c_scr[...] = c_short
        for block in range(blocks):
            at = slice(block * SPAN, (block + 1) * SPAN)
            cb_scr[block] = lax.dot_general(
                c_short[at], b_short[at], (((1,), (1,)), ((), ())), preferred_element_type=F32
            )
        raw = side[:, 2 * state_dim :] + bias_ref[...]
        live = (position < meta_ref[1 + which]).astype(F32)
        delta = (jnp.maximum(raw, 0.0) + jnp.log1p(jnp.exp(-jnp.abs(raw)))) * live
        total = delta * -jnp.exp(log_rate_ref[...])
        within = position % SPAN
        reach = 1
        while reach < SPAN:
            total = total + jnp.where(within >= reach, pltpu.roll(total, reach, 0), 0.0)
            reach *= 2
        turned = jnp.transpose(total)
        for group in range(groups):
            at = slice(group * HEADS_STEP, (group + 1) * HEADS_STEP)
            decay_col[group] = total[:, at]
            delta_col[group] = delta[:, at]
            decay_row[group] = turned[at]

    decays = decay_col[group_here]
    deltas = delta_col[group_here]
    rows_of = decay_row[group_here]
    lower = lax.broadcasted_iota(jnp.int32, (SPAN, SPAN), 0) >= lax.broadcasted_iota(
        jnp.int32, (SPAN, SPAN), 1
    )
    left = lax.broadcasted_iota(jnp.int32, (SPAN, LANES), 1) < LANES // 2
    top = lax.broadcasted_iota(jnp.int32, (LANES, state_dim), 0) < LANES // 2
    for pair in range(HEADS_STEP // 2):
        cols = slice(pair * LANES, (pair + 1) * LANES)
        one, two = 2 * pair, 2 * pair + 1
        x_conv = causal_conv(input_ref[:, cols].astype(F32), taps_ref[:, cols])
        skip = skip_ref[:, cols]
        state = jnp.zeros((LANES, state_dim), F32)
        for block in range(blocks):
            at = slice(block * SPAN, (block + 1) * SPAN)
            x_here = x_conv[at]
            cb = cb_scr[block]
            d_one, d_two = decays[at, one : one + 1], decays[at, two : two + 1]
            mix_one = cb * jnp.exp(
                jnp.where(lower, d_one - rows_of[one : one + 1, at], -jnp.inf)
            )
            mix_two = cb * jnp.exp(
                jnp.where(lower, d_two - rows_of[two : two + 1, at], -jnp.inf)
            )
            decay = jnp.where(left, d_one, d_two)
            x_step = x_here * jnp.where(
                left, deltas[at, one : one + 1], deltas[at, two : two + 1]
            )
            short = x_step.astype(BF)
            zero = jnp.zeros_like(short)
            mixing = jnp.concatenate([mix_one.astype(BF), mix_two.astype(BF)], axis=1)
            spread = jnp.concatenate(
                [jnp.where(left, short, zero), jnp.where(left, zero, short)], axis=0
            )
            out = jnp.dot(mixing, spread, preferred_element_type=F32)
            if block:
                out = out + jnp.exp(decay) * lax.dot_general(
                    c_scr[at],
                    state.astype(BF),
                    (((1,), (1,)), ((), ())),
                    preferred_element_type=F32,
                )
            ending = decay[SPAN - 1 : SPAN]
            weighted = (x_step * jnp.exp(ending - decay)).astype(BF)
            fresh = lax.dot_general(
                weighted, b_scr[at], (((0,), (0,)), ((), ())), preferred_element_type=F32
            )
            if block:
                fade = jnp.where(
                    top,
                    jnp.exp(d_one[SPAN - 1 : SPAN]),
                    jnp.exp(d_two[SPAN - 1 : SPAN]),
                )
                fresh = fade * state + fresh
            state = fresh
            scanned_ref[at, cols] = out + skip * x_here
        state_ref[cols, :] = state


def scan(meta, projected, conv_weight, bias, log_rate, skip, width):
    rows, total = projected.shape
    seq = rows // 2
    state_dim = width // 2
    half = total - width - LANES
    inner = 2 * half
    cols = HEADS_STEP * LANES // 2
    groups = half // cols
    taps = conv_weight.shape[0]
    here = lambda r, g, m: (0, m[0] * groups + g)
    fixed = lambda r, g, m: (0, 0)
    grid_spec = pltpu.PrefetchScalarGridSpec(
        num_scalar_prefetch=1,
        grid=(2, groups),
        in_specs=[
            pl.BlockSpec((seq, cols), lambda r, g, m: (r, g)),
            pl.BlockSpec((seq, width + LANES), lambda r, g, m: (r, half // (width + LANES))),
            pl.BlockSpec((taps, cols), here),
            pl.BlockSpec((taps, width), lambda r, g, m: (0, inner // width)),
            pl.BlockSpec((1, LANES), fixed),
            pl.BlockSpec((1, LANES), fixed),
            pl.BlockSpec((1, cols), here),
        ],
        out_specs=[
            pl.BlockSpec((None, seq, cols), lambda r, g, m: (r, 0, g)),
            pl.BlockSpec((None, cols, state_dim), lambda r, g, m: (r, g, 0)),
        ],
        scratch_shapes=[
            pltpu.VMEM((2 * groups, seq, HEADS_STEP), F32),
            pltpu.VMEM((2 * groups, seq, HEADS_STEP), F32),
            pltpu.VMEM((2 * groups, HEADS_STEP, seq), F32),
            pltpu.VMEM((seq, state_dim), BF),
            pltpu.VMEM((seq, state_dim), BF),
            pltpu.VMEM((seq // SPAN, SPAN, SPAN), F32),
        ],
    )
    return pl.pallas_call(
        scan_kernel,
        grid_spec=grid_spec,
        out_shape=[
            jax.ShapeDtypeStruct((2, seq, half), F32),
            jax.ShapeDtypeStruct((2, half, state_dim), F32),
        ],
        compiler_params=pltpu.CompilerParams(
            dimension_semantics=("arbitrary", "arbitrary"), vmem_limit_bytes=40 << 20
        ),
        cost_estimate=pl.CostEstimate(
            flops=2 * inner * seq * 640, transcendentals=inner * seq * 6, bytes_accessed=9 << 20
        ),
        name="scan",
    )(meta, projected, projected, conv_weight, conv_weight, bias, log_rate, skip)


def project_kernel(tokens_ref, *refs):
    weight = jnp.concatenate([piece[...] for piece in refs[:-1]], axis=0)
    refs[-1][...] = jnp.dot(tokens_ref[...], weight, preferred_element_type=F32).astype(BF)


def project(tokens, pieces):
    rows, model = tokens.shape
    depth, total = pieces[0].shape
    steps = 3
    tile = total // steps
    return pl.pallas_call(
        project_kernel,
        grid=(steps,),
        in_specs=[pl.BlockSpec((rows, model), lambda n: (0, 0))]
        + [pl.BlockSpec((depth, tile), lambda n: (0, n)) for _ in pieces],
        out_specs=pl.BlockSpec((rows, tile), lambda n: (0, n)),
        out_shape=jax.ShapeDtypeStruct((rows, total), BF),
        compiler_params=pltpu.CompilerParams(
            dimension_semantics=("arbitrary",), vmem_limit_bytes=40 << 20
        ),
        cost_estimate=pl.CostEstimate(
            flops=2 * rows * model * total, transcendentals=0, bytes_accessed=10 << 20
        ),
        name="project",
    )(tokens, *pieces)


def gate_kernel(meta_ref, tokens_ref, scanned_ref, gain_ref, *refs):
    gated_ref, square_ref = refs[-2:]
    weight = jnp.concatenate([piece[...] for piece in refs[:-2]], axis=0)
    gate = jnp.dot(tokens_ref[...], weight, preferred_element_type=F32).astype(BF)
    gated = scanned_ref[...] * silu(gate.astype(F32))
    gated_ref[...] = (gated * gain_ref[...]).astype(BF)

    @pl.when(pl.program_id(0) == 0)
    def _():
        square_ref[...] = jnp.zeros_like(square_ref)

    square = gated * gated
    for at in range(0, square.shape[1], LANES):
        square_ref[...] += square[:, at : at + LANES]


def gating(which, meta, tokens, scanned, gain, pieces):
    _, seq, half = scanned.shape
    model = tokens.shape[1]
    depth = pieces[0].shape[0]
    steps = 3
    tile = half // steps
    return pl.pallas_call(
        gate_kernel,
        grid_spec=pltpu.PrefetchScalarGridSpec(
            num_scalar_prefetch=1,
            grid=(steps,),
            in_specs=[
                pl.BlockSpec((seq, model), lambda n, m: (which, 0)),
                pl.BlockSpec((None, seq, tile), lambda n, m: (which, 0, n)),
                pl.BlockSpec((1, tile), lambda n, m: (0, m[0] * steps + n)),
            ]
            + [pl.BlockSpec((depth, tile), lambda n, m: (0, n)) for _ in pieces],
            out_specs=[
                pl.BlockSpec((seq, tile), lambda n, m: (0, n)),
                pl.BlockSpec((seq, LANES), lambda n, m: (0, 0)),
            ],
        ),
        out_shape=[
            jax.ShapeDtypeStruct((seq, half), BF),
            jax.ShapeDtypeStruct((seq, LANES), F32),
        ],
        compiler_params=pltpu.CompilerParams(
            dimension_semantics=("arbitrary",), vmem_limit_bytes=40 << 20
        ),
        cost_estimate=pl.CostEstimate(
            flops=2 * seq * model * half, transcendentals=seq * half, bytes_accessed=10 << 20
        ),
        name="gating",
    )(meta, tokens, scanned, gain, *pieces)


def mix_kernel(meta_ref, mine_ref, other_ref, w_mine_ref, w_other_ref, sq_mine, sq_other, out_ref):
    seq = mine_ref.shape[0]
    dims = (((1,), (1,)), ((), ()))
    inner = 2 * mine_ref.shape[1]
    wide = lax.dot_general(mine_ref[...], w_mine_ref[...], dims, preferred_element_type=F32)
    wide += lax.dot_general(other_ref[...], w_other_ref[...], dims, preferred_element_type=F32)
    mean = jnp.sum(sq_mine[...] + sq_other[...], axis=1, keepdims=True) / inner
    live = lax.broadcasted_iota(jnp.int32, (seq, 1), 0) < meta_ref[1]
    scale = jnp.where(live, lax.rsqrt(mean + EPSILON), 0.0)
    short = (wide * scale).astype(BF)
    padded, kept = wide.shape[1], out_ref.shape[1]
    row = lax.broadcasted_iota(jnp.int32, (padded, kept), 0)
    col = lax.broadcasted_iota(jnp.int32, (padded, kept), 1)
    part = row & (PADDED_ROWS - 1)
    place = (row >> PADDED_SHIFT) * SHARD_ROWS + part
    pick = jnp.where((place == col) & (part < SHARD_ROWS), 1.0, 0.0).astype(BF)
    out_ref[...] = jnp.dot(short, pick, preferred_element_type=F32).astype(BF)


def mix(meta, mine, other, weight, sq_mine, sq_other, model):
    seq, half = mine.shape
    padded = weight.shape[0]
    steps = 4
    fixed = lambda n, m: (0, 0)
    return pl.pallas_call(
        mix_kernel,
        grid_spec=pltpu.PrefetchScalarGridSpec(
            num_scalar_prefetch=1,
            grid=(steps,),
            in_specs=[
                pl.BlockSpec((seq, half), fixed),
                pl.BlockSpec((seq, half), fixed),
                pl.BlockSpec((padded // steps, half), lambda n, m: (n, m[0])),
                pl.BlockSpec((padded // steps, half), lambda n, m: (n, 1 - m[0])),
                pl.BlockSpec((seq, LANES), fixed),
                pl.BlockSpec((seq, LANES), fixed),
            ],
            out_specs=pl.BlockSpec((seq, model // steps), lambda n, m: (0, n)),
        ),
        out_shape=jax.ShapeDtypeStruct((seq, model), BF),
        compiler_params=pltpu.CompilerParams(
            dimension_semantics=("arbitrary",), vmem_limit_bytes=40 << 20
        ),
        cost_estimate=pl.CostEstimate(
            flops=6 * seq * half * padded, transcendentals=0, bytes_accessed=16 << 20
        ),
        name="mix",
    )(meta, mine, other, weight, weight, sq_mine, sq_other)


EVERYONE = ("req", "unit")
DEVICES = 128
CORE = 16
SHARD_ROWS = 12
PADDED_ROWS = 16
PADDED_SHIFT = 4
COLOURS = 3
LINKS = (1 << 2, 1, 1 << 5, 3 << 2, 3, 3 << 5)


def link_of(colour, core, step):
    return LINKS[(colour + 3 * core + step) % 6]


def hop(value, mask_of):
    return lax.ppermute(
        value, EVERYONE, [(d, d ^ mask_of((d // CORE) % 2)) for d in range(DEVICES)]
    )


def swap(value):
    return hop(value, lambda core: CORE)


def double(held, step):
    return held, [
        hop(piece, lambda core, c=c: link_of(c, core, step)) for c, piece in enumerate(held)
    ]


def row_sources(me, core):
    sources = []
    block = jnp.arange(64, dtype=jnp.int32)
    row = jnp.arange(8, dtype=jnp.int32)
    for colour in range(COLOURS):
        masks = []
        for side in range(2):
            mask = jnp.zeros_like(block)
            for step in range(6):
                mask = mask ^ (((block >> step) & 1) * link_of(colour, side, step))
            masks.append(mask)
        chip = (me ^ jnp.where(core == 0, masks[0], masks[1])) & ~CORE
        local = colour * 8 + row
        upper = (local >= SHARD_ROWS).astype(jnp.int32)
        device = chip[:, None] + CORE * upper[None]
        sources.append((device * SHARD_ROWS + (local - SHARD_ROWS * upper)[None]).reshape(-1))
    return jnp.concatenate(sources)


def body(
    tokens,
    lengths,
    gate_proj,
    input_proj,
    state_proj,
    step_proj,
    out_proj,
    conv_weight,
    step_bias,
    log_rate,
    skip_gain,
    norm_gain,
):
    unit_id = lax.axis_index("unit")
    me = lax.axis_index(EVERYONE).astype(jnp.int32)
    core = (me // CORE) % 2
    first_core = core == 0
    seq_len, model_dim = tokens.shape[1:]
    inner_dim = gate_proj.shape[1]
    head_count = log_rate.shape[0]
    head_dim = inner_dim // head_count
    width = state_proj.shape[1]
    half = inner_dim // 2
    spare = LANES - head_count

    side = jnp.pad(jnp.concatenate([state_proj, step_proj], axis=1), ((0, 0), (0, spare)))
    low = jnp.concatenate([input_proj[:, :half], side, gate_proj[:, :half]], axis=1).astype(BF)
    high = jnp.concatenate([input_proj[:, half:], side, gate_proj[:, half:]], axis=1).astype(BF)
    sent, out_proj = lax.optimization_barrier((jnp.where(first_core, high, low), out_proj))
    received = swap(sent)
    padded_out = jnp.pad(out_proj.astype(BF), ((0, PADDED_ROWS - SHARD_ROWS), (0, 0)))
    out_weight = lax.all_gather(padded_out, EVERYONE, axis=0, tiled=True)

    kept = jnp.where(first_core, low, high)
    pair = jnp.concatenate(
        [jnp.where(first_core, kept, received), jnp.where(first_core, received, kept)], axis=0
    )
    held = [pair[8 * c : 8 * c + 8] for c in range(COLOURS)]
    for step in range(3):
        held, moved = double(held, step)
        held = [jnp.concatenate([h, m], axis=0) for h, m in zip(held, moved)]
    held, moved = double(held, 3)
    moved, unit_id = lax.optimization_barrier((moved, unit_id))
    held = [jnp.concatenate([h, m], axis=0) for h, m in zip(held, moved)]
    cut = half + width + LANES
    early, late = [h[:, :cut] for h in held], [h[:, cut:] for h in held]
    early, moved = double(early, 4)
    moved, late = lax.optimization_barrier((moved, late))
    early, moved = double([jnp.concatenate([h, m], axis=0) for h, m in zip(early, moved)], 5)
    early = [piece for both in zip(early, moved) for piece in both]
    late, moved = double(late, 4)
    late, moved = double([jnp.concatenate([h, m], axis=0) for h, m in zip(late, moved)], 5)
    late = [piece for both in zip(late, moved) for piece in both]

    own = lax.dynamic_index_in_dim(tokens, unit_id, 0, keepdims=False)
    length = lax.dynamic_slice_in_dim(lengths, unit_id, 1, 0)
    coded = jnp.stack([length // 16, length % 16], axis=1).astype(BF)
    coded = jnp.pad(coded, ((0, 7), (0, model_dim - 2)))
    other = swap(jnp.concatenate([own, coded], axis=0))
    code = other[seq_len, :2].astype(jnp.int32)
    meta = jnp.stack([core, length[0], code[0] * 16 + code[1]])
    both = jnp.concatenate([own, other[:seq_len]], axis=0)
    pick = jnp.arange(model_dim, dtype=jnp.int32)[:, None] == row_sources(me, core)[None]
    both = jnp.dot(both, pick.astype(BF), preferred_element_type=F32).astype(BF)

    projected = project(both, early)
    scanned, state = scan(
        meta,
        projected,
        conv_weight,
        jnp.pad(step_bias, (0, spare))[None],
        jnp.pad(log_rate, (0, spare))[None],
        jnp.repeat(skip_gain, head_dim)[None],
        width,
    )
    state_other = swap(state[1])
    gain = norm_gain[None]
    sent, square_sent = gating(1, meta, both, scanned, gain, late)
    other, square_other = swap(sent), swap(square_sent)
    mine, square = gating(0, meta, both, scanned, gain, late)
    mixed = mix(meta, mine, other, out_weight, square, square_other, model_dim)
    state = jnp.concatenate(
        [jnp.where(first_core, state[0], state_other), jnp.where(first_core, state_other, state[0])]
    )
    return (mixed[None], state.reshape(1, head_count, head_dim, width // 2))


def solution(mesh):
    placed = (
        P("req", None, None),
        P("req"),
        P(("req", "unit"), None),
        P(("req", "unit"), None),
        P(("req", "unit"), None),
        P(("req", "unit"), None),
        P(("req", "unit"), None),
        P(),
        P(),
        P(),
        P(),
        P(),
    )
    return jax.shard_map(
        body,
        mesh=mesh,
        in_specs=placed,
        out_specs=(P(("req", "unit"), None, None), P(("req", "unit"), None, None, None)),
        check_vma=False,
    )
```

```python
import jax
import jax.numpy as jnp
from jax import lax
from jax.experimental import pallas as pl
from jax.experimental.pallas import tpu as pltpu
from jax.sharding import PartitionSpec as P

SPAN = 128
LANES = 128
HEADS_STEP = 8
EPSILON = 1e-05
BF = jnp.bfloat16
F32 = jnp.float32


def in_hbm(value):
    return pltpu.with_memory_space_constraint(value, pltpu.HBM)


def silu(v):
    h = 0.5 * v
    return h + h * jnp.tanh(h)


def causal_conv(values, taps):
    rows = lax.broadcasted_iota(jnp.int32, values.shape, 0)
    count = taps.shape[0]
    total = values * taps[count - 1 : count]
    for back in range(1, count):
        moved = jnp.where(rows >= back, pltpu.roll(values, back, 0), 0.0)
        total = total + moved * taps[count - 1 - back : count - back]
    return silu(total)


def scan_kernel(
    meta_ref,
    input_ref,
    side_ref,
    taps_ref,
    side_taps_ref,
    bias_ref,
    log_rate_ref,
    skip_ref,
    scanned_ref,
    state_ref,
    decay_col,
    delta_col,
    decay_row,
    b_scr,
    c_scr,
    cb_scr,
):
    which = pl.program_id(0)
    step = pl.program_id(1)
    seq = input_ref.shape[0]
    state_dim = side_taps_ref.shape[1] // 2
    groups = decay_col.shape[0]
    blocks = seq // SPAN
    position = lax.broadcasted_iota(jnp.int32, (seq, LANES), 0)
    group_here = meta_ref[0] * pl.num_programs(1) + step

    @pl.when(step == 0)
    def _():
        side = side_ref[...].astype(F32)
        conv = causal_conv(side[:, : 2 * state_dim], side_taps_ref[...])
        b_short = conv[:, :state_dim].astype(BF)
        c_short = conv[:, state_dim:].astype(BF)
        b_scr[...] = b_short
        c_scr[...] = c_short
        for block in range(blocks):
            at = slice(block * SPAN, (block + 1) * SPAN)
            cb_scr[block] = lax.dot_general(
                c_short[at], b_short[at], (((1,), (1,)), ((), ())), preferred_element_type=F32
            )
        raw = side[:, 2 * state_dim :] + bias_ref[...]
        live = (position < meta_ref[1 + which]).astype(F32)
        delta = (jnp.maximum(raw, 0.0) + jnp.log1p(jnp.exp(-jnp.abs(raw)))) * live
        total = delta * -jnp.exp(log_rate_ref[...])
        within = position % SPAN
        reach = 1
        while reach < SPAN:
            total = total + jnp.where(within >= reach, pltpu.roll(total, reach, 0), 0.0)
            reach *= 2
        turned = jnp.transpose(total)
        for group in range(groups):
            at = slice(group * HEADS_STEP, (group + 1) * HEADS_STEP)
            decay_col[group] = total[:, at]
            delta_col[group] = delta[:, at]
            decay_row[group] = turned[at]

    decays = decay_col[group_here]
    deltas = delta_col[group_here]
    rows_of = decay_row[group_here]
    lower = lax.broadcasted_iota(jnp.int32, (SPAN, SPAN), 0) >= lax.broadcasted_iota(
        jnp.int32, (SPAN, SPAN), 1
    )
    left = lax.broadcasted_iota(jnp.int32, (SPAN, LANES), 1) < LANES // 2
    top = lax.broadcasted_iota(jnp.int32, (LANES, state_dim), 0) < LANES // 2
    for pair in range(HEADS_STEP // 2):
        cols = slice(pair * LANES, (pair + 1) * LANES)
        one, two = 2 * pair, 2 * pair + 1
        x_conv = causal_conv(input_ref[:, cols].astype(F32), taps_ref[:, cols])
        head = group_here * HEADS_STEP + one
        skip = jnp.where(left[:1], skip_ref[head], skip_ref[head + 1])
        state = jnp.zeros((LANES, state_dim), F32)
        for block in range(blocks):
            at = slice(block * SPAN, (block + 1) * SPAN)
            x_here = x_conv[at]
            cb = cb_scr[block]
            d_one, d_two = decays[at, one : one + 1], decays[at, two : two + 1]
            mix_one = cb * jnp.exp(
                jnp.where(lower, d_one - rows_of[one : one + 1, at], -jnp.inf)
            )
            mix_two = cb * jnp.exp(
                jnp.where(lower, d_two - rows_of[two : two + 1, at], -jnp.inf)
            )
            decay = jnp.where(left, d_one, d_two)
            x_step = x_here * jnp.where(
                left, deltas[at, one : one + 1], deltas[at, two : two + 1]
            )
            short = x_step.astype(BF)
            zero = jnp.zeros_like(short)
            mixing = jnp.concatenate([mix_one.astype(BF), mix_two.astype(BF)], axis=1)
            spread = jnp.concatenate(
                [jnp.where(left, short, zero), jnp.where(left, zero, short)], axis=0
            )
            out = jnp.dot(mixing, spread, preferred_element_type=F32)
            if block:
                out = out + jnp.exp(decay) * lax.dot_general(
                    c_scr[at],
                    state.astype(BF),
                    (((1,), (1,)), ((), ())),
                    preferred_element_type=F32,
                )
            ending = decay[SPAN - 1 : SPAN]
            weighted = (x_step * jnp.exp(ending - decay)).astype(BF)
            fresh = lax.dot_general(
                weighted, b_scr[at], (((0,), (0,)), ((), ())), preferred_element_type=F32
            )
            if block:
                fade = jnp.where(
                    top,
                    jnp.exp(d_one[SPAN - 1 : SPAN]),
                    jnp.exp(d_two[SPAN - 1 : SPAN]),
                )
                fresh = fade * state + fresh
            state = fresh
            scanned_ref[at, cols] = out + skip * x_here
        state_ref[cols, :] = state


def scan(meta, projected, conv_weight, bias, log_rate, skip, width):
    rows, total = projected.shape
    seq = rows // 2
    state_dim = width // 2
    half = total - width - LANES
    inner = 2 * half
    cols = HEADS_STEP * LANES // 2
    groups = half // cols
    taps = conv_weight.shape[0]
    here = lambda r, g, m: (0, m[0] * groups + g)
    fixed = lambda r, g, m: (0, 0)
    grid_spec = pltpu.PrefetchScalarGridSpec(
        num_scalar_prefetch=1,
        grid=(2, groups),
        in_specs=[
            pl.BlockSpec((seq, cols), lambda r, g, m: (r, g)),
            pl.BlockSpec((seq, width + LANES), lambda r, g, m: (r, half // (width + LANES))),
            pl.BlockSpec((taps, cols), here),
            pl.BlockSpec((taps, width), lambda r, g, m: (0, inner // width)),
            pl.BlockSpec((1, LANES), fixed),
            pl.BlockSpec((1, LANES), fixed),
            pl.BlockSpec(memory_space=pltpu.SMEM),
        ],
        out_specs=[
            pl.BlockSpec((None, seq, cols), lambda r, g, m: (r, 0, g)),
            pl.BlockSpec((None, cols, state_dim), lambda r, g, m: (r, g, 0)),
        ],
        scratch_shapes=[
            pltpu.VMEM((2 * groups, seq, HEADS_STEP), F32),
            pltpu.VMEM((2 * groups, seq, HEADS_STEP), F32),
            pltpu.VMEM((2 * groups, HEADS_STEP, seq), F32),
            pltpu.VMEM((seq, state_dim), BF),
            pltpu.VMEM((seq, state_dim), BF),
            pltpu.VMEM((seq // SPAN, SPAN, SPAN), F32),
        ],
    )
    return pl.pallas_call(
        scan_kernel,
        grid_spec=grid_spec,
        out_shape=[
            pltpu.HBM((2, seq, half), F32),
            pltpu.HBM((2, half, state_dim), F32),
        ],
        compiler_params=pltpu.CompilerParams(
            dimension_semantics=("arbitrary", "arbitrary"), vmem_limit_bytes=24 << 20
        ),
        cost_estimate=pl.CostEstimate(
            flops=2 * inner * seq * 640, transcendentals=inner * seq * 6, bytes_accessed=9 << 20
        ),
        name="scan",
    )(meta, projected, projected, conv_weight, conv_weight, bias, log_rate, skip)


def project_kernel(tokens_ref, *refs):
    weight = jnp.concatenate([piece[...] for piece in refs[:-1]], axis=0)
    refs[-1][...] = jnp.dot(tokens_ref[...], weight, preferred_element_type=F32).astype(BF)


def project(tokens, pieces):
    rows, model = tokens.shape
    depth, total = pieces[0].shape
    steps = 3
    tile = total // steps
    return pl.pallas_call(
        project_kernel,
        grid=(steps,),
        in_specs=[pl.BlockSpec((rows, model), lambda n: (0, 0))]
        + [pl.BlockSpec((depth, tile), lambda n: (0, n)) for _ in pieces],
        out_specs=pl.BlockSpec((rows, tile), lambda n: (0, n)),
        out_shape=jax.ShapeDtypeStruct((rows, total), BF),
        compiler_params=pltpu.CompilerParams(
            dimension_semantics=("arbitrary",), vmem_limit_bytes=24 << 20
        ),
        cost_estimate=pl.CostEstimate(
            flops=2 * rows * model * total, transcendentals=0, bytes_accessed=10 << 20
        ),
        name="project",
    )(tokens, *pieces)


def gate_kernel(meta_ref, tokens_ref, scanned_ref, gain_ref, *refs):
    gated_ref, square_ref = refs[-2:]
    weight = jnp.concatenate([piece[...] for piece in refs[:-2]], axis=0)
    gate = jnp.dot(tokens_ref[...], weight, preferred_element_type=F32).astype(BF)
    gated = scanned_ref[...] * silu(gate.astype(F32))
    gated_ref[...] = (gated * gain_ref[...]).astype(BF)

    @pl.when(pl.program_id(0) == 0)
    def _():
        square_ref[...] = jnp.zeros_like(square_ref)

    square = gated * gated
    for at in range(0, square.shape[1], LANES):
        square_ref[...] += square[:, at : at + LANES]


def gating(which, meta, tokens, scanned, gain, pieces):
    _, seq, half = scanned.shape
    model = tokens.shape[1]
    depth = pieces[0].shape[0]
    steps = 3
    tile = half // steps
    return pl.pallas_call(
        gate_kernel,
        grid_spec=pltpu.PrefetchScalarGridSpec(
            num_scalar_prefetch=1,
            grid=(steps,),
            in_specs=[
                pl.BlockSpec((seq, model), lambda n, m: (which, 0)),
                pl.BlockSpec((None, seq, tile), lambda n, m: (which, 0, n)),
                pl.BlockSpec((1, tile), lambda n, m: (0, m[0] * steps + n)),
            ]
            + [pl.BlockSpec((depth, tile), lambda n, m: (0, n)) for _ in pieces],
            out_specs=[
                pl.BlockSpec((seq, tile), lambda n, m: (0, n)),
                pl.BlockSpec((seq, LANES), lambda n, m: (0, 0)),
            ],
        ),
        out_shape=[
            pltpu.HBM((seq, half), BF),
            pltpu.HBM((seq, LANES), F32),
        ],
        compiler_params=pltpu.CompilerParams(
            dimension_semantics=("arbitrary",), vmem_limit_bytes=24 << 20
        ),
        cost_estimate=pl.CostEstimate(
            flops=2 * seq * model * half, transcendentals=seq * half, bytes_accessed=10 << 20
        ),
        name="gating",
    )(meta, tokens, in_hbm(scanned), gain, *map(in_hbm, pieces))


def share_kernel(gated_ref, weight_ref, out_ref):
    out_ref[...] = lax.dot_general(
        gated_ref[...], weight_ref[...], (((1,), (1,)), ((), ())), preferred_element_type=F32
    )


def out_share(gated, weight):
    seq, half = gated.shape
    model = weight.shape[0]
    steps = 4
    tile = model // steps
    return pl.pallas_call(
        share_kernel,
        grid=(steps,),
        in_specs=[
            pl.BlockSpec((seq, half), lambda n: (0, 0)),
            pl.BlockSpec((tile, half), lambda n: (n, 0)),
        ],
        out_specs=pl.BlockSpec((seq, tile), lambda n: (0, n)),
        out_shape=jax.ShapeDtypeStruct((seq, model), F32),
        compiler_params=pltpu.CompilerParams(
            dimension_semantics=("arbitrary",), vmem_limit_bytes=24 << 20
        ),
        cost_estimate=pl.CostEstimate(
            flops=2 * seq * half * model, transcendentals=0, bytes_accessed=8 << 20
        ),
        name="out_share",
    )(in_hbm(gated), in_hbm(weight))


def mix_kernel(meta_ref, mine_ref, weight_ref, share_ref, sq_mine, sq_other, pick_ref, out_ref):
    seq = mine_ref.shape[0]
    inner = 2 * mine_ref.shape[1]
    total = share_ref[...] + lax.dot_general(
        mine_ref[...], weight_ref[...], (((1,), (1,)), ((), ())), preferred_element_type=F32
    )
    mean = jnp.sum(sq_mine[...] + sq_other[...], axis=1, keepdims=True) / inner
    live = lax.broadcasted_iota(jnp.int32, (seq, 1), 0) < meta_ref[1]
    scale = jnp.where(live, lax.rsqrt(mean + EPSILON), 0.0)
    short = (total * scale).astype(BF)
    out_ref[...] = jnp.dot(short, pick_ref[...], preferred_element_type=F32).astype(BF)


def mix(meta, mine, weight, share, sq_mine, sq_other):
    seq, half = mine.shape
    model = weight.shape[0]
    steps = 4
    tile = model // steps
    column = jnp.arange(tile, dtype=jnp.int32)
    chip, rest = column // (2 * SHARD_ROWS), column % (2 * SHARD_ROWS)
    place = rest // SHARD_ROWS * (tile // 2) + chip * SHARD_ROWS + rest % SHARD_ROWS
    pick = (place[:, None] == column[None]).astype(BF)
    fixed = lambda n, m: (0, 0)
    return pl.pallas_call(
        mix_kernel,
        grid_spec=pltpu.PrefetchScalarGridSpec(
            num_scalar_prefetch=1,
            grid=(steps,),
            in_specs=[
                pl.BlockSpec((seq, half), fixed),
                pl.BlockSpec((tile, half), lambda n, m: (n, 0)),
                pl.BlockSpec((seq, tile), lambda n, m: (0, n)),
                pl.BlockSpec((seq, LANES), fixed),
                pl.BlockSpec((seq, LANES), fixed),
                pl.BlockSpec((tile, tile), fixed),
            ],
            out_specs=pl.BlockSpec((seq, tile), lambda n, m: (0, n)),
        ),
        out_shape=jax.ShapeDtypeStruct((seq, model), BF),
        compiler_params=pltpu.CompilerParams(
            dimension_semantics=("arbitrary",), vmem_limit_bytes=24 << 20
        ),
        cost_estimate=pl.CostEstimate(
            flops=2 * seq * half * model, transcendentals=0, bytes_accessed=8 << 20
        ),
        name="mix",
    )(meta, in_hbm(mine), in_hbm(weight), share, sq_mine, sq_other, pick)


EVERYONE = ("req", "unit")
DEVICES = 128
CORE = 16
SHARD_ROWS = 12
COLOURS = 3
SAME_CORE = [[d for d in range(DEVICES) if d // CORE % 2 == core] for core in range(2)]
LINKS = (1 << 2, 1, 1 << 5, 3 << 2, 3, 3 << 5)


def link_of(colour, core, step):
    return LINKS[(colour + 3 * core + step) % 6]


def hop(value, mask_of):
    return lax.ppermute(
        value, EVERYONE, [(d, d ^ mask_of((d // CORE) % 2)) for d in range(DEVICES)]
    )


def swap(value):
    return hop(value, lambda core: CORE)


def moved_over(held, step):
    return [hop(piece, lambda core, c=c: link_of(c, core, step)) for c, piece in enumerate(held)]


def joined(held, moved):
    return [
        lax.optimization_barrier(jnp.concatenate([h, m], axis=0)) for h, m in zip(held, moved)
    ]


def row_sources(me, core):
    sources = []
    block = jnp.arange(64, dtype=jnp.int32)
    row = jnp.arange(8, dtype=jnp.int32)
    for colour in range(COLOURS):
        masks = []
        for side in range(2):
            mask = jnp.zeros_like(block)
            for step in range(6):
                mask = mask ^ (((block >> step) & 1) * link_of(colour, side, step))
            masks.append(mask)
        chip = (me ^ jnp.where(core == 0, masks[0], masks[1])) & ~CORE
        local = colour * 8 + row
        upper = (local >= SHARD_ROWS).astype(jnp.int32)
        device = chip[:, None] + CORE * upper[None]
        sources.append((device * SHARD_ROWS + (local - SHARD_ROWS * upper)[None]).reshape(-1))
    return jnp.concatenate(sources)


def body(
    tokens,
    lengths,
    gate_proj,
    input_proj,
    state_proj,
    step_proj,
    out_proj,
    conv_weight,
    step_bias,
    log_rate,
    skip_gain,
    norm_gain,
):
    unit_id = lax.axis_index("unit")
    me = lax.axis_index(EVERYONE).astype(jnp.int32)
    core = (me // CORE) % 2
    first_core = core == 0
    seq_len, model_dim = tokens.shape[1:]
    inner_dim = gate_proj.shape[1]
    head_count = log_rate.shape[0]
    head_dim = inner_dim // head_count
    width = state_proj.shape[1]
    half = inner_dim // 2
    spare = LANES - head_count

    cut = half + width + LANES
    side = jnp.pad(jnp.concatenate([state_proj, step_proj], axis=1), ((0, 0), (0, spare)))
    low = [input_proj[:, :half], side, gate_proj[:, :half], out_proj[:, :half]]
    high = [input_proj[:, half:], side, gate_proj[:, half:], out_proj[:, half:]]
    low = jnp.concatenate(low, axis=1).astype(BF)
    high = jnp.concatenate(high, axis=1).astype(BF)
    received = swap(jnp.where(first_core, high, low))
    kept = jnp.where(first_core, low, high)
    pair = jnp.concatenate(
        [jnp.where(first_core, kept, received), jnp.where(first_core, received, kept)], axis=0
    )
    out_weight = lax.all_gather(
        pair[:, cut + half :], EVERYONE, axis=0, tiled=True, axis_index_groups=SAME_CORE
    )
    pair = pair[:, : cut + half]
    held = [pair[8 * c : 8 * c + 8] for c in range(COLOURS)]
    for step in range(3):
        held = joined(held, moved_over(held, step))
    moved, unit_id = lax.optimization_barrier((moved_over(held, 3), unit_id))
    held = joined(held, moved)
    early, late = [h[:, :cut] for h in held], [h[:, cut:] for h in held]
    early = joined(early, moved_over(early, 4))
    moved, late = lax.optimization_barrier((moved_over(early, 5), late))
    early = [piece for both in zip(early, moved) for piece in both]
    late = joined(late, moved_over(late, 4))
    own = lax.dynamic_index_in_dim(tokens, unit_id, 0, keepdims=False)
    length = lax.dynamic_slice_in_dim(lengths, unit_id, 1, 0)
    coded = jnp.stack([length // 16, length % 16], axis=1).astype(BF)
    coded = jnp.pad(coded, ((0, 7), (0, model_dim - 2)))
    other = swap(jnp.concatenate([own, coded], axis=0))
    code = other[seq_len, :2].astype(jnp.int32)
    meta = jnp.stack([core, length[0], code[0] * 16 + code[1]])
    both = jnp.concatenate([own, other[:seq_len]], axis=0)
    pick = jnp.arange(model_dim, dtype=jnp.int32)[:, None] == row_sources(me, core)[None]
    both = jnp.dot(both, pick.astype(BF), preferred_element_type=F32).astype(BF)

    projected, late = lax.optimization_barrier((project(both, early), late))
    late = [piece for two in zip(late, moved_over(late, 5)) for piece in two]
    scanned, state = scan(
        meta,
        projected,
        conv_weight,
        jnp.pad(step_bias, (0, spare))[None],
        jnp.pad(log_rate, (0, spare))[None],
        skip_gain,
        width,
    )
    state_other = swap(state[1])
    gain = norm_gain[None]
    sent, square_sent = gating(1, meta, both, scanned, gain, late)
    share, square_other = swap(out_share(sent, out_weight)), swap(square_sent)
    mine, square = gating(0, meta, both, scanned, gain, late)
    mixed = mix(meta, mine, out_weight, share, square, square_other)
    state = jnp.concatenate(
        [jnp.where(first_core, state[0], state_other), jnp.where(first_core, state_other, state[0])]
    )
    return (mixed[None], state.reshape(1, head_count, head_dim, width // 2))


def solution(mesh):
    placed = (
        P("req", None, None),
        P("req"),
        P(("req", "unit"), None),
        P(("req", "unit"), None),
        P(("req", "unit"), None),
        P(("req", "unit"), None),
        P(("req", "unit"), None),
        P(),
        P(),
        P(),
        P(),
        P(),
    )
    return jax.shard_map(
        body,
        mesh=mesh,
        in_specs=placed,
        out_specs=(P(("req", "unit"), None, None), P(("req", "unit"), None, None, None)),
        check_vma=False,
    )
```

```python
import jax
import jax.numpy as jnp
from jax import lax
from jax.experimental import pallas as pl
from jax.experimental.pallas import tpu as pltpu
from jax.sharding import PartitionSpec as P

SPAN = 128
LANES = 128
HEADS_STEP = 8
EPSILON = 1e-05
BF = jnp.bfloat16
F32 = jnp.float32


def silu(v):
    h = 0.5 * v
    return h + h * jnp.tanh(h)


def causal_conv(values, taps):
    rows = lax.broadcasted_iota(jnp.int32, values.shape, 0)
    count = taps.shape[0]
    total = values * taps[count - 1 : count]
    for back in range(1, count):
        moved = jnp.where(rows >= back, pltpu.roll(values, back, 0), 0.0)
        total = total + moved * taps[count - 1 - back : count - back]
    return silu(total)


def scan_kernel(
    meta_ref,
    input_ref,
    side_ref,
    taps_ref,
    side_taps_ref,
    bias_ref,
    log_rate_ref,
    skip_ref,
    scanned_ref,
    state_ref,
    decay_col,
    delta_col,
    decay_row,
    b_scr,
    c_scr,
    cb_scr,
):
    which = pl.program_id(0)
    step = pl.program_id(1)
    seq = input_ref.shape[0]
    state_dim = side_taps_ref.shape[1] // 2
    groups = decay_col.shape[0]
    blocks = seq // SPAN
    position = lax.broadcasted_iota(jnp.int32, (seq, LANES), 0)
    group_here = meta_ref[0] * pl.num_programs(1) + step

    @pl.when(step == 0)
    def _():
        side = side_ref[...].astype(F32)
        conv = causal_conv(side[:, : 2 * state_dim], side_taps_ref[...])
        b_short = conv[:, :state_dim].astype(BF)
        c_short = conv[:, state_dim:].astype(BF)
        b_scr[...] = b_short
        c_scr[...] = c_short
        for block in range(blocks):
            at = slice(block * SPAN, (block + 1) * SPAN)
            cb_scr[block] = lax.dot_general(
                c_short[at], b_short[at], (((1,), (1,)), ((), ())), preferred_element_type=F32
            )
        raw = side[:, 2 * state_dim :] + bias_ref[...]
        live = (position < meta_ref[1 + which]).astype(F32)
        delta = (jnp.maximum(raw, 0.0) + jnp.log1p(jnp.exp(-jnp.abs(raw)))) * live
        total = delta * -jnp.exp(log_rate_ref[...])
        within = position % SPAN
        reach = 1
        while reach < SPAN:
            total = total + jnp.where(within >= reach, pltpu.roll(total, reach, 0), 0.0)
            reach *= 2
        turned = jnp.transpose(total)
        for group in range(groups):
            at = slice(group * HEADS_STEP, (group + 1) * HEADS_STEP)
            decay_col[group] = total[:, at]
            delta_col[group] = delta[:, at]
            decay_row[group] = turned[at]

    decays = decay_col[group_here]
    deltas = delta_col[group_here]
    rows_of = decay_row[group_here]
    lower = lax.broadcasted_iota(jnp.int32, (SPAN, SPAN), 0) >= lax.broadcasted_iota(
        jnp.int32, (SPAN, SPAN), 1
    )
    left = lax.broadcasted_iota(jnp.int32, (SPAN, LANES), 1) < LANES // 2
    top = lax.broadcasted_iota(jnp.int32, (LANES, state_dim), 0) < LANES // 2
    for pair in range(HEADS_STEP // 2):
        cols = slice(pair * LANES, (pair + 1) * LANES)
        one, two = 2 * pair, 2 * pair + 1
        x_conv = causal_conv(input_ref[:, cols].astype(F32), taps_ref[:, cols])
        head = group_here * HEADS_STEP + one
        skip = jnp.where(left[:1], skip_ref[head], skip_ref[head + 1])
        state = jnp.zeros((LANES, state_dim), F32)
        for block in range(blocks):
            at = slice(block * SPAN, (block + 1) * SPAN)
            x_here = x_conv[at]
            cb = cb_scr[block]
            d_one, d_two = decays[at, one : one + 1], decays[at, two : two + 1]
            mix_one = cb * jnp.exp(
                jnp.where(lower, d_one - rows_of[one : one + 1, at], -jnp.inf)
            )
            mix_two = cb * jnp.exp(
                jnp.where(lower, d_two - rows_of[two : two + 1, at], -jnp.inf)
            )
            decay = jnp.where(left, d_one, d_two)
            x_step = x_here * jnp.where(
                left, deltas[at, one : one + 1], deltas[at, two : two + 1]
            )
            short = x_step.astype(BF)
            zero = jnp.zeros_like(short)
            mixing = jnp.concatenate([mix_one.astype(BF), mix_two.astype(BF)], axis=1)
            spread = jnp.concatenate(
                [jnp.where(left, short, zero), jnp.where(left, zero, short)], axis=0
            )
            out = jnp.dot(mixing, spread, preferred_element_type=F32)
            if block:
                out = out + jnp.exp(decay) * lax.dot_general(
                    c_scr[at],
                    state.astype(BF),
                    (((1,), (1,)), ((), ())),
                    preferred_element_type=F32,
                )
            ending = decay[SPAN - 1 : SPAN]
            weighted = (x_step * jnp.exp(ending - decay)).astype(BF)
            fresh = lax.dot_general(
                weighted, b_scr[at], (((0,), (0,)), ((), ())), preferred_element_type=F32
            )
            if block:
                fade = jnp.where(
                    top,
                    jnp.exp(d_one[SPAN - 1 : SPAN]),
                    jnp.exp(d_two[SPAN - 1 : SPAN]),
                )
                fresh = fade * state + fresh
            state = fresh
            scanned_ref[at, cols] = out + skip * x_here
        state_ref[cols, :] = state


def scan(meta, projected, conv_weight, bias, log_rate, skip, width):
    rows, total = projected.shape
    seq = rows // 2
    state_dim = width // 2
    half = total - width - LANES
    inner = 2 * half
    cols = HEADS_STEP * LANES // 2
    groups = half // cols
    taps = conv_weight.shape[0]
    here = lambda r, g, m: (0, m[0] * groups + g)
    fixed = lambda r, g, m: (0, 0)
    grid_spec = pltpu.PrefetchScalarGridSpec(
        num_scalar_prefetch=1,
        grid=(2, groups),
        in_specs=[
            pl.BlockSpec((seq, cols), lambda r, g, m: (r, g)),
            pl.BlockSpec((seq, width + LANES), lambda r, g, m: (r, half // (width + LANES))),
            pl.BlockSpec((taps, cols), here),
            pl.BlockSpec((taps, width), lambda r, g, m: (0, inner // width)),
            pl.BlockSpec((1, LANES), fixed),
            pl.BlockSpec((1, LANES), fixed),
            pl.BlockSpec(memory_space=pltpu.SMEM),
        ],
        out_specs=[
            pl.BlockSpec((None, seq, cols), lambda r, g, m: (r, 0, g)),
            pl.BlockSpec((None, cols, state_dim), lambda r, g, m: (r, g, 0)),
        ],
        scratch_shapes=[
            pltpu.VMEM((2 * groups, seq, HEADS_STEP), F32),
            pltpu.VMEM((2 * groups, seq, HEADS_STEP), F32),
            pltpu.VMEM((2 * groups, HEADS_STEP, seq), F32),
            pltpu.VMEM((seq, state_dim), BF),
            pltpu.VMEM((seq, state_dim), BF),
            pltpu.VMEM((seq // SPAN, SPAN, SPAN), F32),
        ],
    )
    return pl.pallas_call(
        scan_kernel,
        grid_spec=grid_spec,
        out_shape=[
            jax.ShapeDtypeStruct((2, seq, half), F32),
            jax.ShapeDtypeStruct((2, half, state_dim), F32),
        ],
        compiler_params=pltpu.CompilerParams(
            dimension_semantics=("arbitrary", "arbitrary"), vmem_limit_bytes=24 << 20
        ),
        cost_estimate=pl.CostEstimate(
            flops=2 * inner * seq * 640, transcendentals=inner * seq * 6, bytes_accessed=9 << 20
        ),
        name="scan",
    )(meta, projected, projected, conv_weight, conv_weight, bias, log_rate, skip)


def project_kernel(tokens_ref, *refs):
    weight = jnp.concatenate([piece[...] for piece in refs[:-1]], axis=0)
    refs[-1][...] = jnp.dot(tokens_ref[...], weight, preferred_element_type=F32).astype(BF)


def project(tokens, pieces):
    rows, model = tokens.shape
    depth, total = pieces[0].shape
    steps = 3
    tile = total // steps
    return pl.pallas_call(
        project_kernel,
        grid=(steps,),
        in_specs=[pl.BlockSpec((rows, model), lambda n: (0, 0))]
        + [pl.BlockSpec((depth, tile), lambda n: (0, n)) for _ in pieces],
        out_specs=pl.BlockSpec((rows, tile), lambda n: (0, n)),
        out_shape=jax.ShapeDtypeStruct((rows, total), BF),
        compiler_params=pltpu.CompilerParams(
            dimension_semantics=("arbitrary",), vmem_limit_bytes=24 << 20
        ),
        cost_estimate=pl.CostEstimate(
            flops=2 * rows * model * total, transcendentals=0, bytes_accessed=10 << 20
        ),
        name="project",
    )(tokens, *pieces)


def gate_kernel(meta_ref, tokens_ref, scanned_ref, gain_ref, *refs):
    gated_ref, square_ref = refs[-2:]
    weight = jnp.concatenate([piece[...] for piece in refs[:-2]], axis=0)
    gate = jnp.dot(tokens_ref[...], weight, preferred_element_type=F32).astype(BF)
    gated = scanned_ref[...] * silu(gate.astype(F32))
    gated_ref[...] = (gated * gain_ref[...]).astype(BF)

    @pl.when(pl.program_id(0) == 0)
    def _():
        square_ref[...] = jnp.zeros_like(square_ref)

    square = gated * gated
    for at in range(0, square.shape[1], LANES):
        square_ref[...] += square[:, at : at + LANES]


def gating(which, meta, tokens, scanned, gain, pieces):
    _, seq, half = scanned.shape
    model = tokens.shape[1]
    depth = pieces[0].shape[0]
    steps = 3
    tile = half // steps
    return pl.pallas_call(
        gate_kernel,
        grid_spec=pltpu.PrefetchScalarGridSpec(
            num_scalar_prefetch=1,
            grid=(steps,),
            in_specs=[
                pl.BlockSpec((seq, model), lambda n, m: (which, 0)),
                pl.BlockSpec((None, seq, tile), lambda n, m: (which, 0, n)),
                pl.BlockSpec((1, tile), lambda n, m: (0, m[0] * steps + n)),
            ]
            + [pl.BlockSpec((depth, tile), lambda n, m: (0, n)) for _ in pieces],
            out_specs=[
                pl.BlockSpec((seq, tile), lambda n, m: (0, n)),
                pl.BlockSpec((seq, LANES), lambda n, m: (0, 0)),
            ],
        ),
        out_shape=[
            jax.ShapeDtypeStruct((seq, half), BF),
            jax.ShapeDtypeStruct((seq, LANES), F32),
        ],
        compiler_params=pltpu.CompilerParams(
            dimension_semantics=("arbitrary",), vmem_limit_bytes=24 << 20
        ),
        cost_estimate=pl.CostEstimate(
            flops=2 * seq * model * half, transcendentals=seq * half, bytes_accessed=10 << 20
        ),
        name="gating",
    )(meta, tokens, scanned, gain, *pieces)


def place_rows(places_ref, gated_ref, pieces, out_ref):
    step = pl.program_id(0)
    weight = jnp.concatenate([piece[...] for piece in pieces], axis=0)
    total = lax.dot_general(
        weight, gated_ref[...], (((1,), (1,)), ((), ())), preferred_element_type=F32
    )
    each = pieces[0].shape[0] // BLOCK_ROWS
    steps = pl.num_programs(0)
    for index in range(len(pieces)):
        for block in range(each):
            at = (index * each + block) * BLOCK_ROWS
            place = places_ref[(index * steps + step) * each + block]
            out_ref[pl.ds(pl.multiple_of(place, BLOCK_ROWS), BLOCK_ROWS), :] = total[
                at : at + BLOCK_ROWS
            ]


def share_kernel(places_ref, gated_ref, *refs):
    place_rows(places_ref, gated_ref, refs[:-1], refs[-1])


def out_share(places, gated, pieces):
    seq, half = gated.shape
    rows = pieces[0].shape[0]
    model = rows * len(pieces)
    steps = 4
    return pl.pallas_call(
        share_kernel,
        grid_spec=pltpu.PrefetchScalarGridSpec(
            num_scalar_prefetch=1,
            grid=(steps,),
            in_specs=[pl.BlockSpec((seq, half), lambda n, p: (0, 0))]
            + [pl.BlockSpec((rows // steps, half), lambda n, p: (n, 1)) for _ in pieces],
            out_specs=pl.BlockSpec((model, seq), lambda n, p: (0, 0)),
        ),
        out_shape=jax.ShapeDtypeStruct((model, seq), F32),
        compiler_params=pltpu.CompilerParams(
            dimension_semantics=("arbitrary",), vmem_limit_bytes=20 << 20
        ),
        cost_estimate=pl.CostEstimate(
            flops=2 * seq * half * model, transcendentals=0, bytes_accessed=8 << 20
        ),
        name="out_share",
    )(places, gated, *pieces)


def mix_kernel(meta_ref, places_ref, mine_ref, share_ref, sq_mine, sq_other, pick_ref, *refs):
    pieces, out_ref, total_scr = refs[:-2], refs[-2], refs[-1]
    place_rows(places_ref, mine_ref, pieces, total_scr)

    @pl.when(pl.program_id(0) == pl.num_programs(0) - 1)
    def _():
        seq = mine_ref.shape[0]
        inner = 2 * mine_ref.shape[1]
        squares = jnp.transpose(sq_mine[...] + sq_other[...])
        mean = jnp.sum(squares, axis=0, keepdims=True) / inner
        live = lax.broadcasted_iota(jnp.int32, (1, seq), 1) < meta_ref[1]
        scale = jnp.where(live, lax.rsqrt(mean + EPSILON), 0.0)
        tile = pick_ref.shape[0]
        for at in range(0, out_ref.shape[1], tile):
            rows = slice(at, at + tile)
            short = ((total_scr[rows] + share_ref[rows]) * scale).astype(BF)
            out_ref[:, rows] = lax.dot_general(
                short, pick_ref[...], (((0,), (0,)), ((), ())), preferred_element_type=F32
            ).astype(BF)


def mix(meta, places, mine, share, sq_mine, sq_other, pieces):
    seq, half = mine.shape
    rows = pieces[0].shape[0]
    model = rows * len(pieces)
    steps = 4
    tile = model // 4
    column = jnp.arange(tile, dtype=jnp.int32)
    chip, rest = column // (2 * SHARD_ROWS), column % (2 * SHARD_ROWS)
    target = rest // SHARD_ROWS * (tile // 2) + chip * SHARD_ROWS + rest % SHARD_ROWS
    pick = (target[:, None] == column[None]).astype(BF)
    fixed = lambda n, m, p: (0, 0)
    return pl.pallas_call(
        mix_kernel,
        grid_spec=pltpu.PrefetchScalarGridSpec(
            num_scalar_prefetch=2,
            grid=(steps,),
            in_specs=[
                pl.BlockSpec((seq, half), fixed),
                pl.BlockSpec((model, seq), fixed),
                pl.BlockSpec((seq, LANES), fixed),
                pl.BlockSpec((seq, LANES), fixed),
                pl.BlockSpec((tile, tile), fixed),
            ]
            + [pl.BlockSpec((rows // steps, half), lambda n, m, p: (n, 1)) for _ in pieces],
            out_specs=pl.BlockSpec((seq, model), fixed),
            scratch_shapes=[pltpu.VMEM((model, seq), F32)],
        ),
        out_shape=jax.ShapeDtypeStruct((seq, model), BF),
        compiler_params=pltpu.CompilerParams(
            dimension_semantics=("arbitrary",), vmem_limit_bytes=24 << 20
        ),
        cost_estimate=pl.CostEstimate(
            flops=2 * seq * half * model, transcendentals=0, bytes_accessed=8 << 20
        ),
        name="mix",
    )(meta, places, mine, share, sq_mine, sq_other, pick, *pieces)


EVERYONE = ("req", "unit")
DEVICES = 128
CORE = 16
SHARD_ROWS = 12
COLOURS = 3
BLOCK_ROWS = 8
LINKS = (1 << 2, 1, 1 << 5, 3 << 2, 3, 3 << 5)


def link_of(colour, core, step):
    return LINKS[(colour + 3 * core + step) % 6]


def hop(value, mask_of):
    return lax.ppermute(
        value, EVERYONE, [(d, d ^ mask_of((d // CORE) % 2)) for d in range(DEVICES)]
    )


def swap(value):
    return hop(value, lambda core: CORE)


def moved_over(held, step):
    return [hop(piece, lambda core, c=c: link_of(c, core, step)) for c, piece in enumerate(held)]


def joined(held, moved):
    return [
        lax.optimization_barrier(jnp.concatenate([h, m], axis=0)) for h, m in zip(held, moved)
    ]


def gathered_chip(me, core, colour, block):
    mask = jnp.zeros_like(block)
    for step in range(6):
        link = jnp.zeros_like(block)
        for c in range(COLOURS):
            here = jnp.where(core == 0, link_of(c, 0, step), link_of(c, 1, step))
            link = jnp.where(colour == c, here, link)
        mask = mask ^ (((block >> step) & 1) * link)
    return (me ^ mask) & ~CORE


def row_sources(me, core, model):
    row = jnp.arange(model, dtype=jnp.int32)
    colour, block = row // (model // COLOURS), row // BLOCK_ROWS % 64
    local = colour * BLOCK_ROWS + row % BLOCK_ROWS
    upper = (local >= SHARD_ROWS).astype(jnp.int32)
    device = gathered_chip(me, core, colour, block) + CORE * upper
    return device * SHARD_ROWS + local - SHARD_ROWS * upper


def row_places(me, core):
    index = jnp.arange(COLOURS * 64, dtype=jnp.int32)
    chip = gathered_chip(me, core, index // 64, index % 64)
    chip = (chip >> 5) * CORE + (chip & (CORE - 1))
    return chip * 2 * SHARD_ROWS + index // 64 * BLOCK_ROWS


def body(
    tokens,
    lengths,
    gate_proj,
    input_proj,
    state_proj,
    step_proj,
    out_proj,
    conv_weight,
    step_bias,
    log_rate,
    skip_gain,
    norm_gain,
):
    unit_id = lax.axis_index("unit")
    me = lax.axis_index(EVERYONE).astype(jnp.int32)
    core = (me // CORE) % 2
    first_core = core == 0
    seq_len, model_dim = tokens.shape[1:]
    inner_dim = gate_proj.shape[1]
    head_count = log_rate.shape[0]
    head_dim = inner_dim // head_count
    width = state_proj.shape[1]
    half = inner_dim // 2
    spare = LANES - head_count

    cut = half + width + LANES
    length = lax.dynamic_slice_in_dim(lengths, unit_id, 1, 0)
    coded = jnp.stack([length // 16, length % 16], axis=1).astype(F32)
    coded = jnp.pad(coded, ((0, SHARD_ROWS - 1), (0, spare - 2)))
    side = jnp.concatenate([state_proj, step_proj, coded], axis=1)
    low = [input_proj[:, :half], side, gate_proj[:, :half], out_proj[:, :half]]
    high = [input_proj[:, half:], side, gate_proj[:, half:], out_proj[:, half:]]
    low = jnp.concatenate(low, axis=1).astype(BF)
    high = jnp.concatenate(high, axis=1).astype(BF)
    received = swap(jnp.where(first_core, high, low))
    code = received[0, cut - spare : cut - spare + 2].astype(jnp.int32)
    meta = jnp.stack([core, length[0], code[0] * 16 + code[1]])

    kept = jnp.where(first_core, low, high)
    pair = jnp.concatenate(
        [jnp.where(first_core, kept, received), jnp.where(first_core, received, kept)], axis=0
    )
    held = [pair[8 * c : 8 * c + 8] for c in range(COLOURS)]
    for step in range(4):
        if step == 3:
            held, unit_id = lax.optimization_barrier((held, unit_id))
        held = joined(held, moved_over(held, step))
    moved = moved_over(held, 4)

    own = lax.dynamic_index_in_dim(tokens, unit_id, 0, keepdims=False)
    both = jnp.concatenate([own, swap(own)], axis=0)
    pick = jnp.arange(model_dim, dtype=jnp.int32)[:, None] == row_sources(me, core, model_dim)[None]
    both = jnp.dot(both, pick.astype(BF), preferred_element_type=F32).astype(BF)
    small = (meta, row_places(me, core), jnp.pad(step_bias, (0, spare)), jnp.pad(log_rate, (0, spare)))
    moved, both, small = lax.optimization_barrier((moved, both, small))
    meta, places, bias, log_rate = small

    early = joined([h[:, :cut] for h in held], [m[:, :cut] for m in moved])
    late = joined([h[:, cut:] for h in held], [m[:, cut:] for m in moved])
    moved, late = lax.optimization_barrier((moved_over(early, 5), late))
    early = [piece for two in zip(early, moved) for piece in two]
    late = [piece for two in zip(late, moved_over(late, 5)) for piece in two]

    projected = project(both, early)
    scanned, state = scan(
        meta,
        projected,
        conv_weight,
        bias[None],
        log_rate[None],
        skip_gain,
        width,
    )
    state_other = swap(state[1])
    gain = norm_gain[None]
    sent, square_sent = gating(1, meta, both, scanned, gain, late)
    share, square_other = swap(out_share(places, sent, late)), swap(square_sent)
    mine, square = gating(0, meta, both, scanned, gain, late)
    mixed = mix(meta, places, mine, share, square, square_other, late)
    state = jnp.concatenate(
        [jnp.where(first_core, state[0], state_other), jnp.where(first_core, state_other, state[0])]
    )
    return (mixed[None], state.reshape(1, head_count, head_dim, width // 2))


def solution(mesh):
    placed = (
        P("req", None, None),
        P("req"),
        P(("req", "unit"), None),
        P(("req", "unit"), None),
        P(("req", "unit"), None),
        P(("req", "unit"), None),
        P(("req", "unit"), None),
        P(),
        P(),
        P(),
        P(),
        P(),
    )
    return jax.shard_map(
        body,
        mesh=mesh,
        in_specs=placed,
        out_specs=(P(("req", "unit"), None, None), P(("req", "unit"), None, None, None)),
        check_vma=False,
    )
```

```python
import functools

import jax
import jax.numpy as jnp
from jax import lax
from jax.experimental import pallas as pl
from jax.experimental.pallas import tpu as pltpu
from jax.sharding import PartitionSpec as P

SPAN = 128
LANES = 128
HEADS_STEP = 8
EPSILON = 1e-05
BF = jnp.bfloat16
F32 = jnp.float32


def silu(v):
    h = 0.5 * v
    return h + h * jnp.tanh(h)


def causal_conv(values, taps):
    rows = lax.broadcasted_iota(jnp.int32, (BLOCK_ROWS, values.shape[1]), 0)
    count = taps.shape[0]
    total = values * taps[count - 1 : count]
    for back in range(1, count):
        moved = pltpu.roll(values, back, 0)
        moved = jnp.concatenate(
            [jnp.where(rows >= back, moved[:BLOCK_ROWS], 0.0), moved[BLOCK_ROWS:]], axis=0
        )
        total = total + moved * taps[count - 1 - back : count - back]
    return silu(total)


def scan_kernel(
    which,
    meta_ref,
    input_ref,
    side_ref,
    taps_ref,
    side_taps_ref,
    bias_ref,
    log_rate_ref,
    skip_ref,
    scanned_ref,
    state_ref,
    decay_col,
    delta_col,
    decay_row,
    b_scr,
    c_scr,
    cb_scr,
):
    step = pl.program_id(0)
    seq = input_ref.shape[0]
    state_dim = side_taps_ref.shape[1] // 2
    groups = decay_col.shape[0]
    blocks = seq // SPAN
    position = lax.broadcasted_iota(jnp.int32, (seq, LANES), 0)
    group_here = meta_ref[0] * pl.num_programs(0) + step

    @pl.when(step == 0)
    def _():
        side = side_ref[...].astype(F32)
        conv = causal_conv(side[:, : 2 * state_dim], side_taps_ref[...])
        b_short = conv[:, :state_dim].astype(BF)
        c_short = conv[:, state_dim:].astype(BF)
        b_scr[...] = b_short
        c_scr[...] = c_short
        for block in range(blocks):
            at = slice(block * SPAN, (block + 1) * SPAN)
            cb_scr[block] = lax.dot_general(
                c_short[at], b_short[at], (((1,), (1,)), ((), ())), preferred_element_type=F32
            )
        spare = jnp.zeros((1, LANES - bias_ref.shape[1]), F32)
        raw = side[:, 2 * state_dim :] + jnp.concatenate([bias_ref[...], spare], axis=1)
        live = (position < meta_ref[1 + which]).astype(F32)
        delta = (jnp.maximum(raw, 0.0) + jnp.log1p(jnp.exp(-jnp.abs(raw)))) * live
        total = delta * -jnp.exp(jnp.concatenate([log_rate_ref[...], spare], axis=1))
        within = position % SPAN
        reach = 1
        while reach < SPAN:
            total = total + jnp.where(within >= reach, pltpu.roll(total, reach, 0), 0.0)
            reach *= 2
        turned = jnp.transpose(total)
        for group in range(groups):
            at = slice(group * HEADS_STEP, (group + 1) * HEADS_STEP)
            decay_col[group] = total[:, at]
            delta_col[group] = delta[:, at]
            decay_row[group] = turned[at]

    decays = decay_col[group_here]
    deltas = delta_col[group_here]
    rows_of = decay_row[group_here]
    lower = lax.broadcasted_iota(jnp.int32, (SPAN, SPAN), 0) >= lax.broadcasted_iota(
        jnp.int32, (SPAN, SPAN), 1
    )
    left = lax.broadcasted_iota(jnp.int32, (SPAN, LANES), 1) < LANES // 2
    top = lax.broadcasted_iota(jnp.int32, (LANES, state_dim), 0) < LANES // 2
    for pair in range(HEADS_STEP // 2):
        cols = slice(pair * LANES, (pair + 1) * LANES)
        one, two = 2 * pair, 2 * pair + 1
        x_conv = causal_conv(input_ref[:, cols].astype(F32), taps_ref[:, cols])
        head = group_here * HEADS_STEP + one
        skip = jnp.where(left[:1], skip_ref[head], skip_ref[head + 1])
        state = jnp.zeros((LANES, state_dim), F32)
        for block in range(blocks):
            at = slice(block * SPAN, (block + 1) * SPAN)
            x_here = x_conv[at]
            cb = cb_scr[block]
            d_one, d_two = decays[at, one : one + 1], decays[at, two : two + 1]
            mix_one = cb * jnp.exp(
                jnp.where(lower, d_one - rows_of[one : one + 1, at], -jnp.inf)
            )
            mix_two = cb * jnp.exp(
                jnp.where(lower, d_two - rows_of[two : two + 1, at], -jnp.inf)
            )
            decay = jnp.where(left, d_one, d_two)
            x_step = x_here * jnp.where(
                left, deltas[at, one : one + 1], deltas[at, two : two + 1]
            )
            short = x_step.astype(BF)
            zero = jnp.zeros_like(short)
            mixing = jnp.concatenate([mix_one.astype(BF), mix_two.astype(BF)], axis=1)
            spread = jnp.concatenate(
                [jnp.where(left, short, zero), jnp.where(left, zero, short)], axis=0
            )
            out = jnp.dot(mixing, spread, preferred_element_type=F32)
            if block:
                out = out + jnp.exp(decay) * lax.dot_general(
                    c_scr[at],
                    state.astype(BF),
                    (((1,), (1,)), ((), ())),
                    preferred_element_type=F32,
                )
            ending = decay[SPAN - 1 : SPAN]
            weighted = (x_step * jnp.exp(ending - decay)).astype(BF)
            fresh = lax.dot_general(
                weighted, b_scr[at], (((0,), (0,)), ((), ())), preferred_element_type=F32
            )
            if block:
                fade = jnp.where(
                    top,
                    jnp.exp(d_one[SPAN - 1 : SPAN]),
                    jnp.exp(d_two[SPAN - 1 : SPAN]),
                )
                fresh = fade * state + fresh
            state = fresh
            scanned_ref[at, cols] = out + skip * x_here
        state_ref[cols, :] = state


def scan(which, meta, projected, conv_weight, bias, log_rate, skip, width):
    rows, total = projected.shape
    seq = rows // 2
    state_dim = width // 2
    half = total - width - LANES
    inner = 2 * half
    cols = HEADS_STEP * LANES // 2
    groups = half // cols
    taps, heads = conv_weight.shape[0], bias.shape[1]
    here = lambda g, m: (0, m[0] * groups + g)
    fixed = lambda g, m: (0, 0)
    grid_spec = pltpu.PrefetchScalarGridSpec(
        num_scalar_prefetch=1,
        grid=(groups,),
        in_specs=[
            pl.BlockSpec((seq, cols), lambda g, m: (which, g)),
            pl.BlockSpec((seq, width + LANES), lambda g, m: (which, half // (width + LANES))),
            pl.BlockSpec((taps, cols), here),
            pl.BlockSpec((taps, width), lambda g, m: (0, inner // width)),
            pl.BlockSpec((1, heads), fixed),
            pl.BlockSpec((1, heads), fixed),
            pl.BlockSpec(memory_space=pltpu.SMEM),
        ],
        out_specs=[
            pl.BlockSpec((seq, cols), lambda g, m: (0, g)),
            pl.BlockSpec((cols, state_dim), lambda g, m: (g, 0)),
        ],
        scratch_shapes=[
            pltpu.VMEM((2 * groups, seq, HEADS_STEP), F32),
            pltpu.VMEM((2 * groups, seq, HEADS_STEP), F32),
            pltpu.VMEM((2 * groups, HEADS_STEP, seq), F32),
            pltpu.VMEM((seq, state_dim), BF),
            pltpu.VMEM((seq, state_dim), BF),
            pltpu.VMEM((seq // SPAN, SPAN, SPAN), F32),
        ],
    )
    return pl.pallas_call(
        functools.partial(scan_kernel, which),
        grid_spec=grid_spec,
        out_shape=[
            jax.ShapeDtypeStruct((seq, half), F32),
            jax.ShapeDtypeStruct((half, state_dim), F32),
        ],
        compiler_params=pltpu.CompilerParams(
            dimension_semantics=("arbitrary",), vmem_limit_bytes=24 << 20
        ),
        cost_estimate=pl.CostEstimate(
            flops=inner * seq * 640, transcendentals=inner * seq * 3, bytes_accessed=5 << 20
        ),
        name="scan",
    )(meta, projected, projected, conv_weight, conv_weight, bias, log_rate, skip)


def shards_kernel(
    meta_ref, lengths_ref, input_ref, state_ref, step_ref, gate_ref, out_ref, kept_ref, sent_ref
):
    rows, half = input_ref.shape[0], input_ref.shape[1] // 2
    width, heads = state_ref.shape[1], step_ref.shape[1]
    length = lengths_ref[meta_ref[1]]
    row = lax.broadcasted_iota(jnp.int32, (rows, LANES), 0)
    lane = lax.broadcasted_iota(jnp.int32, (rows, LANES), 1)
    coded = jnp.where(lane == heads, length >> 4, jnp.where(lane == heads + 1, length & 15, 0))
    coded = jnp.where(row == 0, coded, 0).astype(F32).astype(BF)
    for ref, core in ((kept_ref, meta_ref[0]), (sent_ref, 1 - meta_ref[0])):
        at = pl.ds(pl.multiple_of(core * half, half), half)
        ref[:, :half] = input_ref[:, at].astype(BF)
        ref[:, half : half + width] = state_ref[...].astype(BF)
        ref[:, half + width : half + width + LANES] = coded
        ref[:, half + width : half + width + heads] = step_ref[...].astype(BF)
        start = half + width + LANES
        ref[:, start : start + half] = gate_ref[:, at].astype(BF)
        ref[:, start + half :] = out_ref[:, at].astype(BF)


def shards(meta, lengths, inputs, state, step, gate, out):
    rows, inner = inputs.shape
    total = 3 * (inner // 2) + state.shape[1] + LANES
    scalars = pl.BlockSpec(memory_space=pltpu.SMEM)
    whole = pl.BlockSpec(memory_space=pltpu.VMEM)
    return pl.pallas_call(
        shards_kernel,
        in_specs=[scalars] * 2 + [whole] * 5,
        out_specs=[whole] * 2,
        out_shape=[jax.ShapeDtypeStruct((rows, total), BF)] * 2,
        name="shards",
    )(meta, lengths, inputs, state, step, gate, out)


def project_kernel(tokens_ref, *refs):
    weight = jnp.concatenate([piece[...] for piece in refs[:-1]], axis=0)
    refs[-1][...] = jnp.dot(tokens_ref[...], weight, preferred_element_type=F32).astype(BF)


def project(tokens, pieces):
    rows, model = tokens.shape
    depth, total = pieces[0].shape
    steps = 3
    tile = total // steps
    return pl.pallas_call(
        project_kernel,
        grid=(steps,),
        in_specs=[pl.BlockSpec((rows, model), lambda n: (0, 0))]
        + [pl.BlockSpec((depth, tile), lambda n: (0, n)) for _ in pieces],
        out_specs=pl.BlockSpec((rows, tile), lambda n: (0, n)),
        out_shape=jax.ShapeDtypeStruct((rows, total), BF),
        compiler_params=pltpu.CompilerParams(
            dimension_semantics=("arbitrary",), vmem_limit_bytes=24 << 20
        ),
        cost_estimate=pl.CostEstimate(
            flops=2 * rows * model * total, transcendentals=0, bytes_accessed=10 << 20
        ),
        name="project",
    )(tokens, *pieces)


def gate_kernel(meta_ref, tokens_ref, scanned_ref, gain_ref, *refs):
    gated_ref, square_ref = refs[-2:]
    weight = jnp.concatenate([piece[...] for piece in refs[:-2]], axis=0)
    gate = jnp.dot(tokens_ref[...], weight, preferred_element_type=F32).astype(BF)
    gated = scanned_ref[...] * silu(gate.astype(F32))
    gated_ref[...] = (gated * gain_ref[...]).astype(BF)

    @pl.when(pl.program_id(0) == 0)
    def _():
        square_ref[...] = jnp.zeros_like(square_ref)

    square = gated * gated
    for at in range(0, square.shape[1], LANES):
        square_ref[...] += square[:, at : at + LANES]


def gating(which, meta, tokens, scanned, gain, pieces):
    seq, half = scanned.shape
    model = tokens.shape[1]
    depth = pieces[0].shape[0]
    steps = 3
    tile = half // steps
    return pl.pallas_call(
        gate_kernel,
        grid_spec=pltpu.PrefetchScalarGridSpec(
            num_scalar_prefetch=1,
            grid=(steps,),
            in_specs=[
                pl.BlockSpec((seq, model), lambda n, m: (which, 0)),
                pl.BlockSpec((seq, tile), lambda n, m: (0, n)),
                pl.BlockSpec((1, tile), lambda n, m: (0, m[0] * steps + n)),
            ]
            + [pl.BlockSpec((depth, tile), lambda n, m: (0, n)) for _ in pieces],
            out_specs=[
                pl.BlockSpec((seq, tile), lambda n, m: (0, n)),
                pl.BlockSpec((seq, LANES), lambda n, m: (0, 0)),
            ],
        ),
        out_shape=[
            jax.ShapeDtypeStruct((seq, half), BF),
            jax.ShapeDtypeStruct((seq, LANES), F32),
        ],
        compiler_params=pltpu.CompilerParams(
            dimension_semantics=("arbitrary",), vmem_limit_bytes=24 << 20
        ),
        cost_estimate=pl.CostEstimate(
            flops=2 * seq * model * half, transcendentals=seq * half, bytes_accessed=10 << 20
        ),
        name="gating",
    )(meta, tokens, scanned, gain, *pieces)


def place_rows(places_ref, gated_ref, pieces, out_ref):
    step = pl.program_id(0)
    weight = jnp.concatenate([piece[...] for piece in pieces], axis=0)
    total = lax.dot_general(
        weight, gated_ref[...], (((1,), (1,)), ((), ())), preferred_element_type=F32
    )
    each = pieces[0].shape[0] // BLOCK_ROWS
    steps = pl.num_programs(0)
    for index in range(len(pieces)):
        for block in range(each):
            at = (index * each + block) * BLOCK_ROWS
            place = places_ref[(index * steps + step) * each + block]
            out_ref[pl.ds(pl.multiple_of(place, BLOCK_ROWS), BLOCK_ROWS), :] = total[
                at : at + BLOCK_ROWS
            ]


def share_kernel(places_ref, gated_ref, *refs):
    place_rows(places_ref, gated_ref, refs[:-1], refs[-1])


def out_share(places, gated, pieces):
    seq, half = gated.shape
    rows = pieces[0].shape[0]
    model = rows * len(pieces)
    steps = 4
    return pl.pallas_call(
        share_kernel,
        grid_spec=pltpu.PrefetchScalarGridSpec(
            num_scalar_prefetch=1,
            grid=(steps,),
            in_specs=[pl.BlockSpec((seq, half), lambda n, p: (0, 0))]
            + [pl.BlockSpec((rows // steps, half), lambda n, p: (n, 1)) for _ in pieces],
            out_specs=pl.BlockSpec((model, seq), lambda n, p: (0, 0)),
        ),
        out_shape=jax.ShapeDtypeStruct((model, seq), F32),
        compiler_params=pltpu.CompilerParams(
            dimension_semantics=("arbitrary",), vmem_limit_bytes=20 << 20
        ),
        cost_estimate=pl.CostEstimate(
            flops=2 * seq * half * model, transcendentals=0, bytes_accessed=8 << 20
        ),
        name="out_share",
    )(places, gated, *pieces)


def mix_kernel(meta_ref, places_ref, mine_ref, share_ref, sq_mine, sq_other, pick_ref, *refs):
    pieces, out_ref, total_scr = refs[:-2], refs[-2], refs[-1]
    place_rows(places_ref, mine_ref, pieces, total_scr)

    @pl.when(pl.program_id(0) == pl.num_programs(0) - 1)
    def _():
        seq = mine_ref.shape[0]
        inner = 2 * mine_ref.shape[1]
        squares = jnp.transpose(sq_mine[...] + sq_other[...])
        mean = jnp.sum(squares, axis=0, keepdims=True) / inner
        live = lax.broadcasted_iota(jnp.int32, (1, seq), 1) < meta_ref[1]
        scale = jnp.where(live, lax.rsqrt(mean + EPSILON), 0.0)
        tile = pick_ref.shape[0]
        for at in range(0, out_ref.shape[1], tile):
            rows = slice(at, at + tile)
            short = ((total_scr[rows] + share_ref[rows]) * scale).astype(BF)
            out_ref[:, rows] = lax.dot_general(
                short, pick_ref[...], (((0,), (0,)), ((), ())), preferred_element_type=F32
            ).astype(BF)


def mix(meta, places, mine, share, sq_mine, sq_other, pieces):
    seq, half = mine.shape
    rows = pieces[0].shape[0]
    model = rows * len(pieces)
    steps = 4
    tile = model // 4
    column = jnp.arange(tile, dtype=jnp.int32)
    chip, rest = column // (2 * SHARD_ROWS), column % (2 * SHARD_ROWS)
    target = rest // SHARD_ROWS * (tile // 2) + chip * SHARD_ROWS + rest % SHARD_ROWS
    pick = (target[:, None] == column[None]).astype(BF)
    fixed = lambda n, m, p: (0, 0)
    return pl.pallas_call(
        mix_kernel,
        grid_spec=pltpu.PrefetchScalarGridSpec(
            num_scalar_prefetch=2,
            grid=(steps,),
            in_specs=[
                pl.BlockSpec((seq, half), fixed),
                pl.BlockSpec((model, seq), fixed),
                pl.BlockSpec((seq, LANES), fixed),
                pl.BlockSpec((seq, LANES), fixed),
                pl.BlockSpec((tile, tile), fixed),
            ]
            + [pl.BlockSpec((rows // steps, half), lambda n, m, p: (n, 1)) for _ in pieces],
            out_specs=pl.BlockSpec((seq, model), fixed),
            scratch_shapes=[pltpu.VMEM((model, seq), F32)],
        ),
        out_shape=jax.ShapeDtypeStruct((seq, model), BF),
        compiler_params=pltpu.CompilerParams(
            dimension_semantics=("arbitrary",), vmem_limit_bytes=24 << 20
        ),
        cost_estimate=pl.CostEstimate(
            flops=2 * seq * half * model, transcendentals=0, bytes_accessed=8 << 20
        ),
        name="mix",
    )(meta, places, mine, share, sq_mine, sq_other, pick, *pieces)


EVERYONE = ("req", "unit")
DEVICES = 128
CORE = 16
SHARD_ROWS = 12
COLOURS = 3
BLOCK_ROWS = 8
LINKS = (1 << 2, 1, 1 << 5, 3 << 2, 3, 3 << 5)


def link_of(colour, core, step):
    return LINKS[(colour + 3 * core + step) % 6]


def hop(value, mask_of):
    return lax.ppermute(
        value, EVERYONE, [(d, d ^ mask_of((d // CORE) % 2)) for d in range(DEVICES)]
    )


def swap(value):
    return hop(value, lambda core: CORE)


def moved_over(held, step):
    return [hop(piece, lambda core, c=c: link_of(c, core, step)) for c, piece in enumerate(held)]


def joined(held, moved):
    return [
        lax.optimization_barrier(jnp.concatenate([h, m], axis=0)) for h, m in zip(held, moved)
    ]


def gathered_chip(me, core, colour, block):
    mask = jnp.zeros_like(block)
    for step in range(6):
        link = jnp.zeros_like(block)
        for c in range(COLOURS):
            here = jnp.where(core == 0, link_of(c, 0, step), link_of(c, 1, step))
            link = jnp.where(colour == c, here, link)
        mask = mask ^ (((block >> step) & 1) * link)
    return (me ^ mask) & ~CORE


def row_sources(me, core, model):
    row = jnp.arange(model, dtype=jnp.int32)
    colour, block = row // (model // COLOURS), row // BLOCK_ROWS % 64
    local = colour * BLOCK_ROWS + row % BLOCK_ROWS
    upper = (local >= SHARD_ROWS).astype(jnp.int32)
    device = gathered_chip(me, core, colour, block) + CORE * upper
    return device * SHARD_ROWS + local - SHARD_ROWS * upper


def row_places(me, core):
    index = jnp.arange(COLOURS * 64, dtype=jnp.int32)
    chip = gathered_chip(me, core, index // 64, index % 64)
    chip = (chip >> 5) * CORE + (chip & (CORE - 1))
    return chip * 2 * SHARD_ROWS + index // 64 * BLOCK_ROWS


def body(
    tokens,
    lengths,
    gate_proj,
    input_proj,
    state_proj,
    step_proj,
    out_proj,
    conv_weight,
    step_bias,
    log_rate,
    skip_gain,
    norm_gain,
):
    unit_id = lax.axis_index("unit")
    me = lax.axis_index(EVERYONE).astype(jnp.int32)
    core = (me // CORE) % 2
    first_core = core == 0
    seq_len, model_dim = tokens.shape[1:]
    inner_dim = gate_proj.shape[1]
    head_count = log_rate.shape[0]
    head_dim = inner_dim // head_count
    width = state_proj.shape[1]
    half = inner_dim // 2
    spare = LANES - head_count

    cut = half + width + LANES
    kept, sent = shards(
        jnp.stack([core, unit_id]), lengths, input_proj, state_proj, step_proj, gate_proj, out_proj
    )
    received = swap(sent)
    pair = jnp.concatenate(
        [jnp.where(first_core, kept, received), jnp.where(first_core, received, kept)], axis=0
    )
    held = [pair[8 * c : 8 * c + 8] for c in range(COLOURS)]
    for step in range(4):
        if step == 3:
            held, unit_id, kept, received = lax.optimization_barrier((held, unit_id, kept, received))
        held = joined(held, moved_over(held, step))
    early, late = [h[:, :cut] for h in held], [h[:, cut:] for h in held]
    early = joined(early, moved_over(early, 4))
    moved = moved_over(early, 5)

    own = lax.dynamic_index_in_dim(tokens, unit_id, 0, keepdims=False)
    both = jnp.concatenate([own, swap(own)], axis=0)
    pick = jnp.arange(model_dim, dtype=jnp.int32)[:, None] == row_sources(me, core, model_dim)[None]
    both = jnp.dot(both, pick.astype(BF), preferred_element_type=F32).astype(BF)
    codes = cut - spare
    codes = [part[0, codes : codes + 2].astype(jnp.int32) for part in (kept, received)]
    meta = jnp.stack([core] + [code[0] * 16 + code[1] for code in codes])
    small = (meta, row_places(me, core))
    moved[0], both, small = lax.optimization_barrier((moved[0], both, small))
    meta, places = small
    for c in range(COLOURS):
        moved[c], late[c] = lax.optimization_barrier((moved[c], late[c]))
    early = [piece for two in zip(early, moved) for piece in two]

    late = joined(late, moved_over(late, 4))
    projected, late = lax.optimization_barrier((project(both, early), late))
    late = [piece for two in zip(late, moved_over(late, 5)) for piece in two]

    inputs = (meta, projected, conv_weight, step_bias[None], log_rate[None], skip_gain, width)
    scanned_other, state_sent = scan(1, *inputs)
    state_other = swap(state_sent)
    scanned, state = scan(0, *inputs)
    scanned_other, scanned, state_other = lax.optimization_barrier(
        (scanned_other, scanned, state_other)
    )
    gain = norm_gain[None]
    sent, square_sent = gating(1, meta, both, scanned_other, gain, late)
    share, square_other = swap(out_share(places, sent, late)), swap(square_sent)
    mine, square = gating(0, meta, both, scanned, gain, late)
    mixed = mix(meta, places, mine, share, square, square_other, late)
    state = jnp.concatenate(
        [jnp.where(first_core, state, state_other), jnp.where(first_core, state_other, state)]
    )
    return (mixed[None], state.reshape(1, head_count, head_dim, width // 2))


def solution(mesh):
    placed = (
        P("req", None, None),
        P("req"),
        P(("req", "unit"), None),
        P(("req", "unit"), None),
        P(("req", "unit"), None),
        P(("req", "unit"), None),
        P(("req", "unit"), None),
        P(),
        P(),
        P(),
        P(),
        P(),
    )
    return jax.shard_map(
        body,
        mesh=mesh,
        in_specs=placed,
        out_specs=(P(("req", "unit"), None, None), P(("req", "unit"), None, None, None)),
        check_vma=False,
    )
```

```python
import functools

import jax
import jax.numpy as jnp
from jax import lax
from jax.experimental import pallas as pl
from jax.experimental.pallas import tpu as pltpu
from jax.sharding import PartitionSpec as P

SPAN = 128
LANES = 128
HEADS = 48
HEADS_STEP = 8
EPSILON = 1e-05
BF = jnp.bfloat16
F32 = jnp.float32


def length_of(shard_ref, heads):
    coded = shard_ref[:1].astype(F32)
    return 16.0 * coded[:, heads : heads + 1] + coded[:, heads + 1 : heads + 2]


def silu(v):
    h = 0.5 * v
    return h + h * jnp.tanh(h)


def causal_conv(values, taps):
    rows = lax.broadcasted_iota(jnp.int32, (BLOCK_ROWS, values.shape[1]), 0)
    count = taps.shape[0]
    total = values * taps[count - 1 : count]
    for back in range(1, count):
        moved = pltpu.roll(values, back, 0)
        moved = jnp.concatenate(
            [jnp.where(rows >= back, moved[:BLOCK_ROWS], 0.0), moved[BLOCK_ROWS:]], axis=0
        )
        total = total + moved * taps[count - 1 - back : count - back]
    return silu(total)


def scan_kernel(
    meta_ref,
    shard_ref,
    input_ref,
    side_ref,
    taps_ref,
    side_taps_ref,
    bias_ref,
    log_rate_ref,
    skip_ref,
    scanned_ref,
    state_ref,
    decay_col,
    delta_col,
    decay_row,
    b_scr,
    c_scr,
    cb_scr,
):
    step = pl.program_id(0)
    seq = input_ref.shape[0]
    state_dim = side_taps_ref.shape[1] // 2
    groups = decay_col.shape[0]
    blocks = seq // SPAN
    position = lax.broadcasted_iota(jnp.int32, (seq, LANES), 0)
    group_here = meta_ref[0] * pl.num_programs(0) + step

    @pl.when(step == 0)
    def _():
        side = side_ref[...].astype(F32)
        conv = causal_conv(side[:, : 2 * state_dim], side_taps_ref[...])
        b_short = conv[:, :state_dim].astype(BF)
        c_short = conv[:, state_dim:].astype(BF)
        b_scr[...] = b_short
        c_scr[...] = c_short
        for block in range(blocks):
            at = slice(block * SPAN, (block + 1) * SPAN)
            cb_scr[block] = lax.dot_general(
                c_short[at], b_short[at], (((1,), (1,)), ((), ())), preferred_element_type=F32
            )
        spare = jnp.zeros((1, LANES - bias_ref.shape[1]), F32)
        raw = side[:, 2 * state_dim :] + jnp.concatenate([bias_ref[...], spare], axis=1)
        live = (position.astype(F32) < length_of(shard_ref, bias_ref.shape[1])).astype(F32)
        delta = (jnp.maximum(raw, 0.0) + jnp.log1p(jnp.exp(-jnp.abs(raw)))) * live
        total = delta * -jnp.exp(jnp.concatenate([log_rate_ref[...], spare], axis=1))
        within = position % SPAN
        reach = 1
        while reach < SPAN:
            total = total + jnp.where(within >= reach, pltpu.roll(total, reach, 0), 0.0)
            reach *= 2
        turned = jnp.transpose(total)
        for group in range(groups):
            at = slice(group * HEADS_STEP, (group + 1) * HEADS_STEP)
            decay_col[group] = total[:, at]
            delta_col[group] = delta[:, at]
            decay_row[group] = turned[at]

    decays = decay_col[group_here]
    deltas = delta_col[group_here]
    rows_of = decay_row[group_here]
    lower = lax.broadcasted_iota(jnp.int32, (SPAN, SPAN), 0) >= lax.broadcasted_iota(
        jnp.int32, (SPAN, SPAN), 1
    )
    left = lax.broadcasted_iota(jnp.int32, (SPAN, LANES), 1) < LANES // 2
    top = lax.broadcasted_iota(jnp.int32, (LANES, state_dim), 0) < LANES // 2
    for pair in range(HEADS_STEP // 2):
        cols = slice(pair * LANES, (pair + 1) * LANES)
        one, two = 2 * pair, 2 * pair + 1
        x_conv = causal_conv(input_ref[:, cols].astype(F32), taps_ref[:, cols])
        head = group_here * HEADS_STEP + one
        skip = jnp.where(left[:1], skip_ref[head], skip_ref[head + 1])
        state = jnp.zeros((LANES, state_dim), F32)
        for block in range(blocks):
            at = slice(block * SPAN, (block + 1) * SPAN)
            x_here = x_conv[at]
            cb = cb_scr[block]
            d_one, d_two = decays[at, one : one + 1], decays[at, two : two + 1]
            mix_one = cb * jnp.exp(
                jnp.where(lower, d_one - rows_of[one : one + 1, at], -jnp.inf)
            )
            mix_two = cb * jnp.exp(
                jnp.where(lower, d_two - rows_of[two : two + 1, at], -jnp.inf)
            )
            decay = jnp.where(left, d_one, d_two)
            x_step = x_here * jnp.where(
                left, deltas[at, one : one + 1], deltas[at, two : two + 1]
            )
            short = x_step.astype(BF)
            zero = jnp.zeros_like(short)
            mixing = jnp.concatenate([mix_one.astype(BF), mix_two.astype(BF)], axis=1)
            spread = jnp.concatenate(
                [jnp.where(left, short, zero), jnp.where(left, zero, short)], axis=0
            )
            out = jnp.dot(mixing, spread, preferred_element_type=F32)
            if block:
                out = out + jnp.exp(decay) * lax.dot_general(
                    c_scr[at],
                    state.astype(BF),
                    (((1,), (1,)), ((), ())),
                    preferred_element_type=F32,
                )
            ending = decay[SPAN - 1 : SPAN]
            weighted = (x_step * jnp.exp(ending - decay)).astype(BF)
            fresh = lax.dot_general(
                weighted, b_scr[at], (((0,), (0,)), ((), ())), preferred_element_type=F32
            )
            if block:
                fade = jnp.where(
                    top,
                    jnp.exp(d_one[SPAN - 1 : SPAN]),
                    jnp.exp(d_two[SPAN - 1 : SPAN]),
                )
                fresh = fade * state + fresh
            state = fresh
            scanned_ref[at, cols] = out + skip * x_here
        state_ref[cols, :] = state


def scan(which, meta, shard, projected, conv_weight, bias, log_rate, skip, width):
    rows, total = projected.shape
    seq = rows // 2
    state_dim = width // 2
    half = total - width - LANES
    inner = 2 * half
    cols = HEADS_STEP * LANES // 2
    groups = half // cols
    taps, heads = conv_weight.shape[0], bias.shape[1]
    here = lambda g, m: (0, m[0] * groups + g)
    fixed = lambda g, m: (0, 0)
    grid_spec = pltpu.PrefetchScalarGridSpec(
        num_scalar_prefetch=1,
        grid=(groups,),
        in_specs=[
            pl.BlockSpec((shard.shape[0], LANES), lambda g, m: (0, total // LANES - 1)),
            pl.BlockSpec((seq, cols), lambda g, m: (which, g)),
            pl.BlockSpec((seq, width + LANES), lambda g, m: (which, half // (width + LANES))),
            pl.BlockSpec((taps, cols), here),
            pl.BlockSpec((taps, width), lambda g, m: (0, inner // width)),
            pl.BlockSpec((1, heads), fixed),
            pl.BlockSpec((1, heads), fixed),
            pl.BlockSpec(memory_space=pltpu.SMEM),
        ],
        out_specs=[
            pl.BlockSpec((seq, cols), lambda g, m: (0, g)),
            pl.BlockSpec((cols, state_dim), lambda g, m: (g, 0)),
        ],
        scratch_shapes=[
            pltpu.VMEM((2 * groups, seq, HEADS_STEP), F32),
            pltpu.VMEM((2 * groups, seq, HEADS_STEP), F32),
            pltpu.VMEM((2 * groups, HEADS_STEP, seq), F32),
            pltpu.VMEM((seq, state_dim), BF),
            pltpu.VMEM((seq, state_dim), BF),
            pltpu.VMEM((seq // SPAN, SPAN, SPAN), F32),
        ],
    )
    return pl.pallas_call(
        scan_kernel,
        grid_spec=grid_spec,
        out_shape=[
            jax.ShapeDtypeStruct((seq, half), F32),
            jax.ShapeDtypeStruct((half, state_dim), F32),
        ],
        compiler_params=pltpu.CompilerParams(
            dimension_semantics=("arbitrary",), vmem_limit_bytes=24 << 20
        ),
        cost_estimate=pl.CostEstimate(
            flops=inner * seq * 640, transcendentals=inner * seq * 3, bytes_accessed=5 << 20
        ),
        name="scan",
    )(meta, shard, projected, projected, conv_weight, conv_weight, bias, log_rate, skip)


def shards_kernel(
    meta_ref, lengths_ref, input_ref, state_ref, step_ref, gate_ref, out_ref, kept_ref, sent_ref
):
    rows, half = input_ref.shape[0], input_ref.shape[1] // 2
    width, heads = state_ref.shape[1], step_ref.shape[1]
    length = lengths_ref[meta_ref[1]]
    row = lax.broadcasted_iota(jnp.int32, (rows, LANES), 0)
    lane = lax.broadcasted_iota(jnp.int32, (rows, LANES), 1)
    coded = jnp.where(lane == heads, length >> 4, jnp.where(lane == heads + 1, length & 15, 0))
    coded = jnp.where(row == 0, coded, 0).astype(F32).astype(BF)
    for ref, core in ((kept_ref, meta_ref[0]), (sent_ref, 1 - meta_ref[0])):
        at = pl.ds(pl.multiple_of(core * half, half), half)
        ref[:, :half] = input_ref[:, at].astype(BF)
        ref[:, half : half + width] = state_ref[...].astype(BF)
        ref[:, half + width : half + width + LANES] = coded
        ref[:, half + width : half + width + heads] = step_ref[...].astype(BF)
        start = half + width + LANES
        ref[:, start : start + half] = gate_ref[:, at].astype(BF)
        ref[:, start + half :] = out_ref[:, at].astype(BF)


def shards(meta, lengths, inputs, state, step, gate, out):
    rows, inner = inputs.shape
    total = 3 * (inner // 2) + state.shape[1] + LANES
    scalars = pl.BlockSpec(memory_space=pltpu.SMEM)
    whole = pl.BlockSpec(memory_space=pltpu.VMEM)
    return pl.pallas_call(
        shards_kernel,
        in_specs=[scalars] * 2 + [whole] * 5,
        out_specs=[whole] * 2,
        out_shape=[jax.ShapeDtypeStruct((rows, total), BF)] * 2,
        name="shards",
    )(meta, lengths, inputs, state, step, gate, out)


def project_kernel(tokens_ref, *refs):
    weight = jnp.concatenate([piece[...] for piece in refs[:-1]], axis=0)
    refs[-1][...] = jnp.dot(tokens_ref[...], weight, preferred_element_type=F32).astype(BF)


def project(tokens, pieces):
    rows, model = tokens.shape
    depth, total = pieces[0].shape
    steps = 3
    tile = total // steps
    return pl.pallas_call(
        project_kernel,
        grid=(steps,),
        in_specs=[pl.BlockSpec((rows, model), lambda n: (0, 0))]
        + [pl.BlockSpec((depth, tile), lambda n: (0, n)) for _ in pieces],
        out_specs=pl.BlockSpec((rows, tile), lambda n: (0, n)),
        out_shape=jax.ShapeDtypeStruct((rows, total), BF),
        compiler_params=pltpu.CompilerParams(
            dimension_semantics=("arbitrary",), vmem_limit_bytes=24 << 20
        ),
        cost_estimate=pl.CostEstimate(
            flops=2 * rows * model * total, transcendentals=0, bytes_accessed=10 << 20
        ),
        name="project",
    )(tokens, *pieces)


def share_kernel(which, meta_ref, places_ref, tokens_ref, scanned_ref, gain_ref, *refs):
    pieces, (share_ref, square_ref, gated_scr) = refs[:-3], refs[-3:]
    seq, half = scanned_ref.shape
    rows = slice(which * seq, (which + 1) * seq)
    tile = half // 3
    square_ref[...] = jnp.zeros_like(square_ref)
    for at in range(0, half, tile):
        cols = slice(at, at + tile)
        weight = jnp.concatenate([piece[:, cols] for piece in pieces], axis=0)
        gate = jnp.dot(tokens_ref[rows], weight, preferred_element_type=F32).astype(BF)
        gated = scanned_ref[:, cols] * silu(gate.astype(F32))
        gain_at = pl.multiple_of(meta_ref[0] * half + at, LANES)
        gated_scr[:, cols] = (gated * gain_ref[:, pl.ds(gain_at, tile)]).astype(BF)
        square = gated * gated
        for lane in range(0, tile, LANES):
            square_ref[...] += square[:, lane : lane + LANES]
    steps = 4
    depth = pieces[0].shape[0] // steps
    each = depth // BLOCK_ROWS
    for step in range(steps):
        weight = jnp.concatenate(
            [piece[step * depth : (step + 1) * depth, half:] for piece in pieces], axis=0
        )
        total = lax.dot_general(
            weight, gated_scr[...], (((1,), (1,)), ((), ())), preferred_element_type=F32
        )
        for index in range(len(pieces)):
            for block in range(each):
                at = (index * each + block) * BLOCK_ROWS
                place = places_ref[(index * steps + step) * each + block]
                share_ref[pl.ds(pl.multiple_of(place, BLOCK_ROWS), BLOCK_ROWS), :] = total[
                    at : at + BLOCK_ROWS
                ]


def out_share(which, meta, places, tokens, scanned, gain, pieces):
    seq, half = scanned.shape
    model = tokens.shape[1]
    scalars = pl.BlockSpec(memory_space=pltpu.SMEM)
    whole = pl.BlockSpec(memory_space=pltpu.VMEM)
    return pl.pallas_call(
        functools.partial(share_kernel, which),
        in_specs=[scalars] * 2 + [whole] * (3 + len(pieces)),
        out_specs=[whole] * 2,
        out_shape=[
            jax.ShapeDtypeStruct((model, seq), F32),
            jax.ShapeDtypeStruct((seq, LANES), F32),
        ],
        scratch_shapes=[pltpu.VMEM((seq, half), BF)],
        compiler_params=pltpu.CompilerParams(vmem_limit_bytes=16 << 20),
        cost_estimate=pl.CostEstimate(
            flops=4 * seq * half * model, transcendentals=seq * half, bytes_accessed=16 << 20
        ),
        name="out_share",
    )(meta, places, tokens, scanned, gain, *pieces)


def mix_kernel(shard_ref, mine_ref, other_ref, sq_mine, sq_other, pick_ref, out_ref):
    seq, model = out_ref.shape
    inner = 2 * model
    squares = jnp.transpose(sq_mine[...] + sq_other[...])
    mean = jnp.sum(squares, axis=0, keepdims=True) / inner
    live = lax.broadcasted_iota(jnp.int32, (1, seq), 1).astype(F32) < length_of(shard_ref, HEADS)
    scale = jnp.where(live, lax.rsqrt(mean + EPSILON), 0.0)
    tile = pick_ref.shape[0]
    for at in range(0, model, tile):
        rows = slice(at, at + tile)
        short = ((mine_ref[rows] + other_ref[rows]) * scale).astype(BF)
        out_ref[:, rows] = lax.dot_general(
            short, pick_ref[...], (((0,), (0,)), ((), ())), preferred_element_type=F32
        ).astype(BF)


def mix(shard, cut, mine, other, sq_mine, sq_other):
    model, seq = mine.shape
    tile = model // 4
    column = jnp.arange(tile, dtype=jnp.int32)
    chip, rest = column // (2 * SHARD_ROWS), column % (2 * SHARD_ROWS)
    target = rest // SHARD_ROWS * (tile // 2) + chip * SHARD_ROWS + rest % SHARD_ROWS
    pick = (target[:, None] == column[None]).astype(BF)
    whole = pl.BlockSpec(memory_space=pltpu.VMEM)
    fixed = lambda i: (0, 0)
    return pl.pallas_call(
        mix_kernel,
        grid=(1,),
        in_specs=[pl.BlockSpec((shard.shape[0], LANES), lambda i: (0, cut // LANES - 1))]
        + [whole] * 5,
        out_specs=whole,
        out_shape=jax.ShapeDtypeStruct((seq, model), BF),
        compiler_params=pltpu.CompilerParams(vmem_limit_bytes=16 << 20),
        cost_estimate=pl.CostEstimate(
            flops=2 * seq * tile * model, transcendentals=0, bytes_accessed=8 << 20
        ),
        name="mix",
    )(shard, mine, other, sq_mine, sq_other, pick)


EVERYONE = ("req", "unit")
DEVICES = 128
CORE = 16
SHARD_ROWS = 12
COLOURS = 3
BLOCK_ROWS = 8
LINKS = (1 << 2, 1, 1 << 5, 3 << 2, 3, 3 << 5)


def link_of(colour, core, step):
    return LINKS[(colour + 3 * core - step) % 6]


def hop(value, mask_of):
    return lax.ppermute(
        value, EVERYONE, [(d, d ^ mask_of((d // CORE) % 2)) for d in range(DEVICES)]
    )


def swap(value):
    return hop(value, lambda core: CORE)


def moved_over(held, step):
    return [hop(piece, lambda core, c=c: link_of(c, core, step)) for c, piece in enumerate(held)]


def joined(held, moved):
    return [
        lax.optimization_barrier(jnp.concatenate([h, m], axis=0)) for h, m in zip(held, moved)
    ]


def gathered_chip(me, core, colour, block):
    mask = jnp.zeros_like(block)
    for step in range(6):
        link = jnp.zeros_like(block)
        for c in range(COLOURS):
            here = jnp.where(core == 0, link_of(c, 0, step), link_of(c, 1, step))
            link = jnp.where(colour == c, here, link)
        mask = mask ^ (((block >> step) & 1) * link)
    return (me ^ mask) & ~CORE


def row_sources(me, core, model):
    row = jnp.arange(model, dtype=jnp.int32)
    colour, block = row // (model // COLOURS), row // BLOCK_ROWS % 64
    local = colour * BLOCK_ROWS + row % BLOCK_ROWS
    upper = (local >= SHARD_ROWS).astype(jnp.int32)
    device = gathered_chip(me, core, colour, block) + CORE * upper
    return device * SHARD_ROWS + local - SHARD_ROWS * upper


def row_places(me, core):
    index = jnp.arange(COLOURS * 64, dtype=jnp.int32)
    chip = gathered_chip(me, core, index // 64, index % 64)
    chip = (chip >> 5) * CORE + (chip & (CORE - 1))
    return chip * 2 * SHARD_ROWS + index // 64 * BLOCK_ROWS


def body(
    tokens,
    lengths,
    gate_proj,
    input_proj,
    state_proj,
    step_proj,
    out_proj,
    conv_weight,
    step_bias,
    log_rate,
    skip_gain,
    norm_gain,
):
    unit_id = lax.axis_index("unit")
    me = lax.axis_index(EVERYONE).astype(jnp.int32)
    core = (me // CORE) % 2
    first_core = core == 0
    seq_len, model_dim = tokens.shape[1:]
    inner_dim = gate_proj.shape[1]
    head_count = log_rate.shape[0]
    head_dim = inner_dim // head_count
    width = state_proj.shape[1]
    half = inner_dim // 2

    cut = half + width + LANES
    meta = jnp.stack([core, unit_id])
    kept, sent = shards(
        meta, lengths, input_proj, state_proj, step_proj, gate_proj, out_proj
    )
    received = swap(sent)
    pair = jnp.concatenate(
        [jnp.where(first_core, kept, received), jnp.where(first_core, received, kept)], axis=0
    )
    held = [pair[8 * c : 8 * c + 8] for c in range(COLOURS)]
    for step in range(4):
        held = joined(held, moved_over(held, step))
    held[2], unit_id = lax.optimization_barrier((held[2], unit_id))
    moved = moved_over(held, 4)

    own = lax.dynamic_index_in_dim(tokens, unit_id, 0, keepdims=False)
    both = jnp.concatenate([own, swap(own)], axis=0)
    pick = jnp.arange(model_dim, dtype=jnp.int32)[:, None] == row_sources(me, core, model_dim)[None]
    both = jnp.dot(both, pick.astype(BF), preferred_element_type=F32).astype(BF)
    moved[0], both, places = lax.optimization_barrier((moved[0], both, row_places(me, core)))
    early = joined([h[:, :cut] for h in held], [m[:, :cut] for m in moved])
    late = joined([h[:, cut:] for h in held], [m[:, cut:] for m in moved])
    moved = moved_over(early, 5)
    for c in range(COLOURS):
        moved[c], late[c] = lax.optimization_barrier((moved[c], late[c]))
    early = [piece for two in zip(early, moved) for piece in two]
    late = [piece for two in zip(late, moved_over(late, 5)) for piece in two]

    projected = project(both, early)
    inputs = (projected, conv_weight, step_bias[None], log_rate[None], skip_gain, width)
    scanned_other, state_sent = scan(1, meta, received, *inputs)
    state_other = swap(state_sent)
    scanned, state = scan(0, meta, kept, *inputs)
    scanned_other, scanned, state_other = lax.optimization_barrier(
        (scanned_other, scanned, state_other)
    )
    shared = (meta, places, both)
    sent, square_sent = out_share(1, *shared, scanned_other, norm_gain[None], late)
    other, square_other = swap(sent), swap(square_sent)
    mine, square = out_share(0, *shared, scanned, norm_gain[None], late)
    mixed = mix(kept, cut, mine, other, square, square_other)
    state = jnp.concatenate(
        [jnp.where(first_core, state, state_other), jnp.where(first_core, state_other, state)]
    )
    return (mixed[None], state.reshape(1, head_count, head_dim, width // 2))


def solution(mesh):
    placed = (
        P("req", None, None),
        P("req"),
        P(("req", "unit"), None),
        P(("req", "unit"), None),
        P(("req", "unit"), None),
        P(("req", "unit"), None),
        P(("req", "unit"), None),
        P(),
        P(),
        P(),
        P(),
        P(),
    )
    return jax.shard_map(
        body,
        mesh=mesh,
        in_specs=placed,
        out_specs=(P(("req", "unit"), None, None), P(("req", "unit"), None, None, None)),
        check_vma=False,
    )
```

```python
import functools

import jax
import jax.numpy as jnp
from jax import lax
from jax.experimental import pallas as pl
from jax.experimental.pallas import tpu as pltpu
from jax.sharding import PartitionSpec as P

SPAN = 128
LANES = 128
HEADS = 48
HEADS_STEP = 8
EPSILON = 1e-05
BF = jnp.bfloat16
F32 = jnp.float32


def length_of(shard_ref, heads):
    coded = shard_ref[:1].astype(F32)
    return 16.0 * coded[:, heads : heads + 1] + coded[:, heads + 1 : heads + 2]


def silu(v):
    h = 0.5 * v
    return h + h * jnp.tanh(h)


def causal_conv(values, taps):
    rows = lax.broadcasted_iota(jnp.int32, (BLOCK_ROWS, values.shape[1]), 0)
    count = taps.shape[0]
    total = values * taps[count - 1 : count]
    for back in range(1, count):
        moved = pltpu.roll(values, back, 0)
        moved = jnp.concatenate(
            [jnp.where(rows >= back, moved[:BLOCK_ROWS], 0.0), moved[BLOCK_ROWS:]], axis=0
        )
        total = total + moved * taps[count - 1 - back : count - back]
    return silu(total)


def scan_kernel(
    meta_ref,
    shard_ref,
    input_ref,
    side_ref,
    taps_ref,
    side_taps_ref,
    bias_ref,
    log_rate_ref,
    skip_ref,
    scanned_ref,
    state_ref,
    decay_col,
    delta_col,
    decay_row,
    b_scr,
    c_scr,
    cb_scr,
):
    step = pl.program_id(0)
    seq = input_ref.shape[0]
    state_dim = side_taps_ref.shape[1] // 2
    groups = decay_col.shape[0]
    blocks = seq // SPAN
    position = lax.broadcasted_iota(jnp.int32, (seq, LANES), 0)
    group_here = meta_ref[0] * pl.num_programs(0) + step

    @pl.when(step == 0)
    def _():
        side = side_ref[...].astype(F32)
        conv = causal_conv(side[:, : 2 * state_dim], side_taps_ref[...])
        b_short = conv[:, :state_dim].astype(BF)
        c_short = conv[:, state_dim:].astype(BF)
        b_scr[...] = b_short
        c_scr[...] = c_short
        for block in range(blocks):
            at = slice(block * SPAN, (block + 1) * SPAN)
            cb_scr[block] = lax.dot_general(
                c_short[at], b_short[at], (((1,), (1,)), ((), ())), preferred_element_type=F32
            )
        spare = jnp.zeros((1, LANES - bias_ref.shape[1]), F32)
        raw = side[:, 2 * state_dim :] + jnp.concatenate([bias_ref[...], spare], axis=1)
        live = (position.astype(F32) < length_of(shard_ref, bias_ref.shape[1])).astype(F32)
        delta = (jnp.maximum(raw, 0.0) + jnp.log1p(jnp.exp(-jnp.abs(raw)))) * live
        total = delta * -jnp.exp(jnp.concatenate([log_rate_ref[...], spare], axis=1))
        within = position % SPAN
        reach = 1
        while reach < SPAN:
            total = total + jnp.where(within >= reach, pltpu.roll(total, reach, 0), 0.0)
            reach *= 2
        turned = jnp.transpose(total)
        for group in range(groups):
            at = slice(group * HEADS_STEP, (group + 1) * HEADS_STEP)
            decay_col[group] = total[:, at]
            delta_col[group] = delta[:, at]
            decay_row[group] = turned[at]

    decays = decay_col[group_here]
    deltas = delta_col[group_here]
    rows_of = decay_row[group_here]
    lower = lax.broadcasted_iota(jnp.int32, (SPAN, SPAN), 0) >= lax.broadcasted_iota(
        jnp.int32, (SPAN, SPAN), 1
    )
    left = lax.broadcasted_iota(jnp.int32, (SPAN, LANES), 1) < LANES // 2
    top = lax.broadcasted_iota(jnp.int32, (LANES, state_dim), 0) < LANES // 2
    for pair in range(HEADS_STEP // 2):
        cols = slice(pair * LANES, (pair + 1) * LANES)
        one, two = 2 * pair, 2 * pair + 1
        x_conv = causal_conv(input_ref[:, cols].astype(F32), taps_ref[:, cols])
        head = group_here * HEADS_STEP + one
        skip = jnp.where(left[:1], skip_ref[head], skip_ref[head + 1])
        state = jnp.zeros((LANES, state_dim), F32)
        for block in range(blocks):
            at = slice(block * SPAN, (block + 1) * SPAN)
            x_here = x_conv[at]
            cb = cb_scr[block]
            d_one, d_two = decays[at, one : one + 1], decays[at, two : two + 1]
            mix_one = cb * jnp.exp(
                jnp.where(lower, d_one - rows_of[one : one + 1, at], -jnp.inf)
            )
            mix_two = cb * jnp.exp(
                jnp.where(lower, d_two - rows_of[two : two + 1, at], -jnp.inf)
            )
            decay = jnp.where(left, d_one, d_two)
            x_step = x_here * jnp.where(
                left, deltas[at, one : one + 1], deltas[at, two : two + 1]
            )
            short = x_step.astype(BF)
            zero = jnp.zeros_like(short)
            mixing = jnp.concatenate([mix_one.astype(BF), mix_two.astype(BF)], axis=1)
            spread = jnp.concatenate(
                [jnp.where(left, short, zero), jnp.where(left, zero, short)], axis=0
            )
            out = jnp.dot(mixing, spread, preferred_element_type=F32)
            if block:
                out = out + jnp.exp(decay) * lax.dot_general(
                    c_scr[at],
                    state.astype(BF),
                    (((1,), (1,)), ((), ())),
                    preferred_element_type=F32,
                )
            ending = decay[SPAN - 1 : SPAN]
            weighted = (x_step * jnp.exp(ending - decay)).astype(BF)
            fresh = lax.dot_general(
                weighted, b_scr[at], (((0,), (0,)), ((), ())), preferred_element_type=F32
            )
            if block:
                fade = jnp.where(
                    top,
                    jnp.exp(d_one[SPAN - 1 : SPAN]),
                    jnp.exp(d_two[SPAN - 1 : SPAN]),
                )
                fresh = fade * state + fresh
            state = fresh
            scanned_ref[at, cols] = out + skip * x_here
        state_ref[cols, :] = state


def scan(which, meta, shard, projected, conv_weight, bias, log_rate, skip, width):
    rows, total = projected.shape
    seq = rows // 2
    state_dim = width // 2
    half = total - width - LANES
    inner = 2 * half
    cols = HEADS_STEP * LANES // 2
    groups = half // cols
    taps, heads = conv_weight.shape[0], bias.shape[1]
    here = lambda g, m: (0, m[0] * groups + g)
    fixed = lambda g, m: (0, 0)
    grid_spec = pltpu.PrefetchScalarGridSpec(
        num_scalar_prefetch=1,
        grid=(groups,),
        in_specs=[
            pl.BlockSpec((shard.shape[0], LANES), lambda g, m: (0, total // LANES - 1)),
            pl.BlockSpec((seq, cols), lambda g, m: (which, g)),
            pl.BlockSpec((seq, width + LANES), lambda g, m: (which, half // (width + LANES))),
            pl.BlockSpec((taps, cols), here),
            pl.BlockSpec((taps, width), lambda g, m: (0, inner // width)),
            pl.BlockSpec((1, heads), fixed),
            pl.BlockSpec((1, heads), fixed),
            pl.BlockSpec(memory_space=pltpu.SMEM),
        ],
        out_specs=[
            pl.BlockSpec((seq, cols), lambda g, m: (0, g)),
            pl.BlockSpec((cols, state_dim), lambda g, m: (g, 0)),
        ],
        scratch_shapes=[
            pltpu.VMEM((2 * groups, seq, HEADS_STEP), F32),
            pltpu.VMEM((2 * groups, seq, HEADS_STEP), F32),
            pltpu.VMEM((2 * groups, HEADS_STEP, seq), F32),
            pltpu.VMEM((seq, state_dim), BF),
            pltpu.VMEM((seq, state_dim), BF),
            pltpu.VMEM((seq // SPAN, SPAN, SPAN), F32),
        ],
    )
    return pl.pallas_call(
        scan_kernel,
        grid_spec=grid_spec,
        out_shape=[
            jax.ShapeDtypeStruct((seq, half), F32),
            jax.ShapeDtypeStruct((half, state_dim), F32),
        ],
        compiler_params=pltpu.CompilerParams(
            dimension_semantics=("arbitrary",), vmem_limit_bytes=24 << 20
        ),
        cost_estimate=pl.CostEstimate(
            flops=inner * seq * 640, transcendentals=inner * seq * 3, bytes_accessed=5 << 20
        ),
        name="scan",
    )(meta, shard, projected, projected, conv_weight, conv_weight, bias, log_rate, skip)


def shards_kernel(
    meta_ref, lengths_ref, input_ref, state_ref, step_ref, gate_ref, out_ref, kept_ref, sent_ref
):
    rows, half = input_ref.shape[0], input_ref.shape[1] // 2
    width, heads = state_ref.shape[1], step_ref.shape[1]
    length = lengths_ref[meta_ref[1]]
    row = lax.broadcasted_iota(jnp.int32, (rows, LANES), 0)
    lane = lax.broadcasted_iota(jnp.int32, (rows, LANES), 1)
    coded = jnp.where(lane == heads, length >> 4, jnp.where(lane == heads + 1, length & 15, 0))
    coded = jnp.where(row == 0, coded, 0).astype(F32).astype(BF)
    for ref, core in ((kept_ref, meta_ref[0]), (sent_ref, 1 - meta_ref[0])):
        at = pl.ds(pl.multiple_of(core * half, half), half)
        ref[:, :half] = input_ref[:, at].astype(BF)
        ref[:, half : half + width] = state_ref[...].astype(BF)
        ref[:, half + width : half + width + LANES] = coded
        ref[:, half + width : half + width + heads] = step_ref[...].astype(BF)
        start = half + width + LANES
        ref[:, start : start + half] = gate_ref[:, at].astype(BF)
        ref[:, start + half :] = out_ref[:, at].astype(BF)


def shards(meta, lengths, inputs, state, step, gate, out):
    rows, inner = inputs.shape
    total = 3 * (inner // 2) + state.shape[1] + LANES
    scalars = pl.BlockSpec(memory_space=pltpu.SMEM)
    whole = pl.BlockSpec(memory_space=pltpu.VMEM)
    return pl.pallas_call(
        shards_kernel,
        in_specs=[scalars] * 2 + [whole] * 5,
        out_specs=[whole] * 2,
        out_shape=[jax.ShapeDtypeStruct((rows, total), BF)] * 2,
        compiler_params=pltpu.CompilerParams(vmem_limit_bytes=6 << 20),
        name="shards",
    )(meta, lengths, inputs, state, step, gate, out)


def join_kernel(held_ref, moved_ref, *outs):
    rows, start = held_ref.shape[0], 0
    for out_ref in outs:
        cols = slice(start, start + out_ref.shape[1])
        out_ref[:rows] = held_ref[:, cols]
        out_ref[rows:] = moved_ref[:, cols]
        start += out_ref.shape[1]


def join(held, moved, *widths):
    rows, total = held.shape
    whole = pl.BlockSpec(memory_space=pltpu.VMEM)
    return pl.pallas_call(
        join_kernel,
        in_specs=[whole] * 2,
        out_specs=[whole] * len(widths),
        out_shape=[jax.ShapeDtypeStruct((2 * rows, width), BF) for width in widths],
        compiler_params=pltpu.CompilerParams(vmem_limit_bytes=6 << 20),
        cost_estimate=pl.CostEstimate(
            flops=0, transcendentals=0, bytes_accessed=8 * rows * total
        ),
        name="join",
    )(held, moved)


def project_kernel(first, tokens_ref, *refs):
    begin_ref, pieces, out_ref = refs[0], refs[:-1], refs[-1]
    if not first:
        pieces = pieces[1:]
    depth, total = pieces[0].shape
    tokens = jnp.concatenate(
        [
            tokens_ref[:, at : at + depth]
            for at in range(0 if first else depth, tokens_ref.shape[1], 2 * depth)
        ],
        axis=1,
    )
    tile = total // 5
    for at in range(0, total, tile):
        cols = slice(at, at + tile)
        weight = jnp.concatenate([piece[:, cols] for piece in pieces], axis=0)
        part = jnp.dot(tokens, weight, preferred_element_type=F32)
        if not first:
            part = part + begin_ref[:, cols]
        out_ref[:, cols] = part.astype(out_ref.dtype)


def project(tokens, pieces, begun=None):
    rows, model = tokens.shape
    depth, total = pieces[0].shape
    first = begun is None
    whole = pl.BlockSpec(memory_space=pltpu.VMEM)
    begun = () if first else (begun,)
    return pl.pallas_call(
        functools.partial(project_kernel, first),
        in_specs=[whole] * (1 + len(begun) + len(pieces)),
        out_specs=whole,
        out_shape=jax.ShapeDtypeStruct((rows, total), F32 if first else BF),
        compiler_params=pltpu.CompilerParams(vmem_limit_bytes=16 << 20),
        cost_estimate=pl.CostEstimate(
            flops=rows * model * total, transcendentals=0, bytes_accessed=10 << 20
        ),
        name="project",
    )(tokens, *begun, *pieces)


def share_kernel(which, meta_ref, places_ref, tokens_ref, scanned_ref, gain_ref, *refs):
    pieces, (share_ref, square_ref, gated_scr) = refs[:-3], refs[-3:]
    seq, half = scanned_ref.shape
    rows = slice(which * seq, (which + 1) * seq)
    tile = half // 3
    square_ref[...] = jnp.zeros_like(square_ref)
    for at in range(0, half, tile):
        cols = slice(at, at + tile)
        weight = jnp.concatenate([piece[:, cols] for piece in pieces], axis=0)
        gate = jnp.dot(tokens_ref[rows], weight, preferred_element_type=F32).astype(BF)
        gated = scanned_ref[:, cols] * silu(gate.astype(F32))
        gain_at = pl.multiple_of(meta_ref[0] * half + at, LANES)
        gated_scr[:, cols] = (gated * gain_ref[:, pl.ds(gain_at, tile)]).astype(BF)
        square = gated * gated
        for lane in range(0, tile, LANES):
            square_ref[...] += square[:, lane : lane + LANES]
    steps = 4
    depth = pieces[0].shape[0] // steps
    each = depth // BLOCK_ROWS
    for step in range(steps):
        weight = jnp.concatenate(
            [piece[step * depth : (step + 1) * depth, half:] for piece in pieces], axis=0
        )
        total = lax.dot_general(
            weight, gated_scr[...], (((1,), (1,)), ((), ())), preferred_element_type=F32
        )
        for index in range(len(pieces)):
            for block in range(each):
                at = (index * each + block) * BLOCK_ROWS
                place = places_ref[(index * steps + step) * each + block]
                share_ref[pl.ds(pl.multiple_of(place, BLOCK_ROWS), BLOCK_ROWS), :] = total[
                    at : at + BLOCK_ROWS
                ]


def out_share(which, meta, places, tokens, scanned, gain, pieces):
    seq, half = scanned.shape
    model = tokens.shape[1]
    scalars = pl.BlockSpec(memory_space=pltpu.SMEM)
    whole = pl.BlockSpec(memory_space=pltpu.VMEM)
    return pl.pallas_call(
        functools.partial(share_kernel, which),
        in_specs=[scalars] * 2 + [whole] * (3 + len(pieces)),
        out_specs=[whole] * 2,
        out_shape=[
            jax.ShapeDtypeStruct((model, seq), F32),
            jax.ShapeDtypeStruct((seq, LANES), F32),
        ],
        scratch_shapes=[pltpu.VMEM((seq, half), BF)],
        compiler_params=pltpu.CompilerParams(vmem_limit_bytes=16 << 20),
        cost_estimate=pl.CostEstimate(
            flops=4 * seq * half * model, transcendentals=seq * half, bytes_accessed=16 << 20
        ),
        name="out_share",
    )(meta, places, tokens, scanned, gain, *pieces)


def mix_kernel(shard_ref, mine_ref, other_ref, sq_mine, sq_other, pick_ref, out_ref):
    seq, model = out_ref.shape
    inner = 2 * model
    squares = jnp.transpose(sq_mine[...] + sq_other[...])
    mean = jnp.sum(squares, axis=0, keepdims=True) / inner
    live = lax.broadcasted_iota(jnp.int32, (1, seq), 1).astype(F32) < length_of(shard_ref, HEADS)
    scale = jnp.where(live, lax.rsqrt(mean + EPSILON), 0.0)
    tile = pick_ref.shape[0]
    for at in range(0, model, tile):
        rows = slice(at, at + tile)
        short = ((mine_ref[rows] + other_ref[rows]) * scale).astype(BF)
        out_ref[:, rows] = lax.dot_general(
            short, pick_ref[...], (((0,), (0,)), ((), ())), preferred_element_type=F32
        ).astype(BF)


def mix(shard, cut, mine, other, sq_mine, sq_other):
    model, seq = mine.shape
    tile = model // 4
    column = jnp.arange(tile, dtype=jnp.int32)
    chip, rest = column // (2 * SHARD_ROWS), column % (2 * SHARD_ROWS)
    target = rest // SHARD_ROWS * (tile // 2) + chip * SHARD_ROWS + rest % SHARD_ROWS
    pick = (target[:, None] == column[None]).astype(BF)
    whole = pl.BlockSpec(memory_space=pltpu.VMEM)
    fixed = lambda i: (0, 0)
    return pl.pallas_call(
        mix_kernel,
        grid=(1,),
        in_specs=[pl.BlockSpec((shard.shape[0], LANES), lambda i: (0, cut // LANES - 1))]
        + [whole] * 5,
        out_specs=whole,
        out_shape=jax.ShapeDtypeStruct((seq, model), BF),
        compiler_params=pltpu.CompilerParams(vmem_limit_bytes=16 << 20),
        cost_estimate=pl.CostEstimate(
            flops=2 * seq * tile * model, transcendentals=0, bytes_accessed=8 << 20
        ),
        name="mix",
    )(shard, mine, other, sq_mine, sq_other, pick)


EVERYONE = ("req", "unit")
DEVICES = 128
CORE = 16
SHARD_ROWS = 12
COLOURS = 3
BLOCK_ROWS = 8
LINKS = (1 << 2, 1, 1 << 5, 3 << 2, 3, 3 << 5)


def link_of(colour, core, step):
    return LINKS[(colour + 3 * core - step) % 6]


def hop(value, mask_of):
    return lax.ppermute(
        value, EVERYONE, [(d, d ^ mask_of((d // CORE) % 2)) for d in range(DEVICES)]
    )


def swap(value):
    return hop(value, lambda core: CORE)


def moved_over(held, step):
    return [hop(piece, lambda core, c=c: link_of(c, core, step)) for c, piece in enumerate(held)]


def joined(held, moved):
    return [
        lax.optimization_barrier(jnp.concatenate([h, m], axis=0)) for h, m in zip(held, moved)
    ]


def gathered_chip(me, core, colour, block):
    mask = jnp.zeros_like(block)
    for step in range(6):
        link = jnp.zeros_like(block)
        for c in range(COLOURS):
            here = jnp.where(core == 0, link_of(c, 0, step), link_of(c, 1, step))
            link = jnp.where(colour == c, here, link)
        mask = mask ^ (((block >> step) & 1) * link)
    return (me ^ mask) & ~CORE


def row_sources(me, core, model):
    row = jnp.arange(model, dtype=jnp.int32)
    colour, block = row // (model // COLOURS), row // BLOCK_ROWS % 64
    local = colour * BLOCK_ROWS + row % BLOCK_ROWS
    upper = (local >= SHARD_ROWS).astype(jnp.int32)
    device = gathered_chip(me, core, colour, block) + CORE * upper
    return device * SHARD_ROWS + local - SHARD_ROWS * upper


def row_places(me, core):
    index = jnp.arange(COLOURS * 64, dtype=jnp.int32)
    chip = gathered_chip(me, core, index // 64, index % 64)
    chip = (chip >> 5) * CORE + (chip & (CORE - 1))
    return chip * 2 * SHARD_ROWS + index // 64 * BLOCK_ROWS


def body(
    tokens,
    lengths,
    gate_proj,
    input_proj,
    state_proj,
    step_proj,
    out_proj,
    conv_weight,
    step_bias,
    log_rate,
    skip_gain,
    norm_gain,
):
    unit_id = lax.axis_index("unit")
    me = lax.axis_index(EVERYONE).astype(jnp.int32)
    core = (me // CORE) % 2
    first_core = core == 0
    seq_len, model_dim = tokens.shape[1:]
    inner_dim = gate_proj.shape[1]
    head_count = log_rate.shape[0]
    head_dim = inner_dim // head_count
    width = state_proj.shape[1]
    half = inner_dim // 2

    cut = half + width + LANES
    meta = jnp.stack([core, unit_id])
    kept, sent = shards(
        meta, lengths, input_proj, state_proj, step_proj, gate_proj, out_proj
    )
    sent, unit_id = lax.optimization_barrier((sent, unit_id))
    received = swap(sent)
    pair = jnp.concatenate(
        [jnp.where(first_core, kept, received), jnp.where(first_core, received, kept)], axis=0
    )
    held = [pair[8 * c : 8 * c + 8] for c in range(COLOURS)]
    for step in range(3):
        held = joined(held, moved_over(held, step))
    held = [join(h, m, cut + 2 * half)[0] for h, m in zip(held, moved_over(held, 3))]
    moved = moved_over(held, 4)

    own = lax.dynamic_index_in_dim(tokens, unit_id, 0, keepdims=False)
    both = jnp.concatenate([own, swap(own)], axis=0)
    pick = jnp.arange(model_dim, dtype=jnp.int32)[:, None] == row_sources(me, core, model_dim)[None]
    both = jnp.dot(both, pick.astype(BF), preferred_element_type=F32).astype(BF)
    moved[0], both, places = lax.optimization_barrier((moved[0], both, row_places(me, core)))
    early, late = zip(*[join(h, m, cut, 2 * half) for h, m in zip(held, moved)])
    late = list(late)
    moved = moved_over(early, 5)
    begun = project(both, early)
    moved[0], begun = lax.optimization_barrier((moved[0], begun))
    for c in range(COLOURS):
        moved[c], late[c] = lax.optimization_barrier((moved[c], late[c]))
    late = [piece for two in zip(late, moved_over(late, 5)) for piece in two]

    projected = project(both, moved, begun)
    inputs = (projected, conv_weight, step_bias[None], log_rate[None], skip_gain, width)
    scanned_other, state_sent = scan(1, meta, received, *inputs)
    state_other = swap(state_sent)
    scanned, state = scan(0, meta, kept, *inputs)
    scanned_other, scanned, state_other = lax.optimization_barrier(
        (scanned_other, scanned, state_other)
    )
    shared = (meta, places, both)
    sent, square_sent = out_share(1, *shared, scanned_other, norm_gain[None], late)
    other, square_other = swap(sent), swap(square_sent)
    mine, square = out_share(0, *shared, scanned, norm_gain[None], late)
    mixed = mix(kept, cut, mine, other, square, square_other)
    state = jnp.concatenate(
        [jnp.where(first_core, state, state_other), jnp.where(first_core, state_other, state)]
    )
    return (mixed[None], state.reshape(1, head_count, head_dim, width // 2))


def solution(mesh):
    placed = (
        P("req", None, None),
        P("req"),
        P(("req", "unit"), None),
        P(("req", "unit"), None),
        P(("req", "unit"), None),
        P(("req", "unit"), None),
        P(("req", "unit"), None),
        P(),
        P(),
        P(),
        P(),
        P(),
    )
    return jax.shard_map(
        body,
        mesh=mesh,
        in_specs=placed,
        out_specs=(P(("req", "unit"), None, None), P(("req", "unit"), None, None, None)),
        check_vma=False,
    )
```

```python
import functools

import jax
import jax.numpy as jnp
from jax import lax
from jax.experimental import pallas as pl
from jax.experimental.pallas import tpu as pltpu
from jax.sharding import PartitionSpec as P

SPAN = 128
LANES = 128
HEADS = 48
HEADS_STEP = 8
EPSILON = 1e-05
LOG2E = 1.4426950408889634
BF = jnp.bfloat16
F32 = jnp.float32


def length_of(shard_ref, heads, start=0):
    coded = shard_ref[:1, start : start + LANES].astype(F32)
    return 16.0 * coded[:, heads : heads + 1] + coded[:, heads + 1 : heads + 2]


def silu(v):
    h = 0.5 * v
    return h + h * jnp.tanh(h)


def causal_conv(values, taps):
    rows = lax.broadcasted_iota(jnp.int32, (BLOCK_ROWS, values.shape[1]), 0)
    count = taps.shape[0]
    total = values * taps[count - 1 : count]
    for back in range(1, count):
        moved = pltpu.roll(values, back, 0)
        moved = jnp.concatenate(
            [jnp.where(rows >= back, moved[:BLOCK_ROWS], 0.0), moved[BLOCK_ROWS:]], axis=0
        )
        total = total + moved * taps[count - 1 - back : count - back]
    return silu(total)


def scan_kernel(
    which,
    meta_ref,
    shard_ref,
    projected_ref,
    taps_ref,
    bias_ref,
    log_rate_ref,
    skip_ref,
    scanned_ref,
    state_ref,
    decay_col,
    delta_row,
    decay_row,
    b_scr,
    c_scr,
    cb_scr,
):
    seq, half = scanned_ref.shape
    state_dim = state_ref.shape[1]
    groups = decay_col.shape[0]
    group_cols = HEADS_STEP * LANES // 2
    blocks = seq // SPAN
    every = slice(which * seq, (which + 1) * seq)
    position = lax.broadcasted_iota(jnp.int32, (seq, LANES), 0)
    lower = lax.broadcasted_iota(jnp.int32, (SPAN, SPAN), 0) >= lax.broadcasted_iota(
        jnp.int32, (SPAN, SPAN), 1
    )
    side = projected_ref[every, half:].astype(F32)
    conv = causal_conv(side[:, : 2 * state_dim], taps_ref[:, 2 * half :])
    b_short = conv[:, :state_dim].astype(BF)
    c_short = conv[:, state_dim:].astype(BF)
    b_scr[...] = b_short
    c_scr[...] = c_short
    for block in range(blocks):
        at = slice(block * SPAN, (block + 1) * SPAN)
        cb_scr[block] = lax.dot_general(
            c_short[at], b_short[at], (((1,), (1,)), ((), ())), preferred_element_type=F32
        )
        cb_scr[block] = jnp.where(lower, cb_scr[block], 0.0)
    spare = jnp.zeros((1, LANES - bias_ref.shape[1]), F32)
    raw = side[:, 2 * state_dim :] + jnp.concatenate([bias_ref[...], spare], axis=1)
    live = (position.astype(F32) < length_of(
            shard_ref, bias_ref.shape[1], half + 2 * state_dim
        )).astype(F32)
    delta = (jnp.maximum(raw, 0.0) + jnp.log1p(jnp.exp(-jnp.abs(raw)))) * live
    total = delta * (-LOG2E * jnp.exp(jnp.concatenate([log_rate_ref[...], spare], axis=1)))
    within = position % SPAN
    reach = 1
    while reach < SPAN:
        total = total + jnp.where(within >= reach, pltpu.roll(total, reach, 0), 0.0)
        reach *= 2
    turned = jnp.transpose(total)
    turned_delta = jnp.transpose(delta)
    for group in range(groups):
        at = slice(group * HEADS_STEP, (group + 1) * HEADS_STEP)
        decay_col[group] = total[:, at]
        delta_row[group] = turned_delta[at]
        decay_row[group] = turned[at]

    left = lax.broadcasted_iota(jnp.int32, (SPAN, LANES), 1) < LANES // 2
    top = lax.broadcasted_iota(jnp.int32, (LANES, state_dim), 0) < LANES // 2

    def group(step, carry):
        group_here = meta_ref[0] * (groups // 2) + step
        decays = decay_col[group_here]
        delta_of = delta_row[group_here]
        rows_of = decay_row[group_here]
        weight_of = delta_of * jnp.exp2(
            jnp.concatenate(
                [
                    rows_of[:, end - 1 : end] - rows_of[:, end - SPAN : end]
                    for end in range(SPAN, seq + 1, SPAN)
                ],
                axis=1,
            )
        )
        for pair in range(HEADS_STEP // 2):
            here = pl.ds(pl.multiple_of(step * group_cols + pair * LANES, LANES), LANES)
            taps_at = pl.multiple_of(meta_ref[0] * half + step * group_cols + pair * LANES, LANES)
            taps_at = pl.ds(taps_at, LANES)
            one, two = 2 * pair, 2 * pair + 1
            x_conv = causal_conv(projected_ref[every, here].astype(F32), taps_ref[:, taps_at])
            head = group_here * HEADS_STEP + one
            skip = jnp.where(left[:1], skip_ref[head], skip_ref[head + 1])
            state = jnp.zeros((LANES, state_dim), F32)
            for block in range(blocks):
                at = slice(block * SPAN, (block + 1) * SPAN)
                x_here = x_conv[at]
                cb = cb_scr[block]
                d_one, d_two = decays[at, one : one + 1], decays[at, two : two + 1]
                mix_one = cb * jnp.exp2(jnp.minimum(d_one - rows_of[one : one + 1, at], 0.0)) * delta_of[one : one + 1, at]
                mix_two = cb * jnp.exp2(jnp.minimum(d_two - rows_of[two : two + 1, at], 0.0)) * delta_of[two : two + 1, at]
                decay = jnp.where(left, d_one, d_two)
                short = x_here.astype(BF)
                zero = jnp.zeros_like(short)
                mixing = jnp.concatenate([mix_one.astype(BF), mix_two.astype(BF)], axis=1)
                spread = jnp.concatenate(
                    [jnp.where(left, short, zero), jnp.where(left, zero, short)], axis=0
                )
                out = jnp.dot(mixing, spread, preferred_element_type=F32)
                if block:
                    out = out + jnp.exp2(decay) * lax.dot_general(
                        c_scr[at],
                        state.astype(BF),
                        (((1,), (1,)), ((), ())),
                        preferred_element_type=F32,
                    )
                weighted = jnp.transpose(short).astype(F32) * jnp.where(
                    top, weight_of[one : one + 1, at], weight_of[two : two + 1, at]
                )
                fresh = jnp.dot(weighted.astype(BF), b_scr[at], preferred_element_type=F32)
                if block:
                    fade = jnp.where(
                        top,
                        jnp.exp2(d_one[SPAN - 1 : SPAN]),
                        jnp.exp2(d_two[SPAN - 1 : SPAN]),
                    )
                    fresh = fade * state + fresh
                state = fresh
                scanned_ref[at, here] = out + skip * x_here
            state_ref[here, :] = state
        return carry

    lax.fori_loop(0, groups // 2, group, 0)


def scan(which, meta, shard, projected, conv_weight, bias, log_rate, skip, width):
    seq, total = projected.shape[0] // 2, projected.shape[1]
    state_dim = width // 2
    half = total - width - LANES
    groups = 2 * half // (HEADS_STEP * LANES // 2)
    scalars = pl.BlockSpec(memory_space=pltpu.SMEM)
    whole = pl.BlockSpec(memory_space=pltpu.VMEM)
    return pl.pallas_call(
        functools.partial(scan_kernel, which),
        in_specs=[scalars] + [whole] * 5 + [scalars],
        out_specs=[whole] * 2,
        out_shape=[
            jax.ShapeDtypeStruct((seq, half), F32),
            jax.ShapeDtypeStruct((half, state_dim), F32),
        ],
        scratch_shapes=[
            pltpu.VMEM((groups, seq, HEADS_STEP), F32),
            pltpu.VMEM((groups, HEADS_STEP, seq), F32),
            pltpu.VMEM((groups, HEADS_STEP, seq), F32),
            pltpu.VMEM((seq, state_dim), BF),
            pltpu.VMEM((seq, state_dim), BF),
            pltpu.VMEM((seq // SPAN, SPAN, SPAN), F32),
        ],
        compiler_params=pltpu.CompilerParams(vmem_limit_bytes=16 << 20),
        cost_estimate=pl.CostEstimate(
            flops=2 * half * seq * 640, transcendentals=half * seq * 6, bytes_accessed=5 << 20
        ),
        name="scan",
    )(meta, shard, projected, conv_weight, bias, log_rate, skip)


def shards_kernel(
    meta_ref, lengths_ref, input_ref, state_ref, step_ref, gate_ref, out_ref, kept_ref, sent_ref
):
    rows, half = input_ref.shape[0], input_ref.shape[1] // 2
    width, heads = state_ref.shape[1], step_ref.shape[1]
    length = lengths_ref[meta_ref[1]]
    row = lax.broadcasted_iota(jnp.int32, (rows, LANES), 0)
    lane = lax.broadcasted_iota(jnp.int32, (rows, LANES), 1)
    coded = jnp.where(lane == heads, length >> 4, jnp.where(lane == heads + 1, length & 15, 0))
    coded = jnp.where(row == 0, coded, 0).astype(F32).astype(BF)
    for ref, core in ((kept_ref, meta_ref[0]), (sent_ref, 1 - meta_ref[0])):
        at = pl.ds(pl.multiple_of(core * half, half), half)
        ref[:, :half] = input_ref[:, at].astype(BF)
        ref[:, half : half + width] = state_ref[...].astype(BF)
        ref[:, half + width : half + width + LANES] = coded
        ref[:, half + width : half + width + heads] = step_ref[...].astype(BF)
        start = half + width + LANES
        ref[:, start : start + half] = gate_ref[:, at].astype(BF)
        ref[:, start + half :] = out_ref[:, at].astype(BF)


def shards(meta, lengths, inputs, state, step, gate, out):
    rows, inner = inputs.shape
    total = 3 * (inner // 2) + state.shape[1] + LANES
    scalars = pl.BlockSpec(memory_space=pltpu.SMEM)
    whole = pl.BlockSpec(memory_space=pltpu.VMEM)
    return pl.pallas_call(
        shards_kernel,
        in_specs=[scalars] * 2 + [whole] * 5,
        out_specs=[whole] * 2,
        out_shape=[jax.ShapeDtypeStruct((rows, total), BF)] * 2,
        name="shards",
    )(meta, lengths, inputs, state, step, gate, out)


def join_kernel(held_ref, moved_ref, *outs):
    rows, start = held_ref.shape[0], 0
    for out_ref in outs:
        cols = slice(start, start + out_ref.shape[1])
        out_ref[:rows] = held_ref[:, cols]
        out_ref[rows:] = moved_ref[:, cols]
        start += out_ref.shape[1]


def join(held, moved, *widths):
    rows, total = held.shape
    whole = pl.BlockSpec(memory_space=pltpu.VMEM)
    return pl.pallas_call(
        join_kernel,
        in_specs=[whole] * 2,
        out_specs=[whole] * len(widths),
        out_shape=[jax.ShapeDtypeStruct((2 * rows, width), BF) for width in widths],
        compiler_params=pltpu.CompilerParams(vmem_limit_bytes=6 << 20),
        cost_estimate=pl.CostEstimate(
            flops=0, transcendentals=0, bytes_accessed=8 * rows * total
        ),
        name="join",
    )(held, moved)


def project_kernel(first, tokens_ref, *refs):
    begin_ref, pieces, out_ref = refs[0], refs[:-1], refs[-1]
    if not first:
        pieces = pieces[1:]
    depth, total = pieces[0].shape
    tokens = jnp.concatenate(
        [
            tokens_ref[:, at : at + depth]
            for at in range(0 if first else depth, tokens_ref.shape[1], 2 * depth)
        ],
        axis=1,
    )
    tile = total // 5
    for at in range(0, total, tile):
        cols = slice(at, at + tile)
        weight = jnp.concatenate([piece[:, cols] for piece in pieces], axis=0)
        part = jnp.dot(tokens, weight, preferred_element_type=F32)
        if not first:
            part = part + begin_ref[:, cols]
        out_ref[:, cols] = part.astype(out_ref.dtype)


def project(tokens, pieces, begun=None):
    rows, model = tokens.shape
    depth, total = pieces[0].shape
    first = begun is None
    whole = pl.BlockSpec(memory_space=pltpu.VMEM)
    begun = () if first else (begun,)
    return pl.pallas_call(
        functools.partial(project_kernel, first),
        in_specs=[whole] * (1 + len(begun) + len(pieces)),
        out_specs=whole,
        out_shape=jax.ShapeDtypeStruct((rows, total), F32 if first else BF),
        compiler_params=pltpu.CompilerParams(vmem_limit_bytes=16 << 20),
        cost_estimate=pl.CostEstimate(
            flops=rows * model * total, transcendentals=0, bytes_accessed=10 << 20
        ),
        name="project",
    )(tokens, *begun, *pieces)


def share_kernel(which, meta_ref, places_ref, tokens_ref, scanned_ref, gain_ref, *refs):
    pieces, (share_ref, square_ref, gated_scr) = refs[:-3], refs[-3:]
    seq, half = scanned_ref.shape
    rows = slice(which * seq, (which + 1) * seq)
    tile = half // 3
    square_ref[...] = jnp.zeros_like(square_ref)
    for at in range(0, half, tile):
        cols = slice(at, at + tile)
        weight = jnp.concatenate([piece[:, cols] for piece in pieces], axis=0)
        gate = jnp.dot(tokens_ref[rows], weight, preferred_element_type=F32).astype(BF)
        gated = scanned_ref[:, cols] * silu(gate.astype(F32))
        gain_at = pl.multiple_of(meta_ref[0] * half + at, LANES)
        gated_scr[:, cols] = (gated * gain_ref[:, pl.ds(gain_at, tile)]).astype(BF)
        square = gated * gated
        for lane in range(0, tile, LANES):
            square_ref[...] += square[:, lane : lane + LANES]
    steps = 4
    depth = pieces[0].shape[0] // steps
    each = depth // BLOCK_ROWS
    for step in range(steps):
        weight = jnp.concatenate(
            [piece[step * depth : (step + 1) * depth, half:] for piece in pieces], axis=0
        )
        total = lax.dot_general(
            weight, gated_scr[...], (((1,), (1,)), ((), ())), preferred_element_type=F32
        )
        for index in range(len(pieces)):
            for block in range(each):
                at = (index * each + block) * BLOCK_ROWS
                place = places_ref[(index * steps + step) * each + block]
                share_ref[pl.ds(pl.multiple_of(place, BLOCK_ROWS), BLOCK_ROWS), :] = total[
                    at : at + BLOCK_ROWS
                ]


def out_share(which, meta, places, tokens, scanned, gain, pieces):
    seq, half = scanned.shape
    model = tokens.shape[1]
    scalars = pl.BlockSpec(memory_space=pltpu.SMEM)
    whole = pl.BlockSpec(memory_space=pltpu.VMEM)
    return pl.pallas_call(
        functools.partial(share_kernel, which),
        in_specs=[scalars] * 2 + [whole] * (3 + len(pieces)),
        out_specs=[whole] * 2,
        out_shape=[
            jax.ShapeDtypeStruct((model, seq), F32),
            jax.ShapeDtypeStruct((seq, LANES), F32),
        ],
        scratch_shapes=[pltpu.VMEM((seq, half), BF)],
        compiler_params=pltpu.CompilerParams(vmem_limit_bytes=16 << 20),
        cost_estimate=pl.CostEstimate(
            flops=4 * seq * half * model, transcendentals=seq * half, bytes_accessed=16 << 20
        ),
        name="out_share",
    )(meta, places, tokens, scanned, gain, *pieces)


def mix_kernel(shard_ref, mine_ref, other_ref, sq_mine, sq_other, pick_ref, out_ref):
    seq, model = out_ref.shape
    inner = 2 * model
    squares = jnp.transpose(sq_mine[...] + sq_other[...])
    mean = jnp.sum(squares, axis=0, keepdims=True) / inner
    live = lax.broadcasted_iota(jnp.int32, (1, seq), 1).astype(F32) < length_of(shard_ref, HEADS)
    scale = jnp.where(live, lax.rsqrt(mean + EPSILON), 0.0)
    tile = pick_ref.shape[0]
    for at in range(0, model, tile):
        rows = slice(at, at + tile)
        short = ((mine_ref[rows] + other_ref[rows]) * scale).astype(BF)
        out_ref[:, rows] = lax.dot_general(
            short, pick_ref[...], (((0,), (0,)), ((), ())), preferred_element_type=F32
        ).astype(BF)


def mix(shard, cut, mine, other, sq_mine, sq_other):
    model, seq = mine.shape
    tile = model // 4
    column = jnp.arange(tile, dtype=jnp.int32)
    chip, rest = column // (2 * SHARD_ROWS), column % (2 * SHARD_ROWS)
    target = rest // SHARD_ROWS * (tile // 2) + chip * SHARD_ROWS + rest % SHARD_ROWS
    pick = (target[:, None] == column[None]).astype(BF)
    whole = pl.BlockSpec(memory_space=pltpu.VMEM)
    fixed = lambda i: (0, 0)
    return pl.pallas_call(
        mix_kernel,
        grid=(1,),
        in_specs=[pl.BlockSpec((shard.shape[0], LANES), lambda i: (0, cut // LANES - 1))]
        + [whole] * 5,
        out_specs=whole,
        out_shape=jax.ShapeDtypeStruct((seq, model), BF),
        compiler_params=pltpu.CompilerParams(vmem_limit_bytes=16 << 20),
        cost_estimate=pl.CostEstimate(
            flops=2 * seq * tile * model, transcendentals=0, bytes_accessed=8 << 20
        ),
        name="mix",
    )(shard, mine, other, sq_mine, sq_other, pick)


EVERYONE = ("req", "unit")
DEVICES = 128
CORE = 16
SHARD_ROWS = 12
COLOURS = 3
BLOCK_ROWS = 8
LINKS = (1 << 2, 1, 1 << 5, 3 << 2, 3, 3 << 5)


def link_of(colour, core, step):
    return LINKS[(colour + 3 * core - step) % 6]


def hop(value, mask_of):
    return lax.ppermute(
        value, EVERYONE, [(d, d ^ mask_of((d // CORE) % 2)) for d in range(DEVICES)]
    )


def swap(value):
    return hop(value, lambda core: CORE)


def moved_over(held, step):
    return [hop(piece, lambda core, c=c: link_of(c, core, step)) for c, piece in enumerate(held)]


def joined(held, moved):
    return [
        lax.optimization_barrier(jnp.concatenate([h, m], axis=0)) for h, m in zip(held, moved)
    ]


def gathered_chip(me, core, colour, block):
    mask = jnp.zeros_like(block)
    for step in range(6):
        link = jnp.zeros_like(block)
        for c in range(COLOURS):
            here = jnp.where(core == 0, link_of(c, 0, step), link_of(c, 1, step))
            link = jnp.where(colour == c, here, link)
        mask = mask ^ (((block >> step) & 1) * link)
    return (me ^ mask) & ~CORE


def row_sources(me, core, model):
    row = jnp.arange(model, dtype=jnp.int32)
    colour, block = row // (model // COLOURS), row // BLOCK_ROWS % 64
    local = colour * BLOCK_ROWS + row % BLOCK_ROWS
    upper = (local >= SHARD_ROWS).astype(jnp.int32)
    device = gathered_chip(me, core, colour, block) + CORE * upper
    return device * SHARD_ROWS + local - SHARD_ROWS * upper


def row_places(me, core):
    index = jnp.arange(COLOURS * 64, dtype=jnp.int32)
    chip = gathered_chip(me, core, index // 64, index % 64)
    chip = (chip >> 5) * CORE + (chip & (CORE - 1))
    return chip * 2 * SHARD_ROWS + index // 64 * BLOCK_ROWS


def body(
    tokens,
    lengths,
    gate_proj,
    input_proj,
    state_proj,
    step_proj,
    out_proj,
    conv_weight,
    step_bias,
    log_rate,
    skip_gain,
    norm_gain,
):
    unit_id = lax.axis_index("unit")
    me = lax.axis_index(EVERYONE).astype(jnp.int32)
    core = (me // CORE) % 2
    first_core = core == 0
    seq_len, model_dim = tokens.shape[1:]
    inner_dim = gate_proj.shape[1]
    head_count = log_rate.shape[0]
    head_dim = inner_dim // head_count
    width = state_proj.shape[1]
    half = inner_dim // 2

    cut = half + width + LANES
    meta = jnp.stack([core, unit_id])
    kept, sent = shards(
        meta, lengths, input_proj, state_proj, step_proj, gate_proj, out_proj
    )
    sent, unit_id = lax.optimization_barrier((sent, unit_id))
    received = swap(sent)
    pair = jnp.concatenate(
        [jnp.where(first_core, kept, received), jnp.where(first_core, received, kept)], axis=0
    )
    held = [pair[8 * c : 8 * c + 8] for c in range(COLOURS)]
    for step in range(3):
        held = joined(held, moved_over(held, step))
    held = [join(h, m, cut + 2 * half)[0] for h, m in zip(held, moved_over(held, 3))]
    moved = moved_over(held, 4)

    own = lax.dynamic_index_in_dim(tokens, unit_id, 0, keepdims=False)
    both = jnp.concatenate([own, swap(own)], axis=0)
    pick = jnp.arange(model_dim, dtype=jnp.int32)[:, None] == row_sources(me, core, model_dim)[None]
    both = jnp.dot(both, pick.astype(BF), preferred_element_type=F32).astype(BF)
    moved[0], both, places = lax.optimization_barrier((moved[0], both, row_places(me, core)))
    early, late = zip(*[join(h, m, cut, 2 * half) for h, m in zip(held, moved)])
    late = list(late)
    moved = moved_over(early, 5)
    begun = project(both, early)
    moved[0], begun = lax.optimization_barrier((moved[0], begun))
    for c in range(COLOURS):
        moved[c], late[c] = lax.optimization_barrier((moved[c], late[c]))
    late = [piece for two in zip(late, moved_over(late, 5)) for piece in two]

    projected = project(both, moved, begun)
    inputs = (projected, conv_weight, step_bias[None], log_rate[None], skip_gain, width)
    scanned_other, state_sent = scan(1, meta, received, *inputs)
    state_other = swap(state_sent)
    scanned, state = scan(0, meta, kept, *inputs)
    scanned_other, scanned, state_other = lax.optimization_barrier(
        (scanned_other, scanned, state_other)
    )
    shared = (meta, places, both)
    sent, square_sent = out_share(1, *shared, scanned_other, norm_gain[None], late)
    other, square_other = swap(sent), swap(square_sent)
    mine, square = out_share(0, *shared, scanned, norm_gain[None], late)
    mixed = mix(kept, cut, mine, other, square, square_other)
    state = jnp.concatenate(
        [jnp.where(first_core, state, state_other), jnp.where(first_core, state_other, state)]
    )
    return (mixed[None], state.reshape(1, head_count, head_dim, width // 2))


def solution(mesh):
    placed = (
        P("req", None, None),
        P("req"),
        P(("req", "unit"), None),
        P(("req", "unit"), None),
        P(("req", "unit"), None),
        P(("req", "unit"), None),
        P(("req", "unit"), None),
        P(),
        P(),
        P(),
        P(),
        P(),
    )
    return jax.shard_map(
        body,
        mesh=mesh,
        in_specs=placed,
        out_specs=(P(("req", "unit"), None, None), P(("req", "unit"), None, None, None)),
        check_vma=False,
    )
```

```python
import functools

import jax
import jax.numpy as jnp
from jax import lax
from jax.experimental import pallas as pl
from jax.experimental.pallas import tpu as pltpu
from jax.sharding import PartitionSpec as P

SPAN = 128
LANES = 128
HEADS = 48
HEADS_STEP = 8
EPSILON = 1e-05
LOG2E = 1.4426950408889634
BF = jnp.bfloat16
F32 = jnp.float32


def length_of(shard_ref, heads, start=0):
    coded = shard_ref[:1, start : start + LANES].astype(F32)
    return 16.0 * coded[:, heads : heads + 1] + coded[:, heads + 1 : heads + 2]


def silu(v):
    h = 0.5 * v
    return h + h * jnp.tanh(h)


def causal_conv(values, taps):
    rows = lax.broadcasted_iota(jnp.int32, (BLOCK_ROWS, values.shape[1]), 0)
    count = taps.shape[0]
    total = values * taps[count - 1 : count]
    for back in range(1, count):
        moved = pltpu.roll(values, back, 0)
        moved = jnp.concatenate(
            [jnp.where(rows >= back, moved[:BLOCK_ROWS], 0.0), moved[BLOCK_ROWS:]], axis=0
        )
        total = total + moved * taps[count - 1 - back : count - back]
    return silu(total)


def scan_kernel(
    which,
    meta_ref,
    shard_ref,
    projected_ref,
    taps_ref,
    bias_ref,
    log_rate_ref,
    skip_ref,
    scanned_ref,
    state_ref,
    decay_col,
    delta_row,
    decay_row,
    b_scr,
    c_scr,
    cb_scr,
):
    seq, half = scanned_ref.shape
    state_dim = state_ref.shape[1]
    groups = decay_col.shape[0]
    group_cols = HEADS_STEP * LANES // 2
    blocks = seq // SPAN
    every = slice(which * seq, (which + 1) * seq)
    position = lax.broadcasted_iota(jnp.int32, (seq, LANES), 0)
    lower = lax.broadcasted_iota(jnp.int32, (SPAN, SPAN), 0) >= lax.broadcasted_iota(
        jnp.int32, (SPAN, SPAN), 1
    )
    side = projected_ref[every, half:].astype(F32)
    conv = causal_conv(side[:, : 2 * state_dim], taps_ref[:, 2 * half :])
    b_short = conv[:, :state_dim].astype(BF)
    c_short = conv[:, state_dim:].astype(BF)
    b_scr[...] = b_short
    c_scr[...] = c_short
    for block in range(blocks):
        at = slice(block * SPAN, (block + 1) * SPAN)
        cb_scr[block] = lax.dot_general(
            c_short[at], b_short[at], (((1,), (1,)), ((), ())), preferred_element_type=F32
        )
        cb_scr[block] = jnp.where(lower, cb_scr[block], 0.0)
    spare = jnp.zeros((1, LANES - bias_ref.shape[1]), F32)
    raw = side[:, 2 * state_dim :] + jnp.concatenate([bias_ref[...], spare], axis=1)
    live = (position.astype(F32) < length_of(
            shard_ref, bias_ref.shape[1], half + 2 * state_dim
        )).astype(F32)
    delta = (jnp.maximum(raw, 0.0) + jnp.log1p(jnp.exp(-jnp.abs(raw)))) * live
    total = delta * (-LOG2E * jnp.exp(jnp.concatenate([log_rate_ref[...], spare], axis=1)))
    within = position % SPAN
    reach = 1
    while reach < SPAN:
        total = total + jnp.where(within >= reach, pltpu.roll(total, reach, 0), 0.0)
        reach *= 2
    turned = jnp.transpose(total)
    turned_delta = jnp.transpose(delta)
    for group in range(groups):
        at = slice(group * HEADS_STEP, (group + 1) * HEADS_STEP)
        decay_col[group] = total[:, at]
        delta_row[group] = turned_delta[at]
        decay_row[group] = turned[at]

    left = lax.broadcasted_iota(jnp.int32, (SPAN, LANES), 1) < LANES // 2
    top = lax.broadcasted_iota(jnp.int32, (LANES, state_dim), 0) < LANES // 2

    def group(step, carry):
        group_here = meta_ref[0] * (groups // 2) + step
        decays = decay_col[group_here]
        delta_of = delta_row[group_here]
        rows_of = decay_row[group_here]
        weight_of = delta_of * jnp.exp2(
            jnp.concatenate(
                [
                    rows_of[:, end - 1 : end] - rows_of[:, end - SPAN : end]
                    for end in range(SPAN, seq + 1, SPAN)
                ],
                axis=1,
            )
        )
        for pair in range(HEADS_STEP // 2):
            here = pl.ds(pl.multiple_of(step * group_cols + pair * LANES, LANES), LANES)
            taps_at = pl.multiple_of(meta_ref[0] * half + step * group_cols + pair * LANES, LANES)
            taps_at = pl.ds(taps_at, LANES)
            one, two = 2 * pair, 2 * pair + 1
            x_conv = causal_conv(projected_ref[every, here].astype(F32), taps_ref[:, taps_at])
            head = group_here * HEADS_STEP + one
            skip = jnp.where(left[:1], skip_ref[head], skip_ref[head + 1])
            state = jnp.zeros((LANES, state_dim), F32)
            for block in range(blocks):
                at = slice(block * SPAN, (block + 1) * SPAN)
                x_here = x_conv[at]
                cb = cb_scr[block]
                d_one, d_two = decays[at, one : one + 1], decays[at, two : two + 1]
                mix_one = cb * jnp.exp2(jnp.minimum(d_one - rows_of[one : one + 1, at], 0.0)) * delta_of[one : one + 1, at]
                mix_two = cb * jnp.exp2(jnp.minimum(d_two - rows_of[two : two + 1, at], 0.0)) * delta_of[two : two + 1, at]
                decay = jnp.where(left, d_one, d_two)
                short = x_here.astype(BF)
                zero = jnp.zeros_like(short)
                mixing = jnp.concatenate([mix_one.astype(BF), mix_two.astype(BF)], axis=1)
                spread = jnp.concatenate(
                    [jnp.where(left, short, zero), jnp.where(left, zero, short)], axis=0
                )
                out = jnp.dot(mixing, spread, preferred_element_type=F32)
                if block:
                    out = out + jnp.exp2(decay) * lax.dot_general(
                        c_scr[at],
                        state.astype(BF),
                        (((1,), (1,)), ((), ())),
                        preferred_element_type=F32,
                    )
                weighted = jnp.transpose(short).astype(F32) * jnp.where(
                    top, weight_of[one : one + 1, at], weight_of[two : two + 1, at]
                )
                fresh = jnp.dot(weighted.astype(BF), b_scr[at], preferred_element_type=F32)
                if block:
                    fade = jnp.where(
                        top,
                        jnp.exp2(d_one[SPAN - 1 : SPAN]),
                        jnp.exp2(d_two[SPAN - 1 : SPAN]),
                    )
                    fresh = fade * state + fresh
                state = fresh
                scanned_ref[at, here] = out + skip * x_here
            state_ref[here, :] = state
        return carry

    lax.fori_loop(0, groups // 2, group, 0)


def scan(which, meta, shard, projected, conv_weight, bias, log_rate, skip, width):
    seq, total = projected.shape[0] // 2, projected.shape[1]
    state_dim = width // 2
    half = total - width - LANES
    groups = 2 * half // (HEADS_STEP * LANES // 2)
    scalars = pl.BlockSpec(memory_space=pltpu.SMEM)
    whole = pl.BlockSpec(memory_space=pltpu.VMEM)
    return pl.pallas_call(
        functools.partial(scan_kernel, which),
        in_specs=[scalars] + [whole] * 5 + [scalars],
        out_specs=[whole] * 2,
        out_shape=[
            jax.ShapeDtypeStruct((seq, half), F32),
            jax.ShapeDtypeStruct((half, state_dim), F32),
        ],
        scratch_shapes=[
            pltpu.VMEM((groups, seq, HEADS_STEP), F32),
            pltpu.VMEM((groups, HEADS_STEP, seq), F32),
            pltpu.VMEM((groups, HEADS_STEP, seq), F32),
            pltpu.VMEM((seq, state_dim), BF),
            pltpu.VMEM((seq, state_dim), BF),
            pltpu.VMEM((seq // SPAN, SPAN, SPAN), F32),
        ],
        compiler_params=pltpu.CompilerParams(vmem_limit_bytes=16 << 20),
        cost_estimate=pl.CostEstimate(
            flops=2 * half * seq * 640, transcendentals=half * seq * 6, bytes_accessed=5 << 20
        ),
        name="scan",
    )(meta, shard, projected, conv_weight, bias, log_rate, skip)


def shards_kernel(
    meta_ref, lengths_ref, input_ref, state_ref, step_ref, gate_ref, out_ref, kept_ref, sent_ref
):
    rows, half = input_ref.shape[0], input_ref.shape[1] // 2
    width, heads = state_ref.shape[1], step_ref.shape[1]
    length = lengths_ref[meta_ref[1]]
    row = lax.broadcasted_iota(jnp.int32, (rows, LANES), 0)
    lane = lax.broadcasted_iota(jnp.int32, (rows, LANES), 1)
    coded = jnp.where(lane == heads, length >> 4, jnp.where(lane == heads + 1, length & 15, 0))
    coded = jnp.where(row == 0, coded, 0).astype(F32).astype(BF)
    for ref, core in ((kept_ref, meta_ref[0]), (sent_ref, 1 - meta_ref[0])):
        at = pl.ds(pl.multiple_of(core * half, half), half)
        ref[:, :half] = input_ref[:, at].astype(BF)
        ref[:, half : half + width] = state_ref[...].astype(BF)
        ref[:, half + width : half + width + LANES] = coded
        ref[:, half + width : half + width + heads] = step_ref[...].astype(BF)
        start = half + width + LANES
        ref[:, start : start + half] = gate_ref[:, at].astype(BF)
        ref[:, start + half :] = out_ref[:, at].astype(BF)


def shards(meta, lengths, inputs, state, step, gate, out):
    rows, inner = inputs.shape
    total = 3 * (inner // 2) + state.shape[1] + LANES
    scalars = pl.BlockSpec(memory_space=pltpu.SMEM)
    whole = pl.BlockSpec(memory_space=pltpu.VMEM)
    return pl.pallas_call(
        shards_kernel,
        in_specs=[scalars] * 2 + [whole] * 5,
        out_specs=[whole] * 2,
        out_shape=[jax.ShapeDtypeStruct((rows, total), BF)] * 2,
        name="shards",
    )(meta, lengths, inputs, state, step, gate, out)


def join_kernel(start, held_ref, moved_ref, out_ref):
    rows, cols = held_ref.shape[0], slice(start, start + out_ref.shape[1])
    out_ref[:rows] = held_ref[:, cols]
    out_ref[rows:] = moved_ref[:, cols]


def join(held, moved, start, stop):
    rows, width = held.shape[0], stop - start
    whole = pl.BlockSpec(memory_space=pltpu.VMEM)
    return pl.pallas_call(
        functools.partial(join_kernel, start),
        in_specs=[whole] * 2,
        out_specs=whole,
        out_shape=jax.ShapeDtypeStruct((2 * rows, width), BF),
        compiler_params=pltpu.CompilerParams(vmem_limit_bytes=6 << 20),
        cost_estimate=pl.CostEstimate(
            flops=0, transcendentals=0, bytes_accessed=8 * rows * width
        ),
        name="join",
    )(held, moved)


def project_kernel(first, tokens_ref, *refs):
    begin_ref, pieces, out_ref = refs[0], refs[:-1], refs[-1]
    if not first:
        pieces = pieces[1:]
    depth, total = pieces[0].shape
    tokens = jnp.concatenate(
        [
            tokens_ref[:, at : at + depth]
            for at in range(0 if first else depth, tokens_ref.shape[1], 2 * depth)
        ],
        axis=1,
    )
    tile = total // 5
    for at in range(0, total, tile):
        cols = slice(at, at + tile)
        weight = jnp.concatenate([piece[:, cols] for piece in pieces], axis=0)
        part = jnp.dot(tokens, weight, preferred_element_type=F32)
        if not first:
            part = part + begin_ref[:, cols]
        out_ref[:, cols] = part.astype(out_ref.dtype)


def project(tokens, pieces, begun=None):
    rows, model = tokens.shape
    depth, total = pieces[0].shape
    first = begun is None
    whole = pl.BlockSpec(memory_space=pltpu.VMEM)
    begun = () if first else (begun,)
    return pl.pallas_call(
        functools.partial(project_kernel, first),
        in_specs=[whole] * (1 + len(begun) + len(pieces)),
        out_specs=whole,
        out_shape=jax.ShapeDtypeStruct((rows, total), F32 if first else BF),
        compiler_params=pltpu.CompilerParams(vmem_limit_bytes=16 << 20),
        cost_estimate=pl.CostEstimate(
            flops=rows * model * total, transcendentals=0, bytes_accessed=10 << 20
        ),
        name="project",
    )(tokens, *begun, *pieces)


def share_kernel(which, meta_ref, places_ref, tokens_ref, scanned_ref, gain_ref, *refs):
    pieces, (share_ref, square_ref, gated_scr) = refs[:-3], refs[-3:]
    seq, half = scanned_ref.shape
    rows = slice(which * seq, (which + 1) * seq)
    tile = half // 3
    square_ref[...] = jnp.zeros_like(square_ref)
    for at in range(0, half, tile):
        cols = slice(at, at + tile)
        weight = jnp.concatenate([piece[:, cols] for piece in pieces], axis=0)
        gate = jnp.dot(tokens_ref[rows], weight, preferred_element_type=F32).astype(BF)
        gated = scanned_ref[:, cols] * silu(gate.astype(F32))
        gain_at = pl.multiple_of(meta_ref[0] * half + at, LANES)
        gated_scr[:, cols] = (gated * gain_ref[:, pl.ds(gain_at, tile)]).astype(BF)
        square = gated * gated
        for lane in range(0, tile, LANES):
            square_ref[...] += square[:, lane : lane + LANES]
    steps = 4
    depth = pieces[0].shape[0] // steps
    each = depth // BLOCK_ROWS
    for step in range(steps):
        weight = jnp.concatenate(
            [piece[step * depth : (step + 1) * depth, half:] for piece in pieces], axis=0
        )
        total = lax.dot_general(
            weight, gated_scr[...], (((1,), (1,)), ((), ())), preferred_element_type=F32
        )
        for index in range(len(pieces)):
            for block in range(each):
                at = (index * each + block) * BLOCK_ROWS
                place = places_ref[(index * steps + step) * each + block]
                share_ref[pl.ds(pl.multiple_of(place, BLOCK_ROWS), BLOCK_ROWS), :] = total[
                    at : at + BLOCK_ROWS
                ]


def out_share(which, meta, places, tokens, scanned, gain, pieces):
    seq, half = scanned.shape
    model = tokens.shape[1]
    scalars = pl.BlockSpec(memory_space=pltpu.SMEM)
    whole = pl.BlockSpec(memory_space=pltpu.VMEM)
    return pl.pallas_call(
        functools.partial(share_kernel, which),
        in_specs=[scalars] * 2 + [whole] * (3 + len(pieces)),
        out_specs=[whole] * 2,
        out_shape=[
            jax.ShapeDtypeStruct((model, seq), F32),
            jax.ShapeDtypeStruct((seq, LANES), F32),
        ],
        scratch_shapes=[pltpu.VMEM((seq, half), BF)],
        compiler_params=pltpu.CompilerParams(vmem_limit_bytes=16 << 20),
        cost_estimate=pl.CostEstimate(
            flops=4 * seq * half * model, transcendentals=seq * half, bytes_accessed=16 << 20
        ),
        name="out_share",
    )(meta, places, tokens, scanned, gain, *pieces)


def mix_kernel(
    meta_ref,
    shard_ref,
    mine_ref,
    other_ref,
    sq_mine,
    sq_other,
    pick_ref,
    state_ref,
    state_other_ref,
    out_ref,
    state_out_ref,
    sems,
):
    core, half = meta_ref[0], state_ref.shape[0]
    copies = []
    for index, source in enumerate((state_ref, state_other_ref)):
        place = (core if index == 0 else 1 - core) * half
        place = pl.ds(pl.multiple_of(place, half), half)
        copies.append(pltpu.make_async_copy(source, state_out_ref.at[place], sems.at[index]))
        copies[-1].start()
    seq, model = out_ref.shape
    inner = 2 * model
    squares = jnp.transpose(sq_mine[...] + sq_other[...])
    mean = jnp.sum(squares, axis=0, keepdims=True) / inner
    live = lax.broadcasted_iota(jnp.int32, (1, seq), 1).astype(F32) < length_of(shard_ref, HEADS)
    scale = jnp.where(live, lax.rsqrt(mean + EPSILON), 0.0)
    tile = pick_ref.shape[0]
    for at in range(0, model, tile):
        rows = slice(at, at + tile)
        short = ((mine_ref[rows] + other_ref[rows]) * scale).astype(BF)
        out_ref[:, rows] = lax.dot_general(
            short, pick_ref[...], (((0,), (0,)), ((), ())), preferred_element_type=F32
        ).astype(BF)
    for copy in copies:
        copy.wait()


def mix(meta, shard, cut, mine, other, sq_mine, sq_other, state, state_other):
    model, seq = mine.shape
    tile = model // 4
    column = jnp.arange(tile, dtype=jnp.int32)
    chip, rest = column // (2 * SHARD_ROWS), column % (2 * SHARD_ROWS)
    target = rest // SHARD_ROWS * (tile // 2) + chip * SHARD_ROWS + rest % SHARD_ROWS
    pick = (target[:, None] == column[None]).astype(BF)
    whole = pl.BlockSpec(memory_space=pltpu.VMEM)
    anywhere = pl.BlockSpec(memory_space=pl.ANY)
    return pl.pallas_call(
        mix_kernel,
        grid=(1,),
        in_specs=[
            pl.BlockSpec(memory_space=pltpu.SMEM),
            pl.BlockSpec((shard.shape[0], LANES), lambda i: (0, cut // LANES - 1)),
        ]
        + [whole] * 5
        + [anywhere] * 2,
        out_specs=[whole, anywhere],
        out_shape=[
            jax.ShapeDtypeStruct((seq, model), BF),
            jax.ShapeDtypeStruct((2 * state.shape[0], state.shape[1]), F32),
        ],
        scratch_shapes=[pltpu.SemaphoreType.DMA((2,))],
        compiler_params=pltpu.CompilerParams(vmem_limit_bytes=16 << 20),
        cost_estimate=pl.CostEstimate(
            flops=2 * seq * tile * model, transcendentals=0, bytes_accessed=8 << 20
        ),
        name="mix",
    )(meta, shard, mine, other, sq_mine, sq_other, pick, state, state_other)


EVERYONE = ("req", "unit")
DEVICES = 128
CORE = 16
SHARD_ROWS = 12
COLOURS = 3
BLOCK_ROWS = 8
LINKS = (1 << 2, 1, 1 << 5, 3 << 2, 3, 3 << 5)


def link_of(colour, core, step):
    return LINKS[(colour + 3 * core - step) % 6]


def hop(value, mask_of):
    return lax.ppermute(
        value, EVERYONE, [(d, d ^ mask_of((d // CORE) % 2)) for d in range(DEVICES)]
    )


def swap(value):
    return hop(value, lambda core: CORE)


def moved_over(held, step):
    return [hop(piece, lambda core, c=c: link_of(c, core, step)) for c, piece in enumerate(held)]


def joined(held, moved):
    return [
        lax.optimization_barrier(jnp.concatenate([h, m], axis=0)) for h, m in zip(held, moved)
    ]


def gathered_chip(me, core, colour, block):
    mask = jnp.zeros_like(block)
    for step in range(6):
        link = jnp.zeros_like(block)
        for c in range(COLOURS):
            here = jnp.where(core == 0, link_of(c, 0, step), link_of(c, 1, step))
            link = jnp.where(colour == c, here, link)
        mask = mask ^ (((block >> step) & 1) * link)
    return (me ^ mask) & ~CORE


def row_sources(me, core, model):
    row = jnp.arange(model, dtype=jnp.int32)
    colour, block = row // (model // COLOURS), row // BLOCK_ROWS % 64
    local = colour * BLOCK_ROWS + row % BLOCK_ROWS
    upper = (local >= SHARD_ROWS).astype(jnp.int32)
    device = gathered_chip(me, core, colour, block) + CORE * upper
    return device * SHARD_ROWS + local - SHARD_ROWS * upper


def row_places(me, core):
    index = jnp.arange(COLOURS * 64, dtype=jnp.int32)
    chip = gathered_chip(me, core, index // 64, index % 64)
    chip = (chip >> 5) * CORE + (chip & (CORE - 1))
    return chip * 2 * SHARD_ROWS + index // 64 * BLOCK_ROWS


def body(
    tokens,
    lengths,
    gate_proj,
    input_proj,
    state_proj,
    step_proj,
    out_proj,
    conv_weight,
    step_bias,
    log_rate,
    skip_gain,
    norm_gain,
):
    unit_id = lax.axis_index("unit")
    me = lax.axis_index(EVERYONE).astype(jnp.int32)
    core = (me // CORE) % 2
    first_core = core == 0
    seq_len, model_dim = tokens.shape[1:]
    inner_dim = gate_proj.shape[1]
    head_count = log_rate.shape[0]
    head_dim = inner_dim // head_count
    width = state_proj.shape[1]
    half = inner_dim // 2

    cut = half + width + LANES
    meta = jnp.stack([core, unit_id])
    kept, sent = shards(
        meta, lengths, input_proj, state_proj, step_proj, gate_proj, out_proj
    )
    sent, unit_id = lax.optimization_barrier((sent, unit_id))
    own = lax.dynamic_index_in_dim(tokens, unit_id, 0, keepdims=False)
    received, own = lax.optimization_barrier((swap(sent), own))
    pair = jnp.concatenate(
        [jnp.where(first_core, kept, received), jnp.where(first_core, received, kept)], axis=0
    )
    held = [pair[8 * c : 8 * c + 8] for c in range(COLOURS)]
    for step in range(3):
        held = joined(held, moved_over(held, step))
    held = [join(h, m, 0, cut + 2 * half) for h, m in zip(held, moved_over(held, 3))]
    moved = moved_over(held, 4)

    both = jnp.concatenate([own, swap(own)], axis=0)
    pick = jnp.arange(model_dim, dtype=jnp.int32)[:, None] == row_sources(me, core, model_dim)[None]
    both = jnp.dot(both, pick.astype(BF), preferred_element_type=F32).astype(BF)
    moved[0], both, places = lax.optimization_barrier((moved[0], both, row_places(me, core)))
    early = [join(h, m, 0, cut) for h, m in zip(held, moved)]
    early[2], held, rest = lax.optimization_barrier((early[2], held, moved))
    late = [join(h, m, cut, cut + 2 * half) for h, m in zip(held, rest)]
    moved = moved_over(early, 5)
    late[2], begun = lax.optimization_barrier((late[2], project(both, early)))
    late = [piece for two in zip(late, moved_over(late, 5)) for piece in two]

    projected = project(both, moved, begun)
    inputs = (projected, conv_weight, step_bias[None], log_rate[None], skip_gain, width)
    scanned_other, state_sent = scan(1, meta, received, *inputs)
    state_other = swap(state_sent)
    scanned, state = scan(0, meta, kept, *inputs)
    scanned_other, scanned, state_other = lax.optimization_barrier(
        (scanned_other, scanned, state_other)
    )
    shared = (meta, places, both)
    sent, square_sent = out_share(1, *shared, scanned_other, norm_gain[None], late)
    other, square_other = swap(sent), swap(square_sent)
    mine, square = out_share(0, *shared, scanned, norm_gain[None], late)
    mixed, state = mix(
        meta, kept, cut, mine, other, square, square_other, state, state_other
    )
    return (mixed[None], state.reshape(1, head_count, head_dim, width // 2))


def solution(mesh):
    placed = (
        P("req", None, None),
        P("req"),
        P(("req", "unit"), None),
        P(("req", "unit"), None),
        P(("req", "unit"), None),
        P(("req", "unit"), None),
        P(("req", "unit"), None),
        P(),
        P(),
        P(),
        P(),
        P(),
    )
    return jax.shard_map(
        body,
        mesh=mesh,
        in_specs=placed,
        out_specs=(P(("req", "unit"), None, None), P(("req", "unit"), None, None, None)),
        check_vma=False,
    )
```

```python
import functools

import jax
import jax.numpy as jnp
from jax import lax
from jax.experimental import pallas as pl
from jax.experimental.pallas import tpu as pltpu
from jax.sharding import PartitionSpec as P

SPAN = 128
LANES = 128
HEADS = 48
HEADS_STEP = 8
EPSILON = 1e-05
LOG2E = 1.4426950408889634
BF = jnp.bfloat16
F32 = jnp.float32


def length_of(shard_ref, heads, start=0):
    coded = shard_ref[:1, start : start + LANES].astype(F32)
    return 16.0 * coded[:, heads : heads + 1] + coded[:, heads + 1 : heads + 2]


def silu(v):
    h = 0.5 * v
    return h + h * jnp.tanh(h)


def causal_conv(values, taps):
    rows = lax.broadcasted_iota(jnp.int32, (BLOCK_ROWS, values.shape[1]), 0)
    count = taps.shape[0]
    total = values * taps[count - 1 : count]
    for back in range(1, count):
        moved = pltpu.roll(values, back, 0)
        moved = jnp.concatenate(
            [jnp.where(rows >= back, moved[:BLOCK_ROWS], 0.0), moved[BLOCK_ROWS:]], axis=0
        )
        total = total + moved * taps[count - 1 - back : count - back]
    return silu(total)


def scan_kernel(
    which,
    meta_ref,
    shard_ref,
    projected_ref,
    taps_ref,
    bias_ref,
    log_rate_ref,
    skip_ref,
    scanned_ref,
    state_ref,
    decay_col,
    delta_row,
    decay_row,
    b_scr,
    c_scr,
    cb_scr,
):
    seq, half = scanned_ref.shape
    state_dim = state_ref.shape[1]
    groups = decay_col.shape[0]
    group_cols = HEADS_STEP * LANES // 2
    blocks = seq // SPAN
    every = slice(which * seq, (which + 1) * seq)
    position = lax.broadcasted_iota(jnp.int32, (seq, LANES), 0)
    lower = lax.broadcasted_iota(jnp.int32, (SPAN, SPAN), 0) >= lax.broadcasted_iota(
        jnp.int32, (SPAN, SPAN), 1
    )
    side = projected_ref[every, half:].astype(F32)
    conv = causal_conv(side[:, : 2 * state_dim], taps_ref[:, 2 * half :])
    b_short = conv[:, :state_dim].astype(BF)
    c_short = conv[:, state_dim:].astype(BF)
    b_scr[...] = b_short
    c_scr[...] = c_short
    for block in range(blocks):
        at = slice(block * SPAN, (block + 1) * SPAN)
        cb_scr[block] = lax.dot_general(
            c_short[at], b_short[at], (((1,), (1,)), ((), ())), preferred_element_type=F32
        )
        cb_scr[block] = jnp.where(lower, cb_scr[block], 0.0)
    spare = jnp.zeros((1, LANES - bias_ref.shape[1]), F32)
    raw = side[:, 2 * state_dim :] + jnp.concatenate([bias_ref[...], spare], axis=1)
    live = (position.astype(F32) < length_of(
            shard_ref, bias_ref.shape[1], half + 2 * state_dim
        )).astype(F32)
    delta = (jnp.maximum(raw, 0.0) + jnp.log1p(jnp.exp(-jnp.abs(raw)))) * live
    total = delta * (-LOG2E * jnp.exp(jnp.concatenate([log_rate_ref[...], spare], axis=1)))
    within = position % SPAN
    reach = 1
    while reach < SPAN:
        total = total + jnp.where(within >= reach, pltpu.roll(total, reach, 0), 0.0)
        reach *= 2
    turned = jnp.transpose(total)
    turned_delta = jnp.transpose(delta)
    for group in range(groups):
        at = slice(group * HEADS_STEP, (group + 1) * HEADS_STEP)
        decay_col[group] = total[:, at]
        delta_row[group] = turned_delta[at]
        decay_row[group] = turned[at]

    left = lax.broadcasted_iota(jnp.int32, (SPAN, LANES), 1) < LANES // 2
    top = lax.broadcasted_iota(jnp.int32, (LANES, state_dim), 0) < LANES // 2

    def group(step, carry):
        group_here = meta_ref[0] * (groups // 2) + step
        decays = decay_col[group_here]
        delta_of = delta_row[group_here]
        rows_of = decay_row[group_here]
        weight_of = delta_of * jnp.exp2(
            jnp.concatenate(
                [
                    rows_of[:, end - 1 : end] - rows_of[:, end - SPAN : end]
                    for end in range(SPAN, seq + 1, SPAN)
                ],
                axis=1,
            )
        )
        for pair in range(HEADS_STEP // 2):
            here = pl.ds(pl.multiple_of(step * group_cols + pair * LANES, LANES), LANES)
            taps_at = pl.multiple_of(meta_ref[0] * half + step * group_cols + pair * LANES, LANES)
            taps_at = pl.ds(taps_at, LANES)
            one, two = 2 * pair, 2 * pair + 1
            x_conv = causal_conv(projected_ref[every, here].astype(F32), taps_ref[:, taps_at])
            head = group_here * HEADS_STEP + one
            skip = jnp.where(left[:1], skip_ref[head], skip_ref[head + 1])
            state = jnp.zeros((LANES, state_dim), F32)
            for block in range(blocks):
                at = slice(block * SPAN, (block + 1) * SPAN)
                x_here = x_conv[at]
                cb = cb_scr[block]
                d_one, d_two = decays[at, one : one + 1], decays[at, two : two + 1]
                mix_one = cb * jnp.exp2(jnp.minimum(d_one - rows_of[one : one + 1, at], 0.0)) * delta_of[one : one + 1, at]
                mix_two = cb * jnp.exp2(jnp.minimum(d_two - rows_of[two : two + 1, at], 0.0)) * delta_of[two : two + 1, at]
                decay = jnp.where(left, d_one, d_two)
                short = x_here.astype(BF)
                zero = jnp.zeros_like(short)
                mixing = jnp.concatenate([mix_one.astype(BF), mix_two.astype(BF)], axis=1)
                spread = jnp.concatenate(
                    [jnp.where(left, short, zero), jnp.where(left, zero, short)], axis=0
                )
                out = jnp.dot(mixing, spread, preferred_element_type=F32)
                if block:
                    out = out + jnp.exp2(decay) * lax.dot_general(
                        c_scr[at],
                        state.astype(BF),
                        (((1,), (1,)), ((), ())),
                        preferred_element_type=F32,
                    )
                weighted = jnp.transpose(short).astype(F32) * jnp.where(
                    top, weight_of[one : one + 1, at], weight_of[two : two + 1, at]
                )
                fresh = jnp.dot(weighted.astype(BF), b_scr[at], preferred_element_type=F32)
                if block:
                    fade = jnp.where(
                        top,
                        jnp.exp2(d_one[SPAN - 1 : SPAN]),
                        jnp.exp2(d_two[SPAN - 1 : SPAN]),
                    )
                    fresh = fade * state + fresh
                state = fresh
                scanned_ref[at, here] = out + skip * x_here
            state_ref[here, :] = state
        return carry

    lax.fori_loop(0, groups // 2, group, 0)


def scan(which, meta, shard, projected, conv_weight, bias, log_rate, skip, width):
    seq, total = projected.shape[0] // 2, projected.shape[1]
    state_dim = width // 2
    half = total - width - LANES
    groups = 2 * half // (HEADS_STEP * LANES // 2)
    scalars = pl.BlockSpec(memory_space=pltpu.SMEM)
    whole = pl.BlockSpec(memory_space=pltpu.VMEM)
    return pl.pallas_call(
        functools.partial(scan_kernel, which),
        in_specs=[scalars] + [whole] * 5 + [scalars],
        out_specs=[whole] * 2,
        out_shape=[
            jax.ShapeDtypeStruct((seq, half), F32),
            jax.ShapeDtypeStruct((half, state_dim), F32),
        ],
        scratch_shapes=[
            pltpu.VMEM((groups, seq, HEADS_STEP), F32),
            pltpu.VMEM((groups, HEADS_STEP, seq), F32),
            pltpu.VMEM((groups, HEADS_STEP, seq), F32),
            pltpu.VMEM((seq, state_dim), BF),
            pltpu.VMEM((seq, state_dim), BF),
            pltpu.VMEM((seq // SPAN, SPAN, SPAN), F32),
        ],
        compiler_params=pltpu.CompilerParams(vmem_limit_bytes=16 << 20),
        cost_estimate=pl.CostEstimate(
            flops=2 * half * seq * 640, transcendentals=half * seq * 6, bytes_accessed=5 << 20
        ),
        name="scan",
    )(meta, shard, projected, conv_weight, bias, log_rate, skip)


def shards_kernel(
    meta_ref, lengths_ref, input_ref, state_ref, step_ref, gate_ref, out_ref, kept_ref, sent_ref
):
    rows, half = input_ref.shape[0], input_ref.shape[1] // 2
    width, heads = state_ref.shape[1], step_ref.shape[1]
    length = lengths_ref[meta_ref[1]]
    row = lax.broadcasted_iota(jnp.int32, (rows, LANES), 0)
    lane = lax.broadcasted_iota(jnp.int32, (rows, LANES), 1)
    coded = jnp.where(lane == heads, length >> 4, jnp.where(lane == heads + 1, length & 15, 0))
    coded = jnp.where(row == 0, coded, 0).astype(F32).astype(BF)
    for ref, core in ((kept_ref, meta_ref[0]), (sent_ref, 1 - meta_ref[0])):
        at = pl.ds(pl.multiple_of(core * half, half), half)
        ref[:, :half] = input_ref[:, at].astype(BF)
        ref[:, half : half + width] = state_ref[...].astype(BF)
        ref[:, half + width : half + width + LANES] = coded
        ref[:, half + width : half + width + heads] = step_ref[...].astype(BF)
        start = half + width + LANES
        ref[:, start : start + half] = gate_ref[:, at].astype(BF)
        ref[:, start + half :] = out_ref[:, at].astype(BF)


def shards(meta, lengths, inputs, state, step, gate, out):
    rows, inner = inputs.shape
    total = 3 * (inner // 2) + state.shape[1] + LANES
    scalars = pl.BlockSpec(memory_space=pltpu.SMEM)
    whole = pl.BlockSpec(memory_space=pltpu.VMEM)
    return pl.pallas_call(
        shards_kernel,
        in_specs=[scalars] * 2 + [whole] * 5,
        out_specs=[whole] * 2,
        out_shape=[jax.ShapeDtypeStruct((rows, total), BF)] * 2,
        name="shards",
    )(meta, lengths, inputs, state, step, gate, out)


def join_kernel(start, held_ref, moved_ref, out_ref):
    rows, cols = held_ref.shape[0], slice(start, start + out_ref.shape[1])
    out_ref[:rows] = held_ref[:, cols]
    out_ref[rows:] = moved_ref[:, cols]


def join(held, moved, start, stop):
    rows, width = held.shape[0], stop - start
    whole = pl.BlockSpec(memory_space=pltpu.VMEM)
    return pl.pallas_call(
        functools.partial(join_kernel, start),
        in_specs=[whole] * 2,
        out_specs=whole,
        out_shape=jax.ShapeDtypeStruct((2 * rows, width), BF),
        compiler_params=pltpu.CompilerParams(vmem_limit_bytes=6 << 20),
        cost_estimate=pl.CostEstimate(
            flops=0, transcendentals=0, bytes_accessed=8 * rows * width
        ),
        name="join",
    )(held, moved)


def project_kernel(first, tokens_ref, *refs):
    begin_ref, pieces, out_ref = refs[0], refs[:-1], refs[-1]
    if not first:
        pieces = pieces[1:]
    depth, total = pieces[0].shape
    tokens = jnp.concatenate(
        [
            tokens_ref[:, at : at + depth]
            for at in range(0 if first else depth, tokens_ref.shape[1], 2 * depth)
        ],
        axis=1,
    )
    tile = total // 5
    for at in range(0, total, tile):
        cols = slice(at, at + tile)
        weight = jnp.concatenate([piece[:, cols] for piece in pieces], axis=0)
        part = jnp.dot(tokens, weight, preferred_element_type=F32)
        if not first:
            part = part + begin_ref[:, cols]
        out_ref[:, cols] = part.astype(out_ref.dtype)


def project(tokens, pieces, begun=None):
    rows, model = tokens.shape
    depth, total = pieces[0].shape
    first = begun is None
    whole = pl.BlockSpec(memory_space=pltpu.VMEM)
    begun = () if first else (begun,)
    return pl.pallas_call(
        functools.partial(project_kernel, first),
        in_specs=[whole] * (1 + len(begun) + len(pieces)),
        out_specs=whole,
        out_shape=jax.ShapeDtypeStruct((rows, total), F32 if first else BF),
        compiler_params=pltpu.CompilerParams(vmem_limit_bytes=16 << 20),
        cost_estimate=pl.CostEstimate(
            flops=rows * model * total, transcendentals=0, bytes_accessed=10 << 20
        ),
        name="project",
    )(tokens, *begun, *pieces)


def share_kernel(which, count, meta_ref, places_ref, tokens_ref, scanned_ref, gain_ref, *refs):
    pieces, states, (share_ref, square_ref, *rest) = refs[:count], (), refs[count:]
    copies = []
    if which == 0:
        states, (share_ref, square_ref, state_out_ref, gated_scr, sems) = (
            refs[count : count + 2],
            refs[count + 2 :],
        )
        core, rows_half = meta_ref[0], states[0].shape[0]
        for index, source in enumerate(states):
            place = (core if index == 0 else 1 - core) * rows_half
            place = pl.ds(pl.multiple_of(place, rows_half), rows_half)
            copies.append(pltpu.make_async_copy(source, state_out_ref.at[place], sems.at[index]))
            copies[-1].start()
    else:
        (gated_scr,) = rest
    seq, half = scanned_ref.shape
    rows = slice(which * seq, (which + 1) * seq)
    tile = half // 3
    square_ref[...] = jnp.zeros_like(square_ref)
    for at in range(0, half, tile):
        cols = slice(at, at + tile)
        weight = jnp.concatenate([piece[:, cols] for piece in pieces], axis=0)
        gate = jnp.dot(tokens_ref[rows], weight, preferred_element_type=F32).astype(BF)
        gated = scanned_ref[:, cols] * silu(gate.astype(F32))
        gain_at = pl.multiple_of(meta_ref[0] * half + at, LANES)
        gated_scr[:, cols] = (gated * gain_ref[:, pl.ds(gain_at, tile)]).astype(BF)
        square = gated * gated
        for lane in range(0, tile, LANES):
            square_ref[...] += square[:, lane : lane + LANES]
    steps = 4
    depth = pieces[0].shape[0] // steps
    each = depth // BLOCK_ROWS
    for step in range(steps):
        weight = jnp.concatenate(
            [piece[step * depth : (step + 1) * depth, half:] for piece in pieces], axis=0
        )
        total = lax.dot_general(
            weight, gated_scr[...], (((1,), (1,)), ((), ())), preferred_element_type=F32
        )
        for index in range(len(pieces)):
            for block in range(each):
                at = (index * each + block) * BLOCK_ROWS
                place = places_ref[(index * steps + step) * each + block]
                share_ref[pl.ds(pl.multiple_of(place, BLOCK_ROWS), BLOCK_ROWS), :] = total[
                    at : at + BLOCK_ROWS
                ]
    for copy in copies:
        copy.wait()


def out_share(which, meta, places, tokens, scanned, gain, pieces, states=()):
    seq, half = scanned.shape
    model = tokens.shape[1]
    scalars = pl.BlockSpec(memory_space=pltpu.SMEM)
    whole = pl.BlockSpec(memory_space=pltpu.VMEM)
    anywhere = pl.BlockSpec(memory_space=pl.ANY)
    joined_state = [jax.ShapeDtypeStruct((2 * x.shape[0], x.shape[1]), F32) for x in states[:1]]
    return pl.pallas_call(
        functools.partial(share_kernel, which, len(pieces)),
        in_specs=[scalars] * 2 + [whole] * (3 + len(pieces)) + [anywhere] * len(states),
        out_specs=[whole] * 2 + [anywhere] * len(joined_state),
        out_shape=[
            jax.ShapeDtypeStruct((model, seq), F32),
            jax.ShapeDtypeStruct((seq, LANES), F32),
        ]
        + joined_state,
        scratch_shapes=[pltpu.VMEM((seq, half), BF)]
        + [pltpu.SemaphoreType.DMA((2,))] * len(joined_state),
        compiler_params=pltpu.CompilerParams(vmem_limit_bytes=16 << 20),
        cost_estimate=pl.CostEstimate(
            flops=4 * seq * half * model, transcendentals=seq * half, bytes_accessed=16 << 20
        ),
        name="out_share",
    )(meta, places, tokens, scanned, gain, *pieces, *states)


def mix_kernel(shard_ref, mine_ref, other_ref, sq_mine, sq_other, pick_ref, out_ref):
    seq, model = out_ref.shape
    inner = 2 * model
    squares = jnp.transpose(sq_mine[...] + sq_other[...])
    mean = jnp.sum(squares, axis=0, keepdims=True) / inner
    live = lax.broadcasted_iota(jnp.int32, (1, seq), 1).astype(F32) < length_of(shard_ref, HEADS)
    scale = jnp.where(live, lax.rsqrt(mean + EPSILON), 0.0)
    tile = pick_ref.shape[0]
    for at in range(0, model, tile):
        rows = slice(at, at + tile)
        short = ((mine_ref[rows] + other_ref[rows]) * scale).astype(BF)
        out_ref[:, rows] = lax.dot_general(
            short, pick_ref[...], (((0,), (0,)), ((), ())), preferred_element_type=F32
        ).astype(BF)


def mix(shard, cut, mine, other, sq_mine, sq_other):
    model, seq = mine.shape
    tile = model // 4
    column = jnp.arange(tile, dtype=jnp.int32)
    chip, rest = column // (2 * SHARD_ROWS), column % (2 * SHARD_ROWS)
    target = rest // SHARD_ROWS * (tile // 2) + chip * SHARD_ROWS + rest % SHARD_ROWS
    pick = (target[:, None] == column[None]).astype(BF)
    whole = pl.BlockSpec(memory_space=pltpu.VMEM)
    return pl.pallas_call(
        mix_kernel,
        grid=(1,),
        in_specs=[pl.BlockSpec((shard.shape[0], LANES), lambda i: (0, cut // LANES - 1))]
        + [whole] * 5,
        out_specs=whole,
        out_shape=jax.ShapeDtypeStruct((seq, model), BF),
        compiler_params=pltpu.CompilerParams(vmem_limit_bytes=16 << 20),
        cost_estimate=pl.CostEstimate(
            flops=2 * seq * tile * model, transcendentals=0, bytes_accessed=8 << 20
        ),
        name="mix",
    )(shard, mine, other, sq_mine, sq_other, pick)


EVERYONE = ("req", "unit")
DEVICES = 128
CORE = 16
SHARD_ROWS = 12
COLOURS = 3
BLOCK_ROWS = 8
LINKS = (1 << 2, 1, 1 << 5, 3 << 2, 3, 3 << 5)


def link_of(colour, core, step):
    return LINKS[(colour + 3 * core - step) % 6]


def hop(value, mask_of):
    return lax.ppermute(
        value, EVERYONE, [(d, d ^ mask_of((d // CORE) % 2)) for d in range(DEVICES)]
    )


def swap(value):
    return hop(value, lambda core: CORE)


def moved_over(held, step):
    return [hop(piece, lambda core, c=c: link_of(c, core, step)) for c, piece in enumerate(held)]


def joined(held, moved):
    return [
        lax.optimization_barrier(jnp.concatenate([h, m], axis=0)) for h, m in zip(held, moved)
    ]


def gathered_chip(me, core, colour, block):
    mask = jnp.zeros_like(block)
    for step in range(6):
        link = jnp.zeros_like(block)
        for c in range(COLOURS):
            here = jnp.where(core == 0, link_of(c, 0, step), link_of(c, 1, step))
            link = jnp.where(colour == c, here, link)
        mask = mask ^ (((block >> step) & 1) * link)
    return (me ^ mask) & ~CORE


def row_sources(me, core, model):
    row = jnp.arange(model, dtype=jnp.int32)
    colour, block = row // (model // COLOURS), row // BLOCK_ROWS % 64
    local = colour * BLOCK_ROWS + row % BLOCK_ROWS
    upper = (local >= SHARD_ROWS).astype(jnp.int32)
    device = gathered_chip(me, core, colour, block) + CORE * upper
    return device * SHARD_ROWS + local - SHARD_ROWS * upper


def row_places(me, core):
    index = jnp.arange(COLOURS * 64, dtype=jnp.int32)
    chip = gathered_chip(me, core, index // 64, index % 64)
    chip = (chip >> 5) * CORE + (chip & (CORE - 1))
    return chip * 2 * SHARD_ROWS + index // 64 * BLOCK_ROWS


def body(
    tokens,
    lengths,
    gate_proj,
    input_proj,
    state_proj,
    step_proj,
    out_proj,
    conv_weight,
    step_bias,
    log_rate,
    skip_gain,
    norm_gain,
):
    unit_id = lax.axis_index("unit")
    me = lax.axis_index(EVERYONE).astype(jnp.int32)
    core = (me // CORE) % 2
    first_core = core == 0
    seq_len, model_dim = tokens.shape[1:]
    inner_dim = gate_proj.shape[1]
    head_count = log_rate.shape[0]
    head_dim = inner_dim // head_count
    width = state_proj.shape[1]
    half = inner_dim // 2

    cut = half + width + LANES
    meta = jnp.stack([core, unit_id])
    kept, sent = shards(
        meta, lengths, input_proj, state_proj, step_proj, gate_proj, out_proj
    )
    sent, unit_id = lax.optimization_barrier((sent, unit_id))
    received = swap(sent)
    pair = jnp.concatenate(
        [jnp.where(first_core, kept, received), jnp.where(first_core, received, kept)], axis=0
    )
    held = [pair[8 * c : 8 * c + 8] for c in range(COLOURS)]
    for step in range(3):
        held = joined(held, moved_over(held, step))
    held = [join(h, m, 0, cut + 2 * half) for h, m in zip(held, moved_over(held, 3))]
    moved = moved_over(held, 4)

    own = lax.dynamic_index_in_dim(tokens, unit_id, 0, keepdims=False)
    both = jnp.concatenate([own, swap(own)], axis=0)
    pick = jnp.arange(model_dim, dtype=jnp.int32)[:, None] == row_sources(me, core, model_dim)[None]
    both = jnp.dot(both, pick.astype(BF), preferred_element_type=F32).astype(BF)
    moved[0], both, places = lax.optimization_barrier((moved[0], both, row_places(me, core)))
    early = [join(h, m, 0, cut) for h, m in zip(held, moved)]
    early[2], held = lax.optimization_barrier((early[2], held))
    late = [join(h, m, cut, cut + 2 * half) for h, m in zip(held, moved)]
    moved = moved_over(early, 5)
    late[2], begun = lax.optimization_barrier((late[2], project(both, early)))
    late = [piece for two in zip(late, moved_over(late, 5)) for piece in two]

    projected = project(both, moved, begun)
    inputs = (projected, conv_weight, step_bias[None], log_rate[None], skip_gain, width)
    scanned_other, state_sent = scan(1, meta, received, *inputs)
    state_other = swap(state_sent)
    scanned, state = scan(0, meta, kept, *inputs)
    scanned_other, scanned, state_other = lax.optimization_barrier(
        (scanned_other, scanned, state_other)
    )
    shared = (meta, places, both)
    sent, square_sent = out_share(1, *shared, scanned_other, norm_gain[None], late)
    other, square_other = swap(sent), swap(square_sent)
    mine, square, state = out_share(
        0, *shared, scanned, norm_gain[None], late, (state, state_other)
    )
    mixed = mix(kept, cut, mine, other, square, square_other)
    return (mixed[None], state.reshape(1, head_count, head_dim, width // 2))


def solution(mesh):
    placed = (
        P("req", None, None),
        P("req"),
        P(("req", "unit"), None),
        P(("req", "unit"), None),
        P(("req", "unit"), None),
        P(("req", "unit"), None),
        P(("req", "unit"), None),
        P(),
        P(),
        P(),
        P(),
        P(),
    )
    return jax.shard_map(
        body,
        mesh=mesh,
        in_specs=placed,
        out_specs=(P(("req", "unit"), None, None), P(("req", "unit"), None, None, None)),
        check_vma=False,
    )
```

```python
import functools

import jax
import jax.numpy as jnp
from jax import lax
from jax.experimental import pallas as pl
from jax.experimental.pallas import tpu as pltpu
from jax.sharding import PartitionSpec as P

SPAN = 128
LANES = 128
HEADS = 48
HEADS_STEP = 8
EPSILON = 1e-05
LOG2E = 1.4426950408889634
BF = jnp.bfloat16
F32 = jnp.float32


def length_of(shard_ref, heads, start=0):
    coded = shard_ref[:1, start : start + LANES].astype(F32)
    return 16.0 * coded[:, heads : heads + 1] + coded[:, heads + 1 : heads + 2]


def silu(v):
    h = 0.5 * v
    return h + h * jnp.tanh(h)


def causal_conv(values, taps):
    rows = lax.broadcasted_iota(jnp.int32, (BLOCK_ROWS, values.shape[1]), 0)
    count = taps.shape[0]
    total = values * taps[count - 1 : count]
    for back in range(1, count):
        moved = pltpu.roll(values, back, 0)
        moved = jnp.concatenate(
            [jnp.where(rows >= back, moved[:BLOCK_ROWS], 0.0), moved[BLOCK_ROWS:]], axis=0
        )
        total = total + moved * taps[count - 1 - back : count - back]
    return silu(total)


def scan_kernel(
    which,
    meta_ref,
    shard_ref,
    projected_ref,
    taps_ref,
    bias_ref,
    log_rate_ref,
    skip_ref,
    scanned_ref,
    state_ref,
    decay_col,
    delta_row,
    decay_row,
    b_scr,
    c_scr,
    cb_scr,
):
    seq, half = scanned_ref.shape
    state_dim = state_ref.shape[1]
    groups = decay_col.shape[0]
    group_cols = HEADS_STEP * LANES // 2
    blocks = seq // SPAN
    every = slice(which * seq, (which + 1) * seq)
    position = lax.broadcasted_iota(jnp.int32, (seq, LANES), 0)
    lower = lax.broadcasted_iota(jnp.int32, (SPAN, SPAN), 0) >= lax.broadcasted_iota(
        jnp.int32, (SPAN, SPAN), 1
    )
    side = projected_ref[every, half:].astype(F32)
    conv = causal_conv(side[:, : 2 * state_dim], taps_ref[:, 2 * half :])
    b_short = conv[:, :state_dim].astype(BF)
    c_short = conv[:, state_dim:].astype(BF)
    b_scr[...] = b_short
    c_scr[...] = c_short
    for block in range(blocks):
        at = slice(block * SPAN, (block + 1) * SPAN)
        cb_scr[block] = lax.dot_general(
            c_short[at], b_short[at], (((1,), (1,)), ((), ())), preferred_element_type=F32
        )
        cb_scr[block] = jnp.where(lower, cb_scr[block], 0.0)
    spare = jnp.zeros((1, LANES - bias_ref.shape[1]), F32)
    raw = side[:, 2 * state_dim :] + jnp.concatenate([bias_ref[...], spare], axis=1)
    live = (position.astype(F32) < length_of(
            shard_ref, bias_ref.shape[1], half + 2 * state_dim
        )).astype(F32)
    delta = (jnp.maximum(raw, 0.0) + jnp.log1p(jnp.exp(-jnp.abs(raw)))) * live
    total = delta * (-LOG2E * jnp.exp(jnp.concatenate([log_rate_ref[...], spare], axis=1)))
    within = position % SPAN
    reach = 1
    while reach < SPAN:
        total = total + jnp.where(within >= reach, pltpu.roll(total, reach, 0), 0.0)
        reach *= 2
    turned = jnp.transpose(total)
    turned_delta = jnp.transpose(delta)
    for group in range(groups):
        at = slice(group * HEADS_STEP, (group + 1) * HEADS_STEP)
        decay_col[group] = total[:, at]
        delta_row[group] = turned_delta[at]
        decay_row[group] = turned[at]

    left = lax.broadcasted_iota(jnp.int32, (SPAN, LANES), 1) < LANES // 2
    top = lax.broadcasted_iota(jnp.int32, (LANES, state_dim), 0) < LANES // 2

    def group(step, carry):
        group_here = meta_ref[0] * (groups // 2) + step
        decays = decay_col[group_here]
        delta_of = delta_row[group_here]
        rows_of = decay_row[group_here]
        weight_of = delta_of * jnp.exp2(
            jnp.concatenate(
                [
                    rows_of[:, end - 1 : end] - rows_of[:, end - SPAN : end]
                    for end in range(SPAN, seq + 1, SPAN)
                ],
                axis=1,
            )
        )
        for pair in range(HEADS_STEP // 2):
            here = pl.ds(pl.multiple_of(step * group_cols + pair * LANES, LANES), LANES)
            taps_at = pl.multiple_of(meta_ref[0] * half + step * group_cols + pair * LANES, LANES)
            taps_at = pl.ds(taps_at, LANES)
            one, two = 2 * pair, 2 * pair + 1
            x_conv = causal_conv(projected_ref[every, here].astype(F32), taps_ref[:, taps_at])
            head = group_here * HEADS_STEP + one
            skip = jnp.where(left[:1], skip_ref[head], skip_ref[head + 1])
            state = jnp.zeros((LANES, state_dim), F32)
            for block in range(blocks):
                at = slice(block * SPAN, (block + 1) * SPAN)
                x_here = x_conv[at]
                cb = cb_scr[block]
                d_one, d_two = decays[at, one : one + 1], decays[at, two : two + 1]
                mix_one = cb * jnp.exp2(jnp.minimum(d_one - rows_of[one : one + 1, at], 0.0)) * delta_of[one : one + 1, at]
                mix_two = cb * jnp.exp2(jnp.minimum(d_two - rows_of[two : two + 1, at], 0.0)) * delta_of[two : two + 1, at]
                decay = jnp.where(left, d_one, d_two)
                short = x_here.astype(BF)
                zero = jnp.zeros_like(short)
                mixing = jnp.concatenate([mix_one.astype(BF), mix_two.astype(BF)], axis=1)
                spread = jnp.concatenate(
                    [jnp.where(left, short, zero), jnp.where(left, zero, short)], axis=0
                )
                out = jnp.dot(mixing, spread, preferred_element_type=F32)
                if block:
                    out = out + jnp.exp2(decay) * lax.dot_general(
                        c_scr[at],
                        state.astype(BF),
                        (((1,), (1,)), ((), ())),
                        preferred_element_type=F32,
                    )
                weighted = jnp.transpose(short).astype(F32) * jnp.where(
                    top, weight_of[one : one + 1, at], weight_of[two : two + 1, at]
                )
                fresh = jnp.dot(weighted.astype(BF), b_scr[at], preferred_element_type=F32)
                if block:
                    fade = jnp.where(
                        top,
                        jnp.exp2(d_one[SPAN - 1 : SPAN]),
                        jnp.exp2(d_two[SPAN - 1 : SPAN]),
                    )
                    fresh = fade * state + fresh
                state = fresh
                scanned_ref[at, here] = out + skip * x_here
            state_ref[here, :] = state
        return carry

    lax.fori_loop(0, groups // 2, group, 0)


def scan(which, meta, shard, projected, conv_weight, bias, log_rate, skip, width):
    seq, total = projected.shape[0] // 2, projected.shape[1]
    state_dim = width // 2
    half = total - width - LANES
    groups = 2 * half // (HEADS_STEP * LANES // 2)
    scalars = pl.BlockSpec(memory_space=pltpu.SMEM)
    whole = pl.BlockSpec(memory_space=pltpu.VMEM)
    return pl.pallas_call(
        functools.partial(scan_kernel, which),
        in_specs=[scalars] + [whole] * 5 + [scalars],
        out_specs=[whole] * 2,
        out_shape=[
            jax.ShapeDtypeStruct((seq, half), F32),
            jax.ShapeDtypeStruct((half, state_dim), F32),
        ],
        scratch_shapes=[
            pltpu.VMEM((groups, seq, HEADS_STEP), F32),
            pltpu.VMEM((groups, HEADS_STEP, seq), F32),
            pltpu.VMEM((groups, HEADS_STEP, seq), F32),
            pltpu.VMEM((seq, state_dim), BF),
            pltpu.VMEM((seq, state_dim), BF),
            pltpu.VMEM((seq // SPAN, SPAN, SPAN), F32),
        ],
        compiler_params=pltpu.CompilerParams(vmem_limit_bytes=16 << 20),
        cost_estimate=pl.CostEstimate(
            flops=2 * half * seq * 640, transcendentals=half * seq * 6, bytes_accessed=5 << 20
        ),
        name="scan",
    )(meta, shard, projected, conv_weight, bias, log_rate, skip)


def shards_kernel(
    meta_ref, lengths_ref, input_ref, state_ref, step_ref, gate_ref, out_ref, kept_ref, sent_ref
):
    rows, half = input_ref.shape[0], input_ref.shape[1] // 2
    width, heads = state_ref.shape[1], step_ref.shape[1]
    length = lengths_ref[meta_ref[1]]
    row = lax.broadcasted_iota(jnp.int32, (rows, LANES), 0)
    lane = lax.broadcasted_iota(jnp.int32, (rows, LANES), 1)
    coded = jnp.where(lane == heads, length >> 4, jnp.where(lane == heads + 1, length & 15, 0))
    coded = jnp.where(row == 0, coded, 0).astype(F32).astype(BF)
    for ref, core in ((kept_ref, meta_ref[0]), (sent_ref, 1 - meta_ref[0])):
        at = pl.ds(pl.multiple_of(core * half, half), half)
        ref[:, :half] = input_ref[:, at].astype(BF)
        ref[:, half : half + width] = state_ref[...].astype(BF)
        ref[:, half + width : half + width + LANES] = coded
        ref[:, half + width : half + width + heads] = step_ref[...].astype(BF)
        start = half + width + LANES
        ref[:, start : start + half] = gate_ref[:, at].astype(BF)
        ref[:, start + half :] = out_ref[:, at].astype(BF)


def shards(meta, lengths, inputs, state, step, gate, out):
    rows, inner = inputs.shape
    total = 3 * (inner // 2) + state.shape[1] + LANES
    scalars = pl.BlockSpec(memory_space=pltpu.SMEM)
    whole = pl.BlockSpec(memory_space=pltpu.VMEM)
    return pl.pallas_call(
        shards_kernel,
        in_specs=[scalars] * 2 + [whole] * 5,
        out_specs=[whole] * 2,
        out_shape=[jax.ShapeDtypeStruct((rows, total), BF)] * 2,
        name="shards",
    )(meta, lengths, inputs, state, step, gate, out)


def join_kernel(held_ref, moved_ref, *outs):
    rows, start = held_ref.shape[0], 0
    for out_ref in outs:
        cols = slice(start, start + out_ref.shape[1])
        out_ref[:rows] = held_ref[:, cols]
        out_ref[rows:] = moved_ref[:, cols]
        start += out_ref.shape[1]


def join(held, moved, *widths):
    rows, total = held.shape
    whole = pl.BlockSpec(memory_space=pltpu.VMEM)
    return pl.pallas_call(
        join_kernel,
        in_specs=[whole] * 2,
        out_specs=[whole] * len(widths),
        out_shape=[jax.ShapeDtypeStruct((2 * rows, width), BF) for width in widths],
        compiler_params=pltpu.CompilerParams(vmem_limit_bytes=6 << 20),
        cost_estimate=pl.CostEstimate(
            flops=0, transcendentals=0, bytes_accessed=8 * rows * total
        ),
        name="join",
    )(held, moved)


def project_kernel(first, tokens_ref, *refs):
    begin_ref, pieces, out_ref = refs[0], refs[:-1], refs[-1]
    if not first:
        pieces = pieces[1:]
    depth, total = pieces[0].shape
    tokens = jnp.concatenate(
        [
            tokens_ref[:, at : at + depth]
            for at in range(0 if first else depth, tokens_ref.shape[1], 2 * depth)
        ],
        axis=1,
    )
    tile = total // 5
    for at in range(0, total, tile):
        cols = slice(at, at + tile)
        weight = jnp.concatenate([piece[:, cols] for piece in pieces], axis=0)
        part = jnp.dot(tokens, weight, preferred_element_type=F32)
        if not first:
            part = part + begin_ref[:, cols]
        out_ref[:, cols] = part.astype(out_ref.dtype)


def project(tokens, pieces, begun=None):
    rows, model = tokens.shape
    depth, total = pieces[0].shape
    first = begun is None
    whole = pl.BlockSpec(memory_space=pltpu.VMEM)
    begun = () if first else (begun,)
    return pl.pallas_call(
        functools.partial(project_kernel, first),
        in_specs=[whole] * (1 + len(begun) + len(pieces)),
        out_specs=whole,
        out_shape=jax.ShapeDtypeStruct((rows, total), F32 if first else BF),
        compiler_params=pltpu.CompilerParams(vmem_limit_bytes=16 << 20),
        cost_estimate=pl.CostEstimate(
            flops=rows * model * total, transcendentals=0, bytes_accessed=10 << 20
        ),
        name="project",
    )(tokens, *begun, *pieces)


def share_kernel(which, meta_ref, places_ref, tokens_ref, scanned_ref, gain_ref, *refs):
    pieces, (share_ref, square_ref, gated_scr) = refs[:-3], refs[-3:]
    seq, half = scanned_ref.shape
    rows = slice(which * seq, (which + 1) * seq)
    tile = half // 3
    square_ref[...] = jnp.zeros_like(square_ref)
    for at in range(0, half, tile):
        cols = slice(at, at + tile)
        weight = jnp.concatenate([piece[:, cols] for piece in pieces], axis=0)
        gate = jnp.dot(tokens_ref[rows], weight, preferred_element_type=F32).astype(BF)
        gated = scanned_ref[:, cols] * silu(gate.astype(F32))
        gain_at = pl.multiple_of(meta_ref[0] * half + at, LANES)
        gated_scr[:, cols] = (gated * gain_ref[:, pl.ds(gain_at, tile)]).astype(BF)
        square = gated * gated
        for lane in range(0, tile, LANES):
            square_ref[...] += square[:, lane : lane + LANES]
    steps = 4
    depth = pieces[0].shape[0] // steps
    each = depth // BLOCK_ROWS
    for step in range(steps):
        weight = jnp.concatenate(
            [piece[step * depth : (step + 1) * depth, half:] for piece in pieces], axis=0
        )
        total = lax.dot_general(
            weight, gated_scr[...], (((1,), (1,)), ((), ())), preferred_element_type=F32
        )
        for index in range(len(pieces)):
            for block in range(each):
                at = (index * each + block) * BLOCK_ROWS
                place = places_ref[(index * steps + step) * each + block]
                share_ref[pl.ds(pl.multiple_of(place, BLOCK_ROWS), BLOCK_ROWS), :] = total[
                    at : at + BLOCK_ROWS
                ]


def out_share(which, meta, places, tokens, scanned, gain, pieces):
    seq, half = scanned.shape
    model = tokens.shape[1]
    scalars = pl.BlockSpec(memory_space=pltpu.SMEM)
    whole = pl.BlockSpec(memory_space=pltpu.VMEM)
    return pl.pallas_call(
        functools.partial(share_kernel, which),
        in_specs=[scalars] * 2 + [whole] * (3 + len(pieces)),
        out_specs=[whole] * 2,
        out_shape=[
            jax.ShapeDtypeStruct((model, seq), F32),
            jax.ShapeDtypeStruct((seq, LANES), F32),
        ],
        scratch_shapes=[pltpu.VMEM((seq, half), BF)],
        compiler_params=pltpu.CompilerParams(vmem_limit_bytes=16 << 20),
        cost_estimate=pl.CostEstimate(
            flops=4 * seq * half * model, transcendentals=seq * half, bytes_accessed=16 << 20
        ),
        name="out_share",
    )(meta, places, tokens, scanned, gain, *pieces)


def mix_kernel(shard_ref, mine_ref, other_ref, sq_mine, sq_other, pick_ref, out_ref):
    seq, model = out_ref.shape
    inner = 2 * model
    squares = jnp.transpose(sq_mine[...] + sq_other[...])
    mean = jnp.sum(squares, axis=0, keepdims=True) / inner
    live = lax.broadcasted_iota(jnp.int32, (1, seq), 1).astype(F32) < length_of(shard_ref, HEADS)
    scale = jnp.where(live, lax.rsqrt(mean + EPSILON), 0.0)
    tile = pick_ref.shape[0]
    for at in range(0, model, tile):
        rows = slice(at, at + tile)
        short = ((mine_ref[rows] + other_ref[rows]) * scale).astype(BF)
        out_ref[:, rows] = lax.dot_general(
            short, pick_ref[...], (((0,), (0,)), ((), ())), preferred_element_type=F32
        ).astype(BF)


def mix(shard, cut, mine, other, sq_mine, sq_other):
    model, seq = mine.shape
    tile = model // 4
    column = jnp.arange(tile, dtype=jnp.int32)
    chip, rest = column // (2 * SHARD_ROWS), column % (2 * SHARD_ROWS)
    target = rest // SHARD_ROWS * (tile // 2) + chip * SHARD_ROWS + rest % SHARD_ROWS
    pick = (target[:, None] == column[None]).astype(BF)
    whole = pl.BlockSpec(memory_space=pltpu.VMEM)
    fixed = lambda i: (0, 0)
    return pl.pallas_call(
        mix_kernel,
        grid=(1,),
        in_specs=[pl.BlockSpec((shard.shape[0], LANES), lambda i: (0, cut // LANES - 1))]
        + [whole] * 5,
        out_specs=whole,
        out_shape=jax.ShapeDtypeStruct((seq, model), BF),
        compiler_params=pltpu.CompilerParams(vmem_limit_bytes=16 << 20),
        cost_estimate=pl.CostEstimate(
            flops=2 * seq * tile * model, transcendentals=0, bytes_accessed=8 << 20
        ),
        name="mix",
    )(shard, mine, other, sq_mine, sq_other, pick)


EVERYONE = ("req", "unit")
DEVICES = 128
CORE = 16
SHARD_ROWS = 12
COLOURS = 3
BLOCK_ROWS = 8
LINKS = (1 << 2, 1, 1 << 5, 3 << 2, 3, 3 << 5)


def link_of(colour, core, step):
    return LINKS[(colour + 3 * core - step) % 6]


def hop(value, mask_of):
    return lax.ppermute(
        value, EVERYONE, [(d, d ^ mask_of((d // CORE) % 2)) for d in range(DEVICES)]
    )


def swap(value):
    return hop(value, lambda core: CORE)


def moved_over(held, step):
    return [hop(piece, lambda core, c=c: link_of(c, core, step)) for c, piece in enumerate(held)]


def joined(held, moved):
    return [
        lax.optimization_barrier(jnp.concatenate([h, m], axis=0)) for h, m in zip(held, moved)
    ]


def gathered_chip(me, core, colour, block):
    mask = jnp.zeros_like(block)
    for step in range(6):
        link = jnp.zeros_like(block)
        for c in range(COLOURS):
            here = jnp.where(core == 0, link_of(c, 0, step), link_of(c, 1, step))
            link = jnp.where(colour == c, here, link)
        mask = mask ^ (((block >> step) & 1) * link)
    return (me ^ mask) & ~CORE


def row_sources(me, core, model):
    row = jnp.arange(model, dtype=jnp.int32)
    colour, block = row // (model // COLOURS), row // BLOCK_ROWS % 64
    local = colour * BLOCK_ROWS + row % BLOCK_ROWS
    upper = (local >= SHARD_ROWS).astype(jnp.int32)
    device = gathered_chip(me, core, colour, block) + CORE * upper
    return device * SHARD_ROWS + local - SHARD_ROWS * upper


def row_places(me, core):
    index = jnp.arange(COLOURS * 64, dtype=jnp.int32)
    chip = gathered_chip(me, core, index // 64, index % 64)
    chip = (chip >> 5) * CORE + (chip & (CORE - 1))
    return chip * 2 * SHARD_ROWS + index // 64 * BLOCK_ROWS


def body(
    tokens,
    lengths,
    gate_proj,
    input_proj,
    state_proj,
    step_proj,
    out_proj,
    conv_weight,
    step_bias,
    log_rate,
    skip_gain,
    norm_gain,
):
    unit_id = lax.axis_index("unit")
    me = lax.axis_index(EVERYONE).astype(jnp.int32)
    core = (me // CORE) % 2
    first_core = core == 0
    seq_len, model_dim = tokens.shape[1:]
    inner_dim = gate_proj.shape[1]
    head_count = log_rate.shape[0]
    head_dim = inner_dim // head_count
    width = state_proj.shape[1]
    half = inner_dim // 2

    cut = half + width + LANES
    meta = jnp.stack([core, unit_id])
    kept, sent = shards(
        meta, lengths, input_proj, state_proj, step_proj, gate_proj, out_proj
    )
    sent, unit_id = lax.optimization_barrier((sent, unit_id))
    received = swap(sent)
    pair = jnp.concatenate(
        [jnp.where(first_core, kept, received), jnp.where(first_core, received, kept)], axis=0
    )
    held = [pair[8 * c : 8 * c + 8] for c in range(COLOURS)]
    for step in range(3):
        held = joined(held, moved_over(held, step))
    held = [join(h, m, cut + 2 * half)[0] for h, m in zip(held, moved_over(held, 3))]
    moved = moved_over(held, 4)

    own = lax.dynamic_index_in_dim(tokens, unit_id, 0, keepdims=False)
    both = jnp.concatenate([own, swap(own)], axis=0)
    pick = jnp.arange(model_dim, dtype=jnp.int32)[:, None] == row_sources(me, core, model_dim)[None]
    both = jnp.dot(both, pick.astype(BF), preferred_element_type=F32).astype(BF)
    moved[0], both, places = lax.optimization_barrier((moved[0], both, row_places(me, core)))
    early, late = zip(*[join(h, m, cut, 2 * half) for h, m in zip(held, moved)])
    late = list(late)
    early = list(early)
    early[1], late[0], late[2] = lax.optimization_barrier((early[1], late[0], late[2]))
    moved = moved_over(early, 5)
    begun = project(both, early)
    moved[0], begun = lax.optimization_barrier((moved[0], begun))
    moved[2], late[1] = lax.optimization_barrier((moved[2], late[1]))
    late = [piece for two in zip(late, moved_over(late, 5)) for piece in two]

    projected = project(both, moved, begun)
    inputs = (projected, conv_weight, step_bias[None], log_rate[None], skip_gain, width)
    scanned_other, state_sent = scan(1, meta, received, *inputs)
    state_other = swap(state_sent)
    scanned, state = scan(0, meta, kept, *inputs)
    scanned_other, scanned, state_other = lax.optimization_barrier(
        (scanned_other, scanned, state_other)
    )
    shared = (meta, places, both)
    sent, square_sent = out_share(1, *shared, scanned_other, norm_gain[None], late)
    other, square_other = swap(sent), swap(square_sent)
    mine, square = out_share(0, *shared, scanned, norm_gain[None], late)
    mixed = mix(kept, cut, mine, other, square, square_other)
    state = jnp.concatenate(
        [jnp.where(first_core, state, state_other), jnp.where(first_core, state_other, state)]
    )
    return (mixed[None], state.reshape(1, head_count, head_dim, width // 2))


def solution(mesh):
    placed = (
        P("req", None, None),
        P("req"),
        P(("req", "unit"), None),
        P(("req", "unit"), None),
        P(("req", "unit"), None),
        P(("req", "unit"), None),
        P(("req", "unit"), None),
        P(),
        P(),
        P(),
        P(),
        P(),
    )
    return jax.shard_map(
        body,
        mesh=mesh,
        in_specs=placed,
        out_specs=(P(("req", "unit"), None, None), P(("req", "unit"), None, None, None)),
        check_vma=False,
    )
```

```python
import functools

import jax
import jax.numpy as jnp
from jax import lax
from jax.experimental import pallas as pl
from jax.experimental.pallas import tpu as pltpu
from jax.sharding import PartitionSpec as P

SPAN = 128
LANES = 128
HEADS = 48
HEADS_STEP = 8
EPSILON = 1e-05
LOG2E = 1.4426950408889634
BF = jnp.bfloat16
F32 = jnp.float32


def length_of(shard_ref, heads, start=0):
    coded = shard_ref[:1, start : start + LANES].astype(F32)
    return 16.0 * coded[:, heads : heads + 1] + coded[:, heads + 1 : heads + 2]


def silu(v):
    h = 0.5 * v
    return h + h * jnp.tanh(h)


def causal_conv(values, taps):
    rows = lax.broadcasted_iota(jnp.int32, (BLOCK_ROWS, values.shape[1]), 0)
    count = taps.shape[0]
    total = values * taps[count - 1 : count]
    for back in range(1, count):
        moved = pltpu.roll(values, back, 0)
        moved = jnp.concatenate(
            [jnp.where(rows >= back, moved[:BLOCK_ROWS], 0.0), moved[BLOCK_ROWS:]], axis=0
        )
        total = total + moved * taps[count - 1 - back : count - back]
    return silu(total)


def scan_kernel(
    which,
    meta_ref,
    shard_ref,
    projected_ref,
    taps_ref,
    bias_ref,
    log_rate_ref,
    skip_ref,
    scanned_ref,
    state_ref,
    decay_col,
    delta_row,
    decay_row,
    b_scr,
    c_scr,
    cb_scr,
):
    seq, half = scanned_ref.shape
    state_dim = state_ref.shape[1]
    groups = decay_col.shape[0]
    group_cols = HEADS_STEP * LANES // 2
    blocks = seq // SPAN
    every = slice(which * seq, (which + 1) * seq)
    position = lax.broadcasted_iota(jnp.int32, (seq, LANES), 0)
    lower = lax.broadcasted_iota(jnp.int32, (SPAN, SPAN), 0) >= lax.broadcasted_iota(
        jnp.int32, (SPAN, SPAN), 1
    )
    side = projected_ref[every, half:].astype(F32)
    conv = causal_conv(side[:, : 2 * state_dim], taps_ref[:, 2 * half :])
    b_short = conv[:, :state_dim].astype(BF)
    c_short = conv[:, state_dim:].astype(BF)
    b_scr[...] = b_short
    c_scr[...] = c_short
    for block in range(blocks):
        at = slice(block * SPAN, (block + 1) * SPAN)
        cb_scr[block] = lax.dot_general(
            c_short[at], b_short[at], (((1,), (1,)), ((), ())), preferred_element_type=F32
        )
        cb_scr[block] = jnp.where(lower, cb_scr[block], 0.0)
    spare = jnp.zeros((1, LANES - bias_ref.shape[1]), F32)
    raw = side[:, 2 * state_dim :] + jnp.concatenate([bias_ref[...], spare], axis=1)
    live = (position.astype(F32) < length_of(
            shard_ref, bias_ref.shape[1], half + 2 * state_dim
        )).astype(F32)
    delta = (jnp.maximum(raw, 0.0) + jnp.log1p(jnp.exp(-jnp.abs(raw)))) * live
    total = delta * (-LOG2E * jnp.exp(jnp.concatenate([log_rate_ref[...], spare], axis=1)))
    within = position % SPAN
    reach = 1
    while reach < SPAN:
        total = total + jnp.where(within >= reach, pltpu.roll(total, reach, 0), 0.0)
        reach *= 2
    turned = jnp.transpose(total)
    turned_delta = jnp.transpose(delta)
    for group in range(groups):
        at = slice(group * HEADS_STEP, (group + 1) * HEADS_STEP)
        decay_col[group] = total[:, at]
        delta_row[group] = turned_delta[at]
        decay_row[group] = turned[at]

    left = lax.broadcasted_iota(jnp.int32, (SPAN, LANES), 1) < LANES // 2
    top = lax.broadcasted_iota(jnp.int32, (LANES, state_dim), 0) < LANES // 2

    def group(step, carry):
        group_here = meta_ref[0] * (groups // 2) + step
        decays = decay_col[group_here]
        delta_of = delta_row[group_here]
        rows_of = decay_row[group_here]
        weight_of = delta_of * jnp.exp2(
            jnp.concatenate(
                [
                    rows_of[:, end - 1 : end] - rows_of[:, end - SPAN : end]
                    for end in range(SPAN, seq + 1, SPAN)
                ],
                axis=1,
            )
        )
        for pair in range(HEADS_STEP // 2):
            here = pl.ds(pl.multiple_of(step * group_cols + pair * LANES, LANES), LANES)
            taps_at = pl.multiple_of(meta_ref[0] * half + step * group_cols + pair * LANES, LANES)
            taps_at = pl.ds(taps_at, LANES)
            one, two = 2 * pair, 2 * pair + 1
            x_conv = causal_conv(projected_ref[every, here].astype(F32), taps_ref[:, taps_at])
            head = group_here * HEADS_STEP + one
            skip = jnp.where(left[:1], skip_ref[head], skip_ref[head + 1])
            state = jnp.zeros((LANES, state_dim), F32)
            for block in range(blocks):
                at = slice(block * SPAN, (block + 1) * SPAN)
                x_here = x_conv[at]
                cb = cb_scr[block]
                d_one, d_two = decays[at, one : one + 1], decays[at, two : two + 1]
                mix_one = cb * jnp.exp2(jnp.minimum(d_one - rows_of[one : one + 1, at], 0.0)) * delta_of[one : one + 1, at]
                mix_two = cb * jnp.exp2(jnp.minimum(d_two - rows_of[two : two + 1, at], 0.0)) * delta_of[two : two + 1, at]
                decay = jnp.where(left, d_one, d_two)
                short = x_here.astype(BF)
                zero = jnp.zeros_like(short)
                mixing = jnp.concatenate([mix_one.astype(BF), mix_two.astype(BF)], axis=1)
                spread = jnp.concatenate(
                    [jnp.where(left, short, zero), jnp.where(left, zero, short)], axis=0
                )
                out = jnp.dot(mixing, spread, preferred_element_type=F32)
                if block:
                    out = out + jnp.exp2(decay) * lax.dot_general(
                        c_scr[at],
                        state.astype(BF),
                        (((1,), (1,)), ((), ())),
                        preferred_element_type=F32,
                    )
                weighted = jnp.transpose(short).astype(F32) * jnp.where(
                    top, weight_of[one : one + 1, at], weight_of[two : two + 1, at]
                )
                fresh = jnp.dot(weighted.astype(BF), b_scr[at], preferred_element_type=F32)
                if block:
                    fade = jnp.where(
                        top,
                        jnp.exp2(d_one[SPAN - 1 : SPAN]),
                        jnp.exp2(d_two[SPAN - 1 : SPAN]),
                    )
                    fresh = fade * state + fresh
                state = fresh
                scanned_ref[at, here] = out + skip * x_here
            state_ref[here, :] = state
        return carry

    lax.fori_loop(0, groups // 2, group, 0)


def scan(which, meta, shard, projected, conv_weight, bias, log_rate, skip, width):
    seq, total = projected.shape[0] // 2, projected.shape[1]
    state_dim = width // 2
    half = total - width - LANES
    groups = 2 * half // (HEADS_STEP * LANES // 2)
    scalars = pl.BlockSpec(memory_space=pltpu.SMEM)
    whole = pl.BlockSpec(memory_space=pltpu.VMEM)
    return pl.pallas_call(
        functools.partial(scan_kernel, which),
        in_specs=[scalars] + [whole] * 5 + [scalars],
        out_specs=[whole] * 2,
        out_shape=[
            jax.ShapeDtypeStruct((seq, half), F32),
            jax.ShapeDtypeStruct((half, state_dim), F32),
        ],
        scratch_shapes=[
            pltpu.VMEM((groups, seq, HEADS_STEP), F32),
            pltpu.VMEM((groups, HEADS_STEP, seq), F32),
            pltpu.VMEM((groups, HEADS_STEP, seq), F32),
            pltpu.VMEM((seq, state_dim), BF),
            pltpu.VMEM((seq, state_dim), BF),
            pltpu.VMEM((seq // SPAN, SPAN, SPAN), F32),
        ],
        compiler_params=pltpu.CompilerParams(vmem_limit_bytes=16 << 20),
        cost_estimate=pl.CostEstimate(
            flops=2 * half * seq * 640, transcendentals=half * seq * 6, bytes_accessed=5 << 20
        ),
        name="scan",
    )(meta, shard, projected, conv_weight, bias, log_rate, skip)


def shards_kernel(
    meta_ref, lengths_ref, input_ref, state_ref, step_ref, gate_ref, out_ref, kept_ref, sent_ref
):
    rows, half = input_ref.shape[0], input_ref.shape[1] // 2
    width, heads = state_ref.shape[1], step_ref.shape[1]
    length = lengths_ref[meta_ref[1]]
    row = lax.broadcasted_iota(jnp.int32, (rows, LANES), 0)
    lane = lax.broadcasted_iota(jnp.int32, (rows, LANES), 1)
    coded = jnp.where(lane == heads, length >> 4, jnp.where(lane == heads + 1, length & 15, 0))
    coded = jnp.where(row == 0, coded, 0).astype(F32).astype(BF)
    for ref, core in ((kept_ref, meta_ref[0]), (sent_ref, 1 - meta_ref[0])):
        at = pl.ds(pl.multiple_of(core * half, half), half)
        ref[:, :half] = input_ref[:, at].astype(BF)
        ref[:, half : half + width] = state_ref[...].astype(BF)
        ref[:, half + width : half + width + LANES] = coded
        ref[:, half + width : half + width + heads] = step_ref[...].astype(BF)
        start = half + width + LANES
        ref[:, start : start + half] = gate_ref[:, at].astype(BF)
        ref[:, start + half :] = out_ref[:, at].astype(BF)


def shards(meta, lengths, inputs, state, step, gate, out):
    rows, inner = inputs.shape
    total = 3 * (inner // 2) + state.shape[1] + LANES
    scalars = pl.BlockSpec(memory_space=pltpu.SMEM)
    whole = pl.BlockSpec(memory_space=pltpu.VMEM)
    return pl.pallas_call(
        shards_kernel,
        in_specs=[scalars] * 2 + [whole] * 5,
        out_specs=[whole] * 2,
        out_shape=[jax.ShapeDtypeStruct((rows, total), BF)] * 2,
        name="shards",
    )(meta, lengths, inputs, state, step, gate, out)


def join_kernel(held_ref, moved_ref, *outs):
    rows, start = held_ref.shape[0], 0
    for out_ref in outs:
        cols = slice(start, start + out_ref.shape[1])
        out_ref[:rows] = held_ref[:, cols]
        out_ref[rows:] = moved_ref[:, cols]
        start += out_ref.shape[1]


def join(held, moved, *widths):
    rows, total = held.shape
    whole = pl.BlockSpec(memory_space=pltpu.VMEM)
    return pl.pallas_call(
        join_kernel,
        in_specs=[whole] * 2,
        out_specs=[whole] * len(widths),
        out_shape=[jax.ShapeDtypeStruct((2 * rows, width), BF) for width in widths],
        compiler_params=pltpu.CompilerParams(vmem_limit_bytes=6 << 20),
        cost_estimate=pl.CostEstimate(
            flops=0, transcendentals=0, bytes_accessed=8 * rows * total
        ),
        name="join",
    )(held, moved)


def project_kernel(first, tokens_ref, *refs):
    begin_ref, pieces, out_ref = refs[0], refs[:-1], refs[-1]
    if not first:
        pieces = pieces[1:]
    depth, total = pieces[0].shape
    tokens = jnp.concatenate(
        [
            tokens_ref[:, at : at + depth]
            for at in range(0 if first else depth, tokens_ref.shape[1], 2 * depth)
        ],
        axis=1,
    )
    tile = total // 5
    for at in range(0, total, tile):
        cols = slice(at, at + tile)
        weight = jnp.concatenate([piece[:, cols] for piece in pieces], axis=0)
        part = jnp.dot(tokens, weight, preferred_element_type=F32)
        if not first:
            part = part + begin_ref[:, cols]
        out_ref[:, cols] = part.astype(out_ref.dtype)


def project(tokens, pieces, begun=None):
    rows, model = tokens.shape
    depth, total = pieces[0].shape
    first = begun is None
    whole = pl.BlockSpec(memory_space=pltpu.VMEM)
    begun = () if first else (begun,)
    return pl.pallas_call(
        functools.partial(project_kernel, first),
        in_specs=[whole] * (1 + len(begun) + len(pieces)),
        out_specs=whole,
        out_shape=jax.ShapeDtypeStruct((rows, total), F32 if first else BF),
        compiler_params=pltpu.CompilerParams(vmem_limit_bytes=16 << 20),
        cost_estimate=pl.CostEstimate(
            flops=rows * model * total, transcendentals=0, bytes_accessed=10 << 20
        ),
        name="project",
    )(tokens, *begun, *pieces)


def share_kernel(which, meta_ref, places_ref, tokens_ref, scanned_ref, gain_ref, *refs):
    pieces, (share_ref, square_ref, gated_scr) = refs[:-3], refs[-3:]
    seq, half = scanned_ref.shape
    rows = slice(which * seq, (which + 1) * seq)
    tile = half // 3
    square_ref[...] = jnp.zeros_like(square_ref)
    for at in range(0, half, tile):
        cols = slice(at, at + tile)
        weight = jnp.concatenate([piece[:, cols] for piece in pieces], axis=0)
        gate = jnp.dot(tokens_ref[rows], weight, preferred_element_type=F32).astype(BF)
        gated = scanned_ref[:, cols] * silu(gate.astype(F32))
        gain_at = pl.multiple_of(meta_ref[0] * half + at, LANES)
        gated_scr[:, cols] = (gated * gain_ref[:, pl.ds(gain_at, tile)]).astype(BF)
        square = gated * gated
        for lane in range(0, tile, LANES):
            square_ref[...] += square[:, lane : lane + LANES]
    steps = 4
    depth = pieces[0].shape[0] // steps
    each = depth // BLOCK_ROWS
    for step in range(steps):
        weight = jnp.concatenate(
            [piece[step * depth : (step + 1) * depth, half:] for piece in pieces], axis=0
        )
        total = lax.dot_general(
            weight, gated_scr[...], (((1,), (1,)), ((), ())), preferred_element_type=F32
        )
        for index in range(len(pieces)):
            for block in range(each):
                at = (index * each + block) * BLOCK_ROWS
                place = places_ref[(index * steps + step) * each + block]
                share_ref[pl.ds(pl.multiple_of(place, BLOCK_ROWS), BLOCK_ROWS), :] = total[
                    at : at + BLOCK_ROWS
                ]


def out_share(which, meta, places, tokens, scanned, gain, pieces):
    seq, half = scanned.shape
    model = tokens.shape[1]
    scalars = pl.BlockSpec(memory_space=pltpu.SMEM)
    whole = pl.BlockSpec(memory_space=pltpu.VMEM)
    return pl.pallas_call(
        functools.partial(share_kernel, which),
        in_specs=[scalars] * 2 + [whole] * (3 + len(pieces)),
        out_specs=[whole] * 2,
        out_shape=[
            jax.ShapeDtypeStruct((model, seq), F32),
            jax.ShapeDtypeStruct((seq, LANES), F32),
        ],
        scratch_shapes=[pltpu.VMEM((seq, half), BF)],
        compiler_params=pltpu.CompilerParams(vmem_limit_bytes=16 << 20),
        cost_estimate=pl.CostEstimate(
            flops=4 * seq * half * model, transcendentals=seq * half, bytes_accessed=16 << 20
        ),
        name="out_share",
    )(meta, places, tokens, scanned, gain, *pieces)


def mix_kernel(shard_ref, mine_ref, other_ref, sq_mine, sq_other, pick_ref, out_ref):
    seq, model = out_ref.shape
    inner = 2 * model
    squares = jnp.transpose(sq_mine[...] + sq_other[...])
    mean = jnp.sum(squares, axis=0, keepdims=True) / inner
    live = lax.broadcasted_iota(jnp.int32, (1, seq), 1).astype(F32) < length_of(shard_ref, HEADS)
    scale = jnp.where(live, lax.rsqrt(mean + EPSILON), 0.0)
    tile = pick_ref.shape[0]
    for at in range(0, model, tile):
        rows = slice(at, at + tile)
        short = ((mine_ref[rows] + other_ref[rows]) * scale).astype(BF)
        out_ref[:, rows] = lax.dot_general(
            short, pick_ref[...], (((0,), (0,)), ((), ())), preferred_element_type=F32
        ).astype(BF)


def mix(shard, cut, mine, other, sq_mine, sq_other):
    model, seq = mine.shape
    tile = model // 4
    column = jnp.arange(tile, dtype=jnp.int32)
    chip, rest = column // (2 * SHARD_ROWS), column % (2 * SHARD_ROWS)
    target = rest // SHARD_ROWS * (tile // 2) + chip * SHARD_ROWS + rest % SHARD_ROWS
    pick = (target[:, None] == column[None]).astype(BF)
    whole = pl.BlockSpec(memory_space=pltpu.VMEM)
    fixed = lambda i: (0, 0)
    return pl.pallas_call(
        mix_kernel,
        grid=(1,),
        in_specs=[pl.BlockSpec((shard.shape[0], LANES), lambda i: (0, cut // LANES - 1))]
        + [whole] * 5,
        out_specs=whole,
        out_shape=jax.ShapeDtypeStruct((seq, model), BF),
        compiler_params=pltpu.CompilerParams(vmem_limit_bytes=16 << 20),
        cost_estimate=pl.CostEstimate(
            flops=2 * seq * tile * model, transcendentals=0, bytes_accessed=8 << 20
        ),
        name="mix",
    )(shard, mine, other, sq_mine, sq_other, pick)


EVERYONE = ("req", "unit")
DEVICES = 128
CORE = 16
SHARD_ROWS = 12
COLOURS = 3
BLOCK_ROWS = 8
LINKS = (1 << 2, 1, 1 << 5, 3 << 2, 3, 3 << 5)


def link_of(colour, core, step):
    return LINKS[(colour + 3 * core - step) % 6]


def hop(value, mask_of):
    return lax.ppermute(
        value, EVERYONE, [(d, d ^ mask_of((d // CORE) % 2)) for d in range(DEVICES)]
    )


def swap(value):
    return hop(value, lambda core: CORE)


def moved_over(held, step):
    return [hop(piece, lambda core, c=c: link_of(c, core, step)) for c, piece in enumerate(held)]


def joined(held, moved):
    return [
        lax.optimization_barrier(jnp.concatenate([h, m], axis=0)) for h, m in zip(held, moved)
    ]


def gathered_chip(me, core, colour, block):
    mask = jnp.zeros_like(block)
    for step in range(6):
        link = jnp.zeros_like(block)
        for c in range(COLOURS):
            here = jnp.where(core == 0, link_of(c, 0, step), link_of(c, 1, step))
            link = jnp.where(colour == c, here, link)
        mask = mask ^ (((block >> step) & 1) * link)
    return (me ^ mask) & ~CORE


def row_sources(me, core, model):
    row = jnp.arange(model, dtype=jnp.int32)
    colour, block = row // (model // COLOURS), row // BLOCK_ROWS % 64
    local = colour * BLOCK_ROWS + row % BLOCK_ROWS
    upper = (local >= SHARD_ROWS).astype(jnp.int32)
    device = gathered_chip(me, core, colour, block) + CORE * upper
    return device * SHARD_ROWS + local - SHARD_ROWS * upper


def row_places(me, core):
    index = jnp.arange(COLOURS * 64, dtype=jnp.int32)
    chip = gathered_chip(me, core, index // 64, index % 64)
    chip = (chip >> 5) * CORE + (chip & (CORE - 1))
    return chip * 2 * SHARD_ROWS + index // 64 * BLOCK_ROWS


def body(
    tokens,
    lengths,
    gate_proj,
    input_proj,
    state_proj,
    step_proj,
    out_proj,
    conv_weight,
    step_bias,
    log_rate,
    skip_gain,
    norm_gain,
):
    unit_id = lax.axis_index("unit")
    me = lax.axis_index(EVERYONE).astype(jnp.int32)
    core = (me // CORE) % 2
    first_core = core == 0
    seq_len, model_dim = tokens.shape[1:]
    inner_dim = gate_proj.shape[1]
    head_count = log_rate.shape[0]
    head_dim = inner_dim // head_count
    width = state_proj.shape[1]
    half = inner_dim // 2

    cut = half + width + LANES
    meta = jnp.stack([core, unit_id])
    kept, sent = shards(
        meta, lengths, input_proj, state_proj, step_proj, gate_proj, out_proj
    )
    sent, unit_id = lax.optimization_barrier((sent, unit_id))
    received = swap(sent)
    pair = jnp.concatenate(
        [jnp.where(first_core, kept, received), jnp.where(first_core, received, kept)], axis=0
    )
    held = [pair[8 * c : 8 * c + 8] for c in range(COLOURS)]
    for step in range(3):
        held = joined(held, moved_over(held, step))
    held[2], unit_id = lax.optimization_barrier((held[2], unit_id))
    held = [join(h, m, cut + 2 * half)[0] for h, m in zip(held, moved_over(held, 3))]
    moved = moved_over(held, 4)

    own = lax.dynamic_index_in_dim(tokens, unit_id, 0, keepdims=False)
    both = jnp.concatenate([own, swap(own)], axis=0)
    pick = jnp.arange(model_dim, dtype=jnp.int32)[:, None] == row_sources(me, core, model_dim)[None]
    both = jnp.dot(both, pick.astype(BF), preferred_element_type=F32).astype(BF)
    moved[0], both, places = lax.optimization_barrier((moved[0], both, row_places(me, core)))
    early, late = zip(*[join(h, m, cut, 2 * half) for h, m in zip(held, moved)])
    late = list(late)
    moved = moved_over(early, 5)
    begun = project(both, early)
    moved[0], begun = lax.optimization_barrier((moved[0], begun))
    moved[0], late[0] = lax.optimization_barrier((moved[0], late[0]))
    late = [piece for two in zip(late, moved_over(late, 5)) for piece in two]

    projected = project(both, moved, begun)
    inputs = (projected, conv_weight, step_bias[None], log_rate[None], skip_gain, width)
    scanned_other, state_sent = scan(1, meta, received, *inputs)
    state_other = swap(state_sent)
    scanned, state = scan(0, meta, kept, *inputs)
    scanned_other, scanned, state_other = lax.optimization_barrier(
        (scanned_other, scanned, state_other)
    )
    shared = (meta, places, both)
    sent, square_sent = out_share(1, *shared, scanned_other, norm_gain[None], late)
    other, square_other = swap(sent), swap(square_sent)
    mine, square = out_share(0, *shared, scanned, norm_gain[None], late)
    mixed = mix(kept, cut, mine, other, square, square_other)
    state = jnp.concatenate(
        [jnp.where(first_core, state, state_other), jnp.where(first_core, state_other, state)]
    )
    return (mixed[None], state.reshape(1, head_count, head_dim, width // 2))


def solution(mesh):
    placed = (
        P("req", None, None),
        P("req"),
        P(("req", "unit"), None),
        P(("req", "unit"), None),
        P(("req", "unit"), None),
        P(("req", "unit"), None),
        P(("req", "unit"), None),
        P(),
        P(),
        P(),
        P(),
        P(),
    )
    return jax.shard_map(
        body,
        mesh=mesh,
        in_specs=placed,
        out_specs=(P(("req", "unit"), None, None), P(("req", "unit"), None, None, None)),
        check_vma=False,
    )
```

```python
import functools

import jax
import jax.numpy as jnp
from jax import lax
from jax.experimental import pallas as pl
from jax.experimental.pallas import tpu as pltpu
from jax.sharding import PartitionSpec as P

SPAN = 128
LANES = 128
HEADS = 48
HEADS_STEP = 8
EPSILON = 1e-05
LOG2E = 1.4426950408889634
BF = jnp.bfloat16
F32 = jnp.float32


def length_of(shard_ref, heads, start=0):
    coded = shard_ref[:1, start : start + LANES].astype(F32)
    return 16.0 * coded[:, heads : heads + 1] + coded[:, heads + 1 : heads + 2]


def silu(v):
    h = 0.5 * v
    return h + h * jnp.tanh(h)


def causal_conv(values, taps):
    rows = lax.broadcasted_iota(jnp.int32, (BLOCK_ROWS, values.shape[1]), 0)
    count = taps.shape[0]
    total = values * taps[count - 1 : count]
    for back in range(1, count):
        moved = pltpu.roll(values, back, 0)
        moved = jnp.concatenate(
            [jnp.where(rows >= back, moved[:BLOCK_ROWS], 0.0), moved[BLOCK_ROWS:]], axis=0
        )
        total = total + moved * taps[count - 1 - back : count - back]
    return silu(total)


def scan_kernel(
    which,
    meta_ref,
    shard_ref,
    projected_ref,
    taps_ref,
    bias_ref,
    log_rate_ref,
    skip_ref,
    scanned_ref,
    state_ref,
    decay_col,
    delta_row,
    decay_row,
    b_scr,
    c_scr,
    cb_scr,
):
    seq, half = scanned_ref.shape
    state_dim = state_ref.shape[1]
    groups = decay_col.shape[0]
    group_cols = HEADS_STEP * LANES // 2
    blocks = seq // SPAN
    every = slice(which * seq, (which + 1) * seq)
    position = lax.broadcasted_iota(jnp.int32, (seq, LANES), 0)
    lower = lax.broadcasted_iota(jnp.int32, (SPAN, SPAN), 0) >= lax.broadcasted_iota(
        jnp.int32, (SPAN, SPAN), 1
    )
    side = projected_ref[every, half:].astype(F32)
    conv = causal_conv(side[:, : 2 * state_dim], taps_ref[:, 2 * half :])
    b_short = conv[:, :state_dim].astype(BF)
    c_short = conv[:, state_dim:].astype(BF)
    b_scr[...] = b_short
    c_scr[...] = c_short
    for block in range(blocks):
        at = slice(block * SPAN, (block + 1) * SPAN)
        cb_scr[block] = lax.dot_general(
            c_short[at], b_short[at], (((1,), (1,)), ((), ())), preferred_element_type=F32
        )
        cb_scr[block] = jnp.where(lower, cb_scr[block], 0.0)
    spare = jnp.zeros((1, LANES - bias_ref.shape[1]), F32)
    raw = side[:, 2 * state_dim :] + jnp.concatenate([bias_ref[...], spare], axis=1)
    live = (position.astype(F32) < length_of(
            shard_ref, bias_ref.shape[1], half + 2 * state_dim
        )).astype(F32)
    delta = (jnp.maximum(raw, 0.0) + jnp.log1p(jnp.exp(-jnp.abs(raw)))) * live
    total = delta * (-LOG2E * jnp.exp(jnp.concatenate([log_rate_ref[...], spare], axis=1)))
    within = position % SPAN
    reach = 1
    while reach < SPAN:
        total = total + jnp.where(within >= reach, pltpu.roll(total, reach, 0), 0.0)
        reach *= 2
    turned = jnp.transpose(total)
    turned_delta = jnp.transpose(delta)
    for group in range(groups):
        at = slice(group * HEADS_STEP, (group + 1) * HEADS_STEP)
        decay_col[group] = total[:, at]
        delta_row[group] = turned_delta[at]
        decay_row[group] = turned[at]

    left = lax.broadcasted_iota(jnp.int32, (SPAN, LANES), 1) < LANES // 2
    top = lax.broadcasted_iota(jnp.int32, (LANES, state_dim), 0) < LANES // 2

    def group(step, carry):
        group_here = meta_ref[0] * (groups // 2) + step
        decays = decay_col[group_here]
        delta_of = delta_row[group_here]
        rows_of = decay_row[group_here]
        weight_of = delta_of * jnp.exp2(
            jnp.concatenate(
                [
                    rows_of[:, end - 1 : end] - rows_of[:, end - SPAN : end]
                    for end in range(SPAN, seq + 1, SPAN)
                ],
                axis=1,
            )
        )
        for pair in range(HEADS_STEP // 2):
            here = pl.ds(pl.multiple_of(step * group_cols + pair * LANES, LANES), LANES)
            taps_at = pl.multiple_of(meta_ref[0] * half + step * group_cols + pair * LANES, LANES)
            taps_at = pl.ds(taps_at, LANES)
            one, two = 2 * pair, 2 * pair + 1
            x_conv = causal_conv(projected_ref[every, here].astype(F32), taps_ref[:, taps_at])
            head = group_here * HEADS_STEP + one
            skip = jnp.where(left[:1], skip_ref[head], skip_ref[head + 1])
            state = jnp.zeros((LANES, state_dim), F32)
            for block in range(blocks):
                at = slice(block * SPAN, (block + 1) * SPAN)
                x_here = x_conv[at]
                cb = cb_scr[block]
                d_one, d_two = decays[at, one : one + 1], decays[at, two : two + 1]
                mix_one = cb * jnp.exp2(jnp.minimum(d_one - rows_of[one : one + 1, at], 0.0)) * delta_of[one : one + 1, at]
                mix_two = cb * jnp.exp2(jnp.minimum(d_two - rows_of[two : two + 1, at], 0.0)) * delta_of[two : two + 1, at]
                decay = jnp.where(left, d_one, d_two)
                short = x_here.astype(BF)
                zero = jnp.zeros_like(short)
                mixing = jnp.concatenate([mix_one.astype(BF), mix_two.astype(BF)], axis=1)
                spread = jnp.concatenate(
                    [jnp.where(left, short, zero), jnp.where(left, zero, short)], axis=0
                )
                out = jnp.dot(mixing, spread, preferred_element_type=F32)
                if block:
                    out = out + jnp.exp2(decay) * lax.dot_general(
                        c_scr[at],
                        state.astype(BF),
                        (((1,), (1,)), ((), ())),
                        preferred_element_type=F32,
                    )
                weighted = jnp.transpose(short).astype(F32) * jnp.where(
                    top, weight_of[one : one + 1, at], weight_of[two : two + 1, at]
                )
                fresh = jnp.dot(weighted.astype(BF), b_scr[at], preferred_element_type=F32)
                if block:
                    fade = jnp.where(
                        top,
                        jnp.exp2(d_one[SPAN - 1 : SPAN]),
                        jnp.exp2(d_two[SPAN - 1 : SPAN]),
                    )
                    fresh = fade * state + fresh
                state = fresh
                scanned_ref[at, here] = out + skip * x_here
            state_ref[here, :] = state
        return carry

    lax.fori_loop(0, groups // 2, group, 0)


def scan(which, meta, shard, projected, conv_weight, bias, log_rate, skip, width):
    seq, total = projected.shape[0] // 2, projected.shape[1]
    state_dim = width // 2
    half = total - width - LANES
    groups = 2 * half // (HEADS_STEP * LANES // 2)
    scalars = pl.BlockSpec(memory_space=pltpu.SMEM)
    whole = pl.BlockSpec(memory_space=pltpu.VMEM)
    return pl.pallas_call(
        functools.partial(scan_kernel, which),
        in_specs=[scalars] + [whole] * 5 + [scalars],
        out_specs=[whole] * 2,
        out_shape=[
            jax.ShapeDtypeStruct((seq, half), F32),
            jax.ShapeDtypeStruct((half, state_dim), F32),
        ],
        scratch_shapes=[
            pltpu.VMEM((groups, seq, HEADS_STEP), F32),
            pltpu.VMEM((groups, HEADS_STEP, seq), F32),
            pltpu.VMEM((groups, HEADS_STEP, seq), F32),
            pltpu.VMEM((seq, state_dim), BF),
            pltpu.VMEM((seq, state_dim), BF),
            pltpu.VMEM((seq // SPAN, SPAN, SPAN), F32),
        ],
        compiler_params=pltpu.CompilerParams(vmem_limit_bytes=16 << 20),
        cost_estimate=pl.CostEstimate(
            flops=2 * half * seq * 640, transcendentals=half * seq * 6, bytes_accessed=5 << 20
        ),
        name="scan",
    )(meta, shard, projected, conv_weight, bias, log_rate, skip)


def shards_kernel(
    meta_ref, lengths_ref, input_ref, state_ref, step_ref, gate_ref, out_ref, kept_ref, sent_ref
):
    rows, half = input_ref.shape[0], input_ref.shape[1] // 2
    width, heads = state_ref.shape[1], step_ref.shape[1]
    length = lengths_ref[meta_ref[1]]
    row = lax.broadcasted_iota(jnp.int32, (rows, LANES), 0)
    lane = lax.broadcasted_iota(jnp.int32, (rows, LANES), 1)
    coded = jnp.where(lane == heads, length >> 4, jnp.where(lane == heads + 1, length & 15, 0))
    coded = jnp.where(row == 0, coded, 0).astype(F32).astype(BF)
    for ref, core in ((kept_ref, meta_ref[0]), (sent_ref, 1 - meta_ref[0])):
        at = pl.ds(pl.multiple_of(core * half, half), half)
        ref[:, :half] = input_ref[:, at].astype(BF)
        ref[:, half : half + width] = state_ref[...].astype(BF)
        ref[:, half + width : half + width + LANES] = coded
        ref[:, half + width : half + width + heads] = step_ref[...].astype(BF)
        start = half + width + LANES
        ref[:, start : start + half] = gate_ref[:, at].astype(BF)
        ref[:, start + half :] = out_ref[:, at].astype(BF)


def shards(meta, lengths, inputs, state, step, gate, out):
    rows, inner = inputs.shape
    total = 3 * (inner // 2) + state.shape[1] + LANES
    scalars = pl.BlockSpec(memory_space=pltpu.SMEM)
    whole = pl.BlockSpec(memory_space=pltpu.VMEM)
    return pl.pallas_call(
        shards_kernel,
        in_specs=[scalars] * 2 + [whole] * 5,
        out_specs=[whole] * 2,
        out_shape=[jax.ShapeDtypeStruct((rows, total), BF)] * 2,
        name="shards",
    )(meta, lengths, inputs, state, step, gate, out)


def join_kernel(held_ref, moved_ref, *outs):
    rows, start = held_ref.shape[0], 0
    for out_ref in outs:
        cols = slice(start, start + out_ref.shape[1])
        out_ref[:rows] = held_ref[:, cols]
        out_ref[rows:] = moved_ref[:, cols]
        start += out_ref.shape[1]


def join(held, moved, *widths):
    rows, total = held.shape
    whole = pl.BlockSpec(memory_space=pltpu.VMEM)
    return pl.pallas_call(
        join_kernel,
        in_specs=[whole] * 2,
        out_specs=[whole] * len(widths),
        out_shape=[jax.ShapeDtypeStruct((2 * rows, width), BF) for width in widths],
        compiler_params=pltpu.CompilerParams(vmem_limit_bytes=6 << 20),
        cost_estimate=pl.CostEstimate(
            flops=0, transcendentals=0, bytes_accessed=8 * rows * total
        ),
        name="join",
    )(held, moved)


def project_kernel(first, tokens_ref, *refs):
    begin_ref, pieces, out_ref = refs[0], refs[:-1], refs[-1]
    if not first:
        pieces = pieces[1:]
    depth, total = pieces[0].shape
    tokens = jnp.concatenate(
        [
            tokens_ref[:, at : at + depth]
            for at in range(0 if first else depth, tokens_ref.shape[1], 2 * depth)
        ],
        axis=1,
    )
    tile = total // 5
    for at in range(0, total, tile):
        cols = slice(at, at + tile)
        weight = jnp.concatenate([piece[:, cols] for piece in pieces], axis=0)
        part = jnp.dot(tokens, weight, preferred_element_type=F32)
        if not first:
            part = part + begin_ref[:, cols]
        out_ref[:, cols] = part.astype(out_ref.dtype)


def project(tokens, pieces, begun=None):
    rows, model = tokens.shape
    depth, total = pieces[0].shape
    first = begun is None
    whole = pl.BlockSpec(memory_space=pltpu.VMEM)
    begun = () if first else (begun,)
    return pl.pallas_call(
        functools.partial(project_kernel, first),
        in_specs=[whole] * (1 + len(begun) + len(pieces)),
        out_specs=whole,
        out_shape=jax.ShapeDtypeStruct((rows, total), F32 if first else BF),
        compiler_params=pltpu.CompilerParams(vmem_limit_bytes=16 << 20),
        cost_estimate=pl.CostEstimate(
            flops=rows * model * total, transcendentals=0, bytes_accessed=10 << 20
        ),
        name="project",
    )(tokens, *begun, *pieces)


def share_kernel(which, meta_ref, places_ref, tokens_ref, scanned_ref, gain_ref, *refs):
    pieces, (share_ref, square_ref, gated_scr) = refs[:-3], refs[-3:]
    seq, half = scanned_ref.shape
    rows = slice(which * seq, (which + 1) * seq)
    tile = half // 3
    square_ref[...] = jnp.zeros_like(square_ref)
    for at in range(0, half, tile):
        cols = slice(at, at + tile)
        weight = jnp.concatenate([piece[:, cols] for piece in pieces], axis=0)
        gate = jnp.dot(tokens_ref[rows], weight, preferred_element_type=F32).astype(BF)
        gated = scanned_ref[:, cols] * silu(gate.astype(F32))
        gain_at = pl.multiple_of(meta_ref[0] * half + at, LANES)
        gated_scr[:, cols] = (gated * gain_ref[:, pl.ds(gain_at, tile)]).astype(BF)
        square = gated * gated
        for lane in range(0, tile, LANES):
            square_ref[...] += square[:, lane : lane + LANES]
    steps = 4
    depth = pieces[0].shape[0] // steps
    each = depth // BLOCK_ROWS
    for step in range(steps):
        weight = jnp.concatenate(
            [piece[step * depth : (step + 1) * depth, half:] for piece in pieces], axis=0
        )
        total = lax.dot_general(
            weight, gated_scr[...], (((1,), (1,)), ((), ())), preferred_element_type=F32
        )
        for index in range(len(pieces)):
            for block in range(each):
                at = (index * each + block) * BLOCK_ROWS
                place = places_ref[(index * steps + step) * each + block]
                share_ref[pl.ds(pl.multiple_of(place, BLOCK_ROWS), BLOCK_ROWS), :] = total[
                    at : at + BLOCK_ROWS
                ]


def out_share(which, meta, places, tokens, scanned, gain, pieces):
    seq, half = scanned.shape
    model = tokens.shape[1]
    scalars = pl.BlockSpec(memory_space=pltpu.SMEM)
    whole = pl.BlockSpec(memory_space=pltpu.VMEM)
    return pl.pallas_call(
        functools.partial(share_kernel, which),
        in_specs=[scalars] * 2 + [whole] * (3 + len(pieces)),
        out_specs=[whole] * 2,
        out_shape=[
            jax.ShapeDtypeStruct((model, seq), F32),
            jax.ShapeDtypeStruct((seq, LANES), F32),
        ],
        scratch_shapes=[pltpu.VMEM((seq, half), BF)],
        compiler_params=pltpu.CompilerParams(vmem_limit_bytes=16 << 20),
        cost_estimate=pl.CostEstimate(
            flops=4 * seq * half * model, transcendentals=seq * half, bytes_accessed=16 << 20
        ),
        name="out_share",
    )(meta, places, tokens, scanned, gain, *pieces)


def mix_kernel(shard_ref, mine_ref, other_ref, sq_mine, sq_other, pick_ref, out_ref):
    seq, model = out_ref.shape
    inner = 2 * model
    squares = jnp.transpose(sq_mine[...] + sq_other[...])
    mean = jnp.sum(squares, axis=0, keepdims=True) / inner
    live = lax.broadcasted_iota(jnp.int32, (1, seq), 1).astype(F32) < length_of(shard_ref, HEADS)
    scale = jnp.where(live, lax.rsqrt(mean + EPSILON), 0.0)
    tile = pick_ref.shape[0]
    for at in range(0, model, tile):
        rows = slice(at, at + tile)
        short = ((mine_ref[rows] + other_ref[rows]) * scale).astype(BF)
        out_ref[:, rows] = lax.dot_general(
            short, pick_ref[...], (((0,), (0,)), ((), ())), preferred_element_type=F32
        ).astype(BF)


def mix(shard, cut, mine, other, sq_mine, sq_other):
    model, seq = mine.shape
    tile = model // 4
    column = jnp.arange(tile, dtype=jnp.int32)
    chip, rest = column // (2 * SHARD_ROWS), column % (2 * SHARD_ROWS)
    target = rest // SHARD_ROWS * (tile // 2) + chip * SHARD_ROWS + rest % SHARD_ROWS
    pick = (target[:, None] == column[None]).astype(BF)
    whole = pl.BlockSpec(memory_space=pltpu.VMEM)
    fixed = lambda i: (0, 0)
    return pl.pallas_call(
        mix_kernel,
        grid=(1,),
        in_specs=[pl.BlockSpec((shard.shape[0], LANES), lambda i: (0, cut // LANES - 1))]
        + [whole] * 5,
        out_specs=whole,
        out_shape=jax.ShapeDtypeStruct((seq, model), BF),
        compiler_params=pltpu.CompilerParams(vmem_limit_bytes=16 << 20),
        cost_estimate=pl.CostEstimate(
            flops=2 * seq * tile * model, transcendentals=0, bytes_accessed=8 << 20
        ),
        name="mix",
    )(shard, mine, other, sq_mine, sq_other, pick)


EVERYONE = ("req", "unit")
DEVICES = 128
CORE = 16
SHARD_ROWS = 12
COLOURS = 3
BLOCK_ROWS = 8
LINKS = (1 << 2, 1, 1 << 5, 3 << 2, 3, 3 << 5)


def link_of(colour, core, step):
    return LINKS[(colour + 3 * core - step) % 6]


def hop(value, mask_of):
    return lax.ppermute(
        value, EVERYONE, [(d, d ^ mask_of((d // CORE) % 2)) for d in range(DEVICES)]
    )


def swap(value):
    return hop(value, lambda core: CORE)


def moved_over(held, step):
    return [hop(piece, lambda core, c=c: link_of(c, core, step)) for c, piece in enumerate(held)]


def joined(held, moved):
    return [
        lax.optimization_barrier(jnp.concatenate([h, m], axis=0)) for h, m in zip(held, moved)
    ]


def gathered_chip(me, core, colour, block):
    mask = jnp.zeros_like(block)
    for step in range(6):
        link = jnp.zeros_like(block)
        for c in range(COLOURS):
            here = jnp.where(core == 0, link_of(c, 0, step), link_of(c, 1, step))
            link = jnp.where(colour == c, here, link)
        mask = mask ^ (((block >> step) & 1) * link)
    return (me ^ mask) & ~CORE


def row_sources(me, core, model):
    row = jnp.arange(model, dtype=jnp.int32)
    colour, block = row // (model // COLOURS), row // BLOCK_ROWS % 64
    local = colour * BLOCK_ROWS + row % BLOCK_ROWS
    upper = (local >= SHARD_ROWS).astype(jnp.int32)
    device = gathered_chip(me, core, colour, block) + CORE * upper
    return device * SHARD_ROWS + local - SHARD_ROWS * upper


def row_places(me, core):
    index = jnp.arange(COLOURS * 64, dtype=jnp.int32)
    chip = gathered_chip(me, core, index // 64, index % 64)
    chip = (chip >> 5) * CORE + (chip & (CORE - 1))
    return chip * 2 * SHARD_ROWS + index // 64 * BLOCK_ROWS


def body(
    tokens,
    lengths,
    gate_proj,
    input_proj,
    state_proj,
    step_proj,
    out_proj,
    conv_weight,
    step_bias,
    log_rate,
    skip_gain,
    norm_gain,
):
    unit_id = lax.axis_index("unit")
    me = lax.axis_index(EVERYONE).astype(jnp.int32)
    core = (me // CORE) % 2
    first_core = core == 0
    seq_len, model_dim = tokens.shape[1:]
    inner_dim = gate_proj.shape[1]
    head_count = log_rate.shape[0]
    head_dim = inner_dim // head_count
    width = state_proj.shape[1]
    half = inner_dim // 2

    cut = half + width + LANES
    meta = jnp.stack([core, unit_id])
    kept, sent = shards(
        meta, lengths, input_proj, state_proj, step_proj, gate_proj, out_proj
    )
    sent, unit_id = lax.optimization_barrier((sent, unit_id))
    received = swap(sent)
    pair = jnp.concatenate(
        [jnp.where(first_core, kept, received), jnp.where(first_core, received, kept)], axis=0
    )
    held = [pair[8 * c : 8 * c + 8] for c in range(COLOURS)]
    for step in range(3):
        held = joined(held, moved_over(held, step))
    held[0], unit_id = lax.optimization_barrier((held[0], unit_id))
    held = [join(h, m, cut + 2 * half)[0] for h, m in zip(held, moved_over(held, 3))]
    moved = moved_over(held, 4)

    own = lax.dynamic_index_in_dim(tokens, unit_id, 0, keepdims=False)
    both = jnp.concatenate([own, swap(own)], axis=0)
    pick = jnp.arange(model_dim, dtype=jnp.int32)[:, None] == row_sources(me, core, model_dim)[None]
    both = jnp.dot(both, pick.astype(BF), preferred_element_type=F32).astype(BF)
    moved[0], both, places = lax.optimization_barrier((moved[0], both, row_places(me, core)))
    early, late = zip(*[join(h, m, cut, 2 * half) for h, m in zip(held, moved)])
    late = list(late)
    moved = moved_over(early, 5)
    begun = project(both, early)
    moved[0], begun = lax.optimization_barrier((moved[0], begun))
    moved[0], late[0] = lax.optimization_barrier((moved[0], late[0]))
    late = [piece for two in zip(late, moved_over(late, 5)) for piece in two]

    projected = project(both, moved, begun)
    inputs = (projected, conv_weight, step_bias[None], log_rate[None], skip_gain, width)
    scanned_other, state_sent = scan(1, meta, received, *inputs)
    state_other = swap(state_sent)
    scanned, state = scan(0, meta, kept, *inputs)
    scanned_other, scanned, state_other = lax.optimization_barrier(
        (scanned_other, scanned, state_other)
    )
    shared = (meta, places, both)
    sent, square_sent = out_share(1, *shared, scanned_other, norm_gain[None], late)
    other, square_other = swap(sent), swap(square_sent)
    mine, square = out_share(0, *shared, scanned, norm_gain[None], late)
    mixed = mix(kept, cut, mine, other, square, square_other)
    state = jnp.concatenate(
        [jnp.where(first_core, state, state_other), jnp.where(first_core, state_other, state)]
    )
    return (mixed[None], state.reshape(1, head_count, head_dim, width // 2))


def solution(mesh):
    placed = (
        P("req", None, None),
        P("req"),
        P(("req", "unit"), None),
        P(("req", "unit"), None),
        P(("req", "unit"), None),
        P(("req", "unit"), None),
        P(("req", "unit"), None),
        P(),
        P(),
        P(),
        P(),
        P(),
    )
    return jax.shard_map(
        body,
        mesh=mesh,
        in_specs=placed,
        out_specs=(P(("req", "unit"), None, None), P(("req", "unit"), None, None, None)),
        check_vma=False,
    )
```
